32 devices in a mesh: ax: 4 (over z), xs: 8 (over y, x, core).
Axes of the slice: x: 2, y: 2, z: 4, core: 2. Of those that a mesh axis runs over, the one named last changes fastest.
Arguments:
- adjoint: float32 [512, 10, 1024], P('xs', None, 'ax'), may hold values from -6 to 6
- source: float32 [512, 10, 1024], P('xs', None, 'ax'), may hold values from -6 to 6
- speed: float32 [512, 5, 1024], P('xs', None, 'ax'), may hold values from -2 to 2, as said below
- inverse_step: float32 [512, 5, 1024], P('xs', None, 'ax'), as said below
- coupling: float32 [128, 5, 1024], P('xs', None, 'ax'), may hold values from -4 to 4
- face_line: int32 [128], P('xs'), may hold values from 0 to 63
- face_owner: int32 [128], P('xs'), may hold values from 0 to 127, as said below
- line_length: int32 [512], P('xs'), may hold values from 513 to 1024, as said below
Outputs:
- refreshed: float32 [512, 10, 1024], P('xs', None, 'ax')
- residual: float32 [512, 10, 1024], P('xs', None, 'ax')
The draws below stay inside these ranges and needn't reach their ends.
Inputs may be any that keep to these rules, and one draw needn't show every extreme that they name: Each variable of a line keeps one sign of speed along the whole line, magnitude 0.5 or more. `inverse_step`: positive everywhere. `line_length`: the longest line has all 1024 cells. `face_owner`: each value once; of the 16 faces of one block, at most 2 have slots owned by any one block, and some block has exactly 2 with one owner block.
All inputs are finite; a program needn't handle non-finite values.
Results may differ from the reference program's by a relative error of at most 0.00015.
Values sent between devices are 32-bit elements; how exact they have to be, the bound alone decides.
No kernel may reach another device: no remote copies, remote signals or barrier semaphores. Data moves between devices by JAX's collectives and lax.ppermute only.
A program may use at most 64 MiB of HBM per device.

```python
import math
import jax
import jax.numpy as jnp
from jax import lax

STATE_UNKNOWNS = 5
CELL_DEV = 256
LINES_DEV = 64
FACE_DEV = 8
TRACK_VOLUMES = 1024
NOZZLE_TRACKS = 512
FACES = 64


def draw_speed(key, part):
    sign_key, size_key = jax.random.split(key)
    signs = jnp.where(jax.random.uniform(sign_key, (NOZZLE_TRACKS, STATE_UNKNOWNS, 1)) < 0.7, 1.0, -1.0)
    magnitude = jnp.exp(jax.random.uniform(size_key, (NOZZLE_TRACKS, STATE_UNKNOWNS, TRACK_VOLUMES), jnp.float32, math.log(0.5), math.log(2.0)))
    return (signs * magnitude).astype(jnp.float32)


def draw_inverse_step(key, part):
    speed_seed_handle, tile_seed_handle, jaggedness_seed, spike_seed_handle = jax.random.split(key, 4)
    speed_multiplier = jnp.exp(jax.random.uniform(speed_seed_handle, (NOZZLE_TRACKS, STATE_UNKNOWNS, 1), jnp.float32, math.log(0.05 / TRACK_VOLUMES), math.log(0.05)))
    tile_clusters = jnp.exp(jax.random.uniform(tile_seed_handle, (NOZZLE_TRACKS, STATE_UNKNOWNS, TRACK_VOLUMES // CELL_DEV), jnp.float32, math.log(0.5), math.log(2.0)))
    tile_clusters = jnp.repeat(tile_clusters, CELL_DEV, axis=2)
    jaggedness = jnp.exp(jax.random.uniform(jaggedness_seed, (NOZZLE_TRACKS, STATE_UNKNOWNS, TRACK_VOLUMES), jnp.float32, math.log(0.7), math.log(1.4)))
    spike_clusters = jnp.where(jax.random.uniform(spike_seed_handle, (NOZZLE_TRACKS, STATE_UNKNOWNS, TRACK_VOLUMES)) < 3.0 / TRACK_VOLUMES, 0.3, 0.0)
    return (speed_multiplier * tile_clusters * jaggedness + spike_clusters).astype(jnp.float32)


def draw_line_length(key, part):
    shorter = jax.random.randint(key, (NOZZLE_TRACKS,), 0, TRACK_VOLUMES // 2)
    lengths = (TRACK_VOLUMES - shorter).astype(jnp.int32)
    return lengths.at[0].set(TRACK_VOLUMES)


def draw_face_owner(key, part):
    block_count = FACES // FACE_DEV
    per_block = 2 * FACE_DEV
    source_key, owner_key, order_key, slot_key = jax.random.split(jax.random.fold_in(key, 17), 4)
    source_perm = jax.random.permutation(source_key, block_count).astype(jnp.int32)
    owner_perm = jax.random.permutation(owner_key, block_count).astype(jnp.int32)
    face_order = jax.vmap(lambda k: jax.random.permutation(k, per_block))(jax.random.split(order_key, block_count)).astype(jnp.int32)
    slot_order = jax.vmap(lambda k: jax.random.permutation(k, per_block))(jax.random.split(slot_key, block_count)).astype(jnp.int32)
    b = jnp.arange(block_count, dtype=jnp.int32)[:, None]
    j = jnp.arange(per_block, dtype=jnp.int32)[None, :]
    owner_block = owner_perm[(source_perm[b] + j) % block_count]
    q = slot_order[owner_block, jnp.broadcast_to(j, owner_block.shape)]
    owner_value = q // FACE_DEV * FACES + owner_block * FACE_DEV + q % FACE_DEV
    face_pos = b * per_block + face_order
    result_map = jnp.zeros((2 * FACES,), jnp.int32).at[face_pos.reshape(-1)].set(owner_value.reshape(-1).astype(jnp.int32))
    return result_map


def touch_ends(drawn, stream_key, low, top_value):
    index_at = [jax.random.randint(jax.random.fold_in(stream_key, axis), (), 0, length) for axis, length in enumerate(drawn.shape)]
    main_axis = drawn.shape.index(max(drawn.shape))
    neighbour = index_at[:main_axis] + [(index_at[main_axis] + 1) % drawn.shape[main_axis]] + index_at[main_axis + 1:]
    return drawn.at[tuple(index_at)].set(low).at[tuple(neighbour)].set(top_value)


def level_of(rng, dims, cuts, least, high):
    factor_of, own = 1.0, jax.random.fold_in(rng, 6)
    for position, parts in cuts:
        heights = jnp.exp(jax.random.uniform(jax.random.fold_in(own, position), (parts,), jnp.float32, least / len(cuts), high / len(cuts)))
        factor_of = factor_of * jnp.repeat(heights, dims[position] // parts).reshape([-1 if axis == position else 1 for axis in range(len(dims))])
    return factor_of


def scatter_about(stream_key, shape, deviation, bound, pieces=(), kind=jnp.bfloat16):
    values = deviation * jax.random.normal(stream_key, shape, jnp.float32)
    if pieces:
        values = values * level_of(stream_key, shape, pieces, -0.22, 0.18)
    return jnp.clip(values, -bound, bound).astype(kind)


def setup_inputs(seed: int = 0) -> dict:
    seeds = jax.random.split(jax.random.key(seed), 9)
    adjoint = scatter_about(seeds[0], (NOZZLE_TRACKS, 2 * STATE_UNKNOWNS, TRACK_VOLUMES), 1.0, 6.0, ((0, 8), (2, 4)), jnp.float32)
    source = scatter_about(seeds[1], (NOZZLE_TRACKS, 2 * STATE_UNKNOWNS, TRACK_VOLUMES), 1.0, 6.0, ((0, 8), (2, 4)), jnp.float32)
    speed = draw_speed(jax.random.fold_in(seeds[8], 71), 0)
    inverse_step = draw_inverse_step(jax.random.fold_in(seeds[8], 71), 0)
    coupling = scatter_about(seeds[4], (2 * FACES, STATE_UNKNOWNS, TRACK_VOLUMES), 0.7, 4.0, ((0, 8), (2, 4)), jnp.float32)
    face_line = touch_ends(jax.random.randint(seeds[5], (2 * FACES,), 0, LINES_DEV), jax.random.fold_in(seeds[5], 1), 0, LINES_DEV - 1).astype(jnp.int32)
    face_owner = draw_face_owner(jax.random.fold_in(seeds[8], 71), 0)
    line_length = draw_line_length(jax.random.fold_in(seeds[8], 71), 0)
    return {"adjoint": adjoint, "source": source, "speed": speed, "inverse_step": inverse_step, "coupling": coupling, "face_line": face_line, "face_owner": face_owner, "line_length": line_length}


frequency = 0.7
relaxation = 0.02


def reference(adjoint, source, speed, inverse_step, coupling, face_line, face_owner, line_length):
    cell_index = jnp.arange(TRACK_VOLUMES, dtype=jnp.int32)
    inside = (cell_index[None, :] < line_length[:, None]).astype(jnp.float32)[:, None, :]
    forward_speed = jnp.maximum(speed, 0.0) * inside
    backward_speed = jnp.maximum(-speed, 0.0) * inside
    forward_rows = jnp.concatenate([forward_speed, forward_speed], axis=1)
    backward_rows = jnp.concatenate([backward_speed, backward_speed], axis=1)
    flux_up = forward_rows * adjoint
    flux_down = backward_rows * adjoint
    up_pad = jnp.pad(flux_up, ((0, 0), (0, 0), (0, 2)))
    down_pad = jnp.pad(flux_down, ((0, 0), (0, 0), (2, 0)))
    transport = (1.5 * (flux_up + flux_down) - 2.0 * up_pad[:, :, 1:TRACK_VOLUMES + 1] + 0.5 * up_pad[:, :, 2:]
                 - 2.0 * down_pad[:, :, 1:TRACK_VOLUMES + 1] + 0.5 * down_pad[:, :, 0:TRACK_VOLUMES])
    rotation = jnp.concatenate([-frequency * adjoint[:, STATE_UNKNOWNS:], frequency * adjoint[:, :STATE_UNKNOWNS]], axis=1)
    face_index = jnp.arange(2 * FACES, dtype=jnp.int32)
    source_line = (face_index // (2 * FACE_DEV)) * LINES_DEV + face_line
    slot_index = face_owner % FACES
    target_line = (slot_index // FACE_DEV) * LINES_DEV + slot_index % FACE_DEV
    coupling_rows = jnp.concatenate([coupling, coupling], axis=1)
    partial_value = coupling_rows * adjoint[source_line]
    cross = jnp.zeros_like(adjoint).at[target_line].add(partial_value)
    residual = inside * (source - transport - rotation - cross)
    diagonal = inverse_step + 1.5 * (forward_speed + backward_speed)
    diagonal_rows = jnp.concatenate([diagonal, diagonal], axis=1)
    resid_t = jnp.moveaxis(residual, 2, 0)
    diag_t = jnp.moveaxis(diagonal_rows, 2, 0)
    back_t = jnp.moveaxis(backward_rows, 2, 0)
    fore_t = jnp.moveaxis(forward_rows, 2, 0)
    zeros_state = jnp.zeros((NOZZLE_TRACKS, 2 * STATE_UNKNOWNS), jnp.float32)

    def down_step(carried, items):
        resid_cell, diag_cell, back_cell = items
        value = (resid_cell + 2.0 * carried[0] - 0.5 * carried[1]) / diag_cell
        return (back_cell * value, carried[0]), value

    ignored, lower_sweep = lax.scan(down_step, (zeros_state, zeros_state), (resid_t, diag_t, back_t))

    def up_step(carried, items):
        lower_cell, diag_cell, fore_cell = items
        value = lower_cell + (2.0 * carried[0] - 0.5 * carried[1]) / diag_cell
        return (fore_cell * value, carried[0]), value

    ignored_up, update = lax.scan(up_step, (zeros_state, zeros_state), (lower_sweep, diag_t, fore_t), reverse=True)
    update = jnp.moveaxis(update, 0, 2)
    refreshed = inside * (adjoint + relaxation * update)
    return (refreshed, residual)
```

```python
import functools
import jax
import jax.numpy as jnp
from jax import lax
from jax.experimental import pallas as pl
from jax.experimental.pallas import tpu as pltpu
from jax.sharding import PartitionSpec as P

FACE_DEV = 8

frequency = 0.7
relaxation = 0.02

SEGS = 8
PACK_ROWS = 24


def pack_faces(blocks, cap, line_ref, owner_ref, adj_ref, coup_ref, out_ref):
    faces = coup_ref.shape[1]
    vars_ = coup_ref.shape[0]
    half = adj_ref.shape[2] // 2
    slots = FACE_DEV * blocks
    if blocks * cap != faces:
        for e in range(blocks * cap):
            out_ref[e, 16:24, :] = jnp.full((8, 128), -1.0, jnp.float32)
    dests = []
    for f in range(faces):
        slot = lax.rem(owner_ref[f], slots)
        dest = lax.div(slot, FACE_DEV)
        spot = jnp.int32(0)
        for other in dests:
            spot = spot + (other == dest).astype(jnp.int32)
        dests.append(dest)
        entry = dest * cap + jnp.minimum(spot, cap - 1)
        line = line_ref[f]
        for k in range(vars_):
            c = coup_ref[k, f : f + 1, :]
            re = c * adj_ref[k, pl.ds(line, 1), :]
            im = c * adj_ref[k + vars_, pl.ds(line, 1), :]
            out_ref[entry, 4 * k : 4 * k + 1, :] = re[:, :half]
            out_ref[entry, 4 * k + 1 : 4 * k + 2, :] = re[:, half:]
            out_ref[entry, 4 * k + 2 : 4 * k + 3, :] = im[:, :half]
            out_ref[entry, 4 * k + 3 : 4 * k + 4, :] = im[:, half:]
        number = lax.rem(slot, FACE_DEV).astype(jnp.float32)
        out_ref[entry, 20:24, :] = jnp.full((4, 128), number, jnp.float32)


def sweep_maps(
    len_ref, recv_ref, adj_ref, src_ref, speed_ref, inv_ref,
    msg_ref, aux_ref, part_ref, lift_ref, res_ref,
    a_t, q_t, s_t, i_t, h_s, r_s, c_s, b_s, m_s, o_p, o_x, o_r, t_p, t_x, t_r,
):
    k = pl.program_id(0)
    lines = adj_ref.shape[2]
    cells = adj_ref.shape[3]
    steps = cells // SEGS
    width = 2 * lines
    f32 = jnp.float32
    a_re, a_im = adj_ref[0, 0], adj_ref[1, 0]
    q_re = src_ref[0, 0] + frequency * a_im
    q_im = src_ref[1, 0] - frequency * a_re
    sub = lax.broadcasted_iota(jnp.int32, (FACE_DEV, 128), 0).astype(f32)
    acc = [jnp.zeros((FACE_DEV, 128), f32) for _ in range(4)]
    for e in range(recv_ref.shape[0]):
        hit = jnp.broadcast_to(recv_ref[e, 20:21, :], (FACE_DEV, 128)) == sub
        for j in range(4):
            row = jnp.broadcast_to(recv_ref[e, pl.ds(4 * k + j, 1), :], (FACE_DEV, 128))
            acc[j] = acc[j] + jnp.where(hit, row, 0.0)
    q_t[...] = jnp.concatenate([q_re, q_im], axis=0).T
    top = jnp.concatenate(
        [jnp.concatenate(acc[:2], axis=1), jnp.zeros((lines - FACE_DEV, cells), f32),
         jnp.concatenate(acc[2:], axis=1), jnp.zeros((lines - FACE_DEV, cells), f32)], axis=0)
    q_t[...] = q_t[...] - top.T
    a_t[...] = jnp.concatenate([a_re, a_im], axis=0).T
    sp = speed_ref[0]
    s_t[...] = jnp.concatenate([sp, sp], axis=0).T
    iv = inv_ref[0]
    i_t[...] = jnp.concatenate([iv, iv], axis=0).T
    pos = jnp.broadcast_to(s_t[0:1, :], (SEGS, width)) > 0.0
    seg = lax.broadcasted_iota(jnp.int32, (SEGS, width), 0)
    order = jnp.where(pos, SEGS - 1 - seg, seg)
    length = len_ref[...]
    length = jnp.broadcast_to(jnp.concatenate([length, length], axis=1), (SEGS, width))
    base = lax.axis_index("ax") * cells + seg * steps
    left = length - base

    def at(ref, t):
        lo = ref[pl.ds(t, SEGS, stride=steps), :]
        hi = ref[pl.ds(steps - 1 - t, SEGS, stride=steps), :]
        return jnp.where(pos, hi, lo)

    def before(value, reach, fill):
        up = pltpu.roll(value, reach, 0)
        down = pltpu.roll(value, SEGS - reach, 0)
        return jnp.where(order >= reach, jnp.where(pos, down, up), fill)

    zero = jnp.zeros((SEGS, width), f32)
    one = jnp.ones((SEGS, width), f32)
    y1, y2, p1, p2, w1, w2 = zero, zero, one, zero, zero, one
    fluxes = []
    masks = []
    for t in range(steps):
        a, q, v, inv = at(a_t, t), at(q_t, t), at(s_t, t), at(i_t, t)
        inside = jnp.where(pos, steps - 1 - t, t) < left
        s = jnp.where(inside, jnp.abs(v), 0.0)
        g = s * a
        rd = 1.0 / (inv + 1.5 * s)
        c = s * rd
        h = jnp.where(inside, q, 0.0) - 1.5 * g
        b = g + c * h
        h_s[t] = h
        r_s[t] = jnp.where(inside, relaxation * rd, 0.0)
        c_s[t] = c
        b_s[t] = b
        m_s[t] = jnp.where(inside, a, 0.0)
        c1, c2 = 2.0 * c, -0.5 * c
        y1, y2 = (b + c2 * y2) + c1 * y1, y1
        p1, p2 = c2 * p2 + c1 * p1, p1
        w1, w2 = c2 * w2 + c1 * w1, w1
        if t < 2:
            fluxes.append((g, h, inside))
            masks.append(jnp.where(inside, 1.0, 0.0))
        else:
            o_r[t] = h + jnp.where(inside, 2.0 * g_1 - 0.5 * g_2, 0.0)
        if t == 0:
            g_1 = g
        else:
            g_2, g_1 = g_1, g
    g_end1, g_end2 = g_1, g_2
    e1, e2 = before(g_end1, 1, 0.0), before(g_end2, 1, 0.0)
    g0, h0, in0 = fluxes[0]
    g1_, h1_, in1 = fluxes[1]
    o_r[0] = h0 + jnp.where(in0, 2.0 * e1 - 0.5 * e2, 0.0)
    o_r[1] = h1_ + jnp.where(in1, 2.0 * g0 - 0.5 * e1, 0.0)

    m11, m12, m21, m22, v1, v2 = p1, w1, p2, w2, y1, y2
    for reach in (1, 2, 4):
        a11, a12 = before(m11, reach, 1.0), before(m12, reach, 0.0)
        a21, a22 = before(m21, reach, 0.0), before(m22, reach, 1.0)
        u1, u2 = before(v1, reach, 0.0), before(v2, reach, 0.0)
        m11, m12, m21, m22, v1, v2 = (
            m11 * a11 + m12 * a21,
            m11 * a12 + m12 * a22,
            m21 * a11 + m22 * a21,
            m21 * a12 + m22 * a22,
            m11 * u1 + m12 * u2 + v1,
            m21 * u1 + m22 * u2 + v2,
        )
    pos_row = s_t[0:1, :] > 0.0

    def last(value):
        return jnp.where(pos_row, value[0:1, :], value[SEGS - 1 : SEGS, :])

    def first(value):
        return jnp.where(pos_row, value[SEGS - 1 : SEGS, :], value[0:1, :])

    for row, value in enumerate((m11, m12, m21, m22, v1, v2, g_end1, g_end2)):
        msg_ref[0, row : row + 1, :] = last(value)
    aux_ref[0] = jnp.zeros((8, width), f32)
    aux_ref[0, 0:1, :] = first(masks[0])
    aux_ref[0, 1:2, :] = first(masks[1])
    aux_ref[0, 2:3, :] = jnp.where(pos_row, 1.0, 0.0)

    y1, y2 = before(v1, 1, 0.0), before(v2, 1, 0.0)
    p1, p2 = before(m11, 1, 1.0), before(m21, 1, 0.0)
    w1, w2 = before(m12, 1, 0.0), before(m22, 1, 1.0)
    lane = lax.broadcasted_iota(jnp.int32, (SEGS, width), 1)
    real = lane < lines
    n1, n2 = jnp.where(real, p1, w1), jnp.where(real, p2, w2)
    for t in range(steps):
        c, rd = c_s[t], r_s[t]
        c1, c2 = 2.0 * c, -0.5 * c
        o_p[t] = m_s[t] + (h_s[t] + (2.0 * y1 - 0.5 * y2)) * rd
        o_x[t] = (2.0 * n1 - 0.5 * n2) * rd
        y1, y2 = (b_s[t] + c2 * y2) + c1 * y1, y1
        n1, n2 = c2 * n2 + c1 * n1, n1
    for t in range(steps // 2):
        for src, dst in ((o_p, t_p), (o_x, t_x), (o_r, t_r)):
            lo, hi = src[t], src[steps - 1 - t]
            dst[pl.ds(t, SEGS, stride=steps), :] = jnp.where(pos, hi, lo)
            dst[pl.ds(steps - 1 - t, SEGS, stride=steps), :] = jnp.where(pos, lo, hi)
    back = t_p[...].T
    part_ref[0, 0] = back[:lines]
    part_ref[1, 0] = back[lines:]
    lift_ref[0] = t_x[...].T
    back = t_r[...].T
    res_ref[0, 0] = back[:lines]
    res_ref[1, 0] = back[lines:]


def finish(count, *refs):
    got = refs[: count - 1]
    aux_ref, part_ref, lift_ref, res_ref, new_ref, out_ref = refs[count - 1 :]
    lines, cells = part_ref.shape[2], part_ref.shape[3]
    width = 2 * lines
    place = lax.axis_index("ax")
    aux = aux_ref[0]
    pos = aux[2:3, :] > 0.0
    z1 = jnp.zeros((1, width), jnp.float32)
    z2 = jnp.zeros((1, width), jnp.float32)
    g1, g2 = z1, z2
    for i in range(count - 1, 0, -1):
        low, high = got[i - 1][0], got[count - i - 1][0]
        m = jnp.where(pos, high, low)
        near = jnp.where(place >= i, 1.0, 0.0)
        far = jnp.where(place + i <= count - 1, 1.0, 0.0)
        has = jnp.where(pos, far, near) > 0.0
        n1 = m[0:1] * z1 + m[1:2] * z2 + m[4:5]
        n2 = m[2:3] * z1 + m[3:4] * z2 + m[5:6]
        z1, z2 = jnp.where(has, n1, z1), jnp.where(has, n2, z2)
        if i == 1:
            g1, g2 = jnp.where(has, m[6:7], 0.0), jnp.where(has, m[7:8], 0.0)
    r0 = aux[0:1] * (2.0 * g1 - 0.5 * g2)
    r1 = aux[1:2] * (-0.5 * g1)
    zero = jnp.zeros_like(z1)
    table = jnp.concatenate(
        [z1, z2, jnp.where(pos, 0.0, r0), jnp.where(pos, 0.0, r1),
         jnp.where(pos, r0, 0.0), jnp.where(pos, r1, 0.0), zero, zero], axis=0).T
    cell = lax.broadcasted_iota(jnp.int32, (lines, cells), 1)
    x1, x2 = lift_ref[0, :lines], lift_ref[0, lines:]
    for part in range(2):
        rows = table[part * lines : (part + 1) * lines]
        new_ref[part, 0] = part_ref[part, 0] + (x1 * rows[:, 0:1] + x2 * rows[:, 1:2])
        edge = jnp.where(cell == 0, rows[:, 2:3], 0.0)
        edge = jnp.where(cell == 1, rows[:, 3:4], edge)
        edge = jnp.where(cell == cells - 1, rows[:, 4:5], edge)
        edge = jnp.where(cell == cells - 2, rows[:, 5:6], edge)
        out_ref[part, 0] = res_ref[part, 0] + edge


def whole(shape):
    return pl.BlockSpec(shape, lambda k: (0,) * len(shape))


def shards(adjoint, source, speed, inverse_step, coupling, face_line, face_owner, line_length):
    lines, rows, cells = adjoint.shape
    vars_ = speed.shape[1]
    faces = face_line.shape[0]
    blocks = lax.axis_size("xs")
    count = lax.axis_size("ax")
    cap = max(1, faces // blocks)
    width = 2 * lines
    steps = cells // SEGS
    f32 = jnp.float32
    adj = jnp.transpose(adjoint, (1, 0, 2))
    src = jnp.transpose(source, (1, 0, 2))
    spd = jnp.transpose(speed, (1, 0, 2))
    inv = jnp.transpose(inverse_step, (1, 0, 2))
    cpl = jnp.transpose(coupling, (1, 0, 2))
    smem = pl.BlockSpec(memory_space=pltpu.SMEM)
    vmem = pl.BlockSpec(memory_space=pltpu.VMEM)
    packed = pl.pallas_call(
        functools.partial(pack_faces, blocks, cap),
        out_shape=jax.ShapeDtypeStruct((blocks * cap, PACK_ROWS, cells // 2), f32),
        in_specs=[smem, smem, vmem, vmem],
        out_specs=vmem,
        name="pack_faces",
    )(face_line, face_owner, adj, cpl)
    received = lax.all_to_all(packed, "xs", 0, 0, tiled=True)

    four = lambda x: x.reshape(2, vars_, lines, cells)
    pair = pl.BlockSpec((2, 1, lines, cells), lambda k: (0, k, 0, 0))
    single = pl.BlockSpec((1, lines, cells), lambda k: (k, 0, 0))
    small = pl.BlockSpec((1, 8, width), lambda k: (k, 0, 0))
    double = pl.BlockSpec((1, width, cells), lambda k: (k, 0, 0))
    small_shape = jax.ShapeDtypeStruct((vars_, 8, width), f32)
    pair_shape = jax.ShapeDtypeStruct((2, vars_, lines, cells), f32)
    turned = pltpu.VMEM((cells, width), f32)
    ordered = pltpu.VMEM((steps, SEGS, width), f32)
    msg, aux, part, lift, res = pl.pallas_call(
        sweep_maps,
        grid=(vars_,),
        out_shape=(small_shape, small_shape, pair_shape,
                   jax.ShapeDtypeStruct((vars_, width, cells), f32), pair_shape),
        in_specs=[whole((1, lines)), whole(received.shape), pair, pair, single, single],
        out_specs=(small, small, pair, double, pair),
        scratch_shapes=[turned] * 4 + [ordered] * 8 + [turned] * 3,
        name="sweep_maps",
    )(line_length.reshape(1, lines), received, four(adj), four(src), spd, inv)
    got = [
        lax.ppermute(msg, "ax", [(i, (i + k) % count) for i in range(count)])
        for k in range(1, count)
    ]
    new, out = pl.pallas_call(
        functools.partial(finish, count),
        grid=(vars_,),
        out_shape=(pair_shape, pair_shape),
        in_specs=[small] * count + [pair, double, pair],
        out_specs=(pair, pair),
        name="finish",
    )(*got, aux, part, lift, res)
    back = lambda x: jnp.transpose(x.reshape(rows, lines, cells), (1, 0, 2))
    return (back(new), back(out))


def solution(mesh):
    line = P("xs", None, "ax")
    in_specs = (line,) * 5 + (P("xs"),) * 3
    return jax.shard_map(
        shards, mesh=mesh, in_specs=in_specs, out_specs=(line, line), check_vma=False
    )
```

```python
import functools
import jax
import jax.numpy as jnp
from jax import lax
from jax.experimental import pallas as pl
from jax.experimental.pallas import tpu as pltpu
from jax.sharding import PartitionSpec as P

FACE_DEV = 8

frequency = 0.7
relaxation = 0.02

SEGS = 8
PACK_ROWS = 24
TABLE = 8
F32 = jnp.float32


def pack_faces(blocks, cap, paired, line_hbm, owner_hbm, adj_hbm, coup_hbm, *rest):
    adj_ref = rest[0]
    outs = rest[1:-5]
    stage, line_ref, owner_ref, coup_ref, sems = rest[-5:]
    vars_, faces, cells = coup_ref.shape
    half = cells // 2
    slots = FACE_DEV * blocks
    small = [
        pltpu.make_async_copy(owner_hbm, owner_ref, sems.at[0]),
        pltpu.make_async_copy(line_hbm, line_ref, sems.at[1]),
        pltpu.make_async_copy(coup_hbm, coup_ref, sems.at[2]),
    ]
    large = [
        pltpu.make_async_copy(adj_hbm.at[:, k], adj_ref.at[:, k], sems.at[3 + k])
        for k in range(vars_)
    ]
    for copy in small + large:
        copy.start()
    for copy in small[:2]:
        copy.wait()
    if blocks * cap != faces:
        for e in range(blocks * cap):
            stage[e, 16:24, :] = jnp.full((8, 128), -1.0, F32)
    dests, places = [], []
    for f in range(faces):
        slot = lax.rem(owner_ref[f], slots)
        dest = lax.div(slot, FACE_DEV)
        spot = jnp.int32(0)
        for other in dests:
            spot = spot + (other == dest).astype(jnp.int32)
        dests.append(dest)
        if paired:
            dest = lax.bitwise_xor(dest, lax.axis_index("xs"))
        entry = dest * cap + jnp.minimum(spot, cap - 1)
        places.append((entry, line_ref[f]))
        number = lax.rem(slot, FACE_DEV).astype(F32)
        stage[entry, 20:24, :] = jnp.full((4, 128), number, F32)
    small[2].wait()
    for k in range(vars_):
        large[k].wait()
        for f, (entry, line) in enumerate(places):
            c = coup_ref[k, f : f + 1, :]
            re = c * adj_ref[0, k, pl.ds(line, 1), :]
            im = c * adj_ref[1, k, pl.ds(line, 1), :]
            stage[entry, 4 * k : 4 * k + 1, :] = re[:, :half]
            stage[entry, 4 * k + 1 : 4 * k + 2, :] = re[:, half:]
            stage[entry, 4 * k + 2 : 4 * k + 3, :] = im[:, :half]
            stage[entry, 4 * k + 3 : 4 * k + 4, :] = im[:, half:]
    size = outs[0].shape[0]
    for i, out in enumerate(outs):
        out[...] = stage[i * size : (i + 1) * size]


def sort_halves(cap, sign_ref, *refs):
    *landed, near_ref, far_ref = refs
    for i, ref in enumerate(landed):
        near_ref[i * cap : (i + 1) * cap] = ref[:cap]
        far_ref[i * cap : (i + 1) * cap] = ref[cap:]


def cells_inside(len_ref, cells):
    row = len_ref[...].astype(F32)
    lines = row.shape[1]
    both = jnp.concatenate([row, row], axis=1)
    column = jnp.broadcast_to(both, (8, both.shape[1])).T[:lines, 0:1]
    cell = lax.axis_index("ax") * cells + lax.broadcasted_iota(jnp.int32, (lines, cells), 1)
    return cell.astype(F32) < column


def cell_terms(v, iv, a_re, a_im, q_re, q_im, inside):
    s = jnp.where(inside, jnp.abs(v), 0.0)
    rd = 1.0 / (iv + 1.5 * s)
    c = s * rd
    g_re, g_im = s * a_re, s * a_im
    h_re = jnp.where(inside, q_re, 0.0) - 1.5 * g_re
    h_im = jnp.where(inside, q_im, 0.0) - 1.5 * g_im
    scale = jnp.where(inside, relaxation * rd, 0.0)
    c2 = jnp.concatenate([c, c], axis=0)
    b2 = jnp.concatenate([g_re + c * h_re, g_im + c * h_im], axis=0)
    half = v.shape[1] // 2
    lane = lax.broadcasted_iota(jnp.int32, (2 * v.shape[0], half), 1)
    low = jnp.concatenate([g_re[:, :half], g_im[:, :half]], axis=0)
    high = jnp.concatenate([g_re[:, half:], g_im[:, half:]], axis=0)
    sign = jnp.concatenate([v[:, :half], v[:, :half]], axis=0)
    edges = jnp.where(lane < 2, low, jnp.where(lane >= half - 2, high, sign)).T
    return c2, b2, h_re, h_im, scale, edges


def orders(sign_row):
    width = sign_row.shape[1]
    pos = jnp.broadcast_to(sign_row, (SEGS, width)) > 0.0
    seg = lax.broadcasted_iota(jnp.int32, (SEGS, width), 0)
    return pos, jnp.where(pos, SEGS - 1 - seg, seg)


def before(value, reach, fill, pos, order):
    up = pltpu.roll(value, reach, 0)
    down = pltpu.roll(value, SEGS - reach, 0)
    return jnp.where(order >= reach, jnp.where(pos, down, up), fill)


def segment_scan(slots, c_t, b_t, c_s, b_s, poses):
    steps = c_s.shape[1]
    width = c_s.shape[3]
    zero = jnp.zeros((SEGS, width), F32)
    real = lax.broadcasted_iota(jnp.int32, (SEGS, width), 1) < width // 2
    first, second = jnp.where(real, 1.0, 0.0), jnp.where(real, 0.0, 1.0)
    state = [(zero, zero, first, second) for _ in slots]
    for t in range(steps):
        for i, k in enumerate(slots):
            pos = poses[i]
            y1, y2, n1, n2 = state[i]
            lo, hi = pl.ds(t, SEGS, stride=steps), pl.ds(steps - 1 - t, SEGS, stride=steps)
            cs, bs = c_t.at[k], b_t.at[k]
            c = jnp.where(pos, cs[hi, :], cs[lo, :])
            b = jnp.where(pos, bs[hi, :], bs[lo, :])
            c_s[k, t] = c
            b_s[k, t] = b
            c1, c2 = 2.0 * c, -0.5 * c
            state[i] = ((b + c2 * y2) + c1 * y1, y1, c2 * n2 + c1 * n1, n1)
    return state


def compose(state, pos, order):
    y1, y2, n1, n2 = state
    width = y1.shape[1]
    real = lax.broadcasted_iota(jnp.int32, (SEGS, width), 1) < width // 2
    o1, o2 = pltpu.roll(n1, width // 2, 1), pltpu.roll(n2, width // 2, 1)
    m11, m12 = jnp.where(real, n1, o1), jnp.where(real, o1, n1)
    m21, m22 = jnp.where(real, n2, o2), jnp.where(real, o2, n2)
    v1, v2 = y1, y2
    prev = functools.partial(before, pos=pos, order=order)
    for reach in (1, 2, 4):
        a11, a12 = prev(m11, reach, 1.0), prev(m12, reach, 0.0)
        a21, a22 = prev(m21, reach, 0.0), prev(m22, reach, 1.0)
        u1, u2 = prev(v1, reach, 0.0), prev(v2, reach, 0.0)
        m11, m12, m21, m22, v1, v2 = (
            m11 * a11 + m12 * a21,
            m11 * a12 + m12 * a22,
            m21 * a11 + m22 * a21,
            m21 * a12 + m22 * a22,
            m11 * u1 + m12 * u2 + v1,
            m21 * u1 + m22 * u2 + v2,
        )
    entry = (
        prev(v1, 1, 0.0),
        prev(v2, 1, 0.0),
        jnp.where(real, prev(m11, 1, 1.0), prev(m12, 1, 0.0)),
        jnp.where(real, prev(m21, 1, 0.0), prev(m22, 1, 1.0)),
    )
    return (m11, m12, m21, m22, v1, v2), entry


def put_maps(msg_ref, sign_ref, ent_ref, k, slot, state, edges):
    half = edges.shape[0]
    sign_row = edges[half // 2 : half // 2 + 1]
    pos, order = orders(sign_row)
    maps, entry = compose(state, pos, order)
    up = sign_row > 0.0
    for row, value in enumerate(maps):
        msg_ref[row, k : k + 1, :] = jnp.where(up, value[0:1], value[SEGS - 1 : SEGS])
    msg_ref[6, k : k + 1, :] = jnp.where(up, edges[0:1], edges[half - 1 : half])
    msg_ref[7, k : k + 1, :] = jnp.where(up, edges[1:2], edges[half - 2 : half - 1])
    sign_ref[k : k + 1, :] = sign_row
    for row, value in enumerate(entry):
        ent_ref[slot, row] = value


def main_maps(
    adj_ref, len_hbm, src_hbm, speed_hbm, inv_hbm,
    msg_ref, sign_ref, ent_ref, c_s, b_s, h_ref, scale_ref, in_ref, src_ref, speed_ref, inv_ref,
    c_t, b_t, len_ref, sems,
):
    vars_, lines, cells = speed_ref.shape
    first = pltpu.make_async_copy(len_hbm, len_ref, sems.at[0])
    first.start()
    copies = []
    for k in range(vars_):
        copies.append([
            pltpu.make_async_copy(speed_hbm.at[k], speed_ref.at[k], sems.at[3 * k + 1]),
            pltpu.make_async_copy(inv_hbm.at[k], inv_ref.at[k], sems.at[3 * k + 2]),
            pltpu.make_async_copy(src_hbm.at[:, k], src_ref.at[:, k], sems.at[3 * k + 3]),
        ])
        for copy in copies[k]:
            copy.start()
    first.wait()
    inside = cells_inside(len_ref, cells)
    in_ref[...] = jnp.where(inside, 1.0, 0.0)
    all_edges, poses = [], []
    for k in range(vars_):
        for copy in copies[k]:
            copy.wait()
        a_re, a_im = adj_ref[0, k], adj_ref[1, k]
        q_re = src_ref[0, k] + frequency * a_im
        q_im = src_ref[1, k] - frequency * a_re
        c2, b2, h_re, h_im, scale, edges = cell_terms(
            speed_ref[k], inv_ref[k], a_re, a_im, q_re, q_im, inside)
        h_ref[0, k], h_ref[1, k] = h_re, h_im
        scale_ref[k] = scale
        c_t[k] = c2.T
        b_t[k] = b2.T
        all_edges.append(edges)
        mid = edges.shape[0] // 2
        poses.append(orders(edges[mid : mid + 1])[0])
    states = segment_scan(range(vars_), c_t, b_t, c_s, b_s, poses)
    for k in range(vars_):
        put_maps(msg_ref, sign_ref, ent_ref, k, k, states[k], all_edges[k])


def face_maps(
    counts, in_ref, adj_ref, src_ref, speed_ref, inv_ref, old_msg, old_sign, *rest
):
    recv = rest[: len(counts)]
    msg_ref, sign_ref, ent_ref, c_s, b_s, h_ref, c_t, b_t = rest[len(counts) :]
    vars_, lines, cells = speed_ref.shape
    sub = lax.broadcasted_iota(jnp.int32, (FACE_DEV, 128), 0).astype(F32)
    acc = [jnp.zeros((FACE_DEV, 128), F32) for _ in range(4 * vars_)]
    for ref, number in zip(recv, counts):
        for e in range(number):
            hit = jnp.broadcast_to(ref[e, 20:21, :], (FACE_DEV, 128)) == sub
            for j in range(4 * vars_):
                row = jnp.broadcast_to(ref[e, j : j + 1, :], (FACE_DEV, 128))
                acc[j] = acc[j] + jnp.where(hit, row, 0.0)
    picks = [min(k, vars_ - 1) for k in range(lines // FACE_DEV)]

    def gather(ref):
        return jnp.concatenate([ref[k, :FACE_DEV] for k in picks], axis=0)

    def faces(j):
        return jnp.concatenate(
            [jnp.concatenate([acc[4 * k + j], acc[4 * k + j + 1]], axis=1) for k in picks], axis=0)

    a_re, a_im = gather(adj_ref.at[0]), gather(adj_ref.at[1])
    q_re = gather(src_ref.at[0]) + frequency * a_im - faces(0)
    q_im = gather(src_ref.at[1]) - frequency * a_re - faces(2)
    inside = jnp.concatenate([in_ref[:FACE_DEV]] * len(picks), axis=0) > 0.0
    c2, b2, h_re, h_im, _, edges = cell_terms(
        gather(speed_ref), gather(inv_ref), a_re, a_im, q_re, q_im, inside)
    h_ref[:lines], h_ref[lines:] = h_re, h_im
    c_t[0] = c2.T
    b_t[0] = b2.T
    mid = edges.shape[0] // 2
    state = segment_scan([0], c_t, b_t, c_s, b_s, [orders(edges[mid : mid + 1])[0]])[0]
    msg_ref[...] = old_msg[...]
    sign_ref[...] = old_sign[...]
    put_maps(msg_ref, sign_ref, ent_ref, vars_, 0, state, edges)


def substitute(
    in_ref, adj_ref, speed_ref, sign_ref, ent_ref, c_s, b_s, h_ref, scale_ref,
    ent_f, c_f, b_f, h_f, low_ref, high_ref,
    part_ref, lift_ref, out_hbm,
    u_s, x_s, u_t, x_t, out_ref, sems,
):
    vars_, lines, cells = speed_ref.shape
    steps, width = c_s.shape[1], c_s.shape[3]
    groups = vars_ + 1
    inside = in_ref[...] > 0.0
    lane = lax.broadcasted_iota(jnp.int32, (lines, cells), 1)
    place = lax.axis_index("ax")
    up_all = sign_ref[...] > 0.0
    near = jnp.where(place >= 1, 1.0, 0.0)
    far = jnp.where(place + 1 <= lax.axis_size("ax") - 1, 1.0, 0.0)
    has = jnp.where(up_all, far, near) > 0.0
    g1 = jnp.where(has, jnp.where(up_all, high_ref[6], low_ref[6]), 0.0)
    g2 = jnp.where(has, jnp.where(up_all, high_ref[7], low_ref[7]), 0.0)
    r0, r1 = 2.0 * g1 - 0.5 * g2, -0.5 * g1
    table = jnp.concatenate(
        [jnp.where(up_all, 0.0, r0), jnp.where(up_all, 0.0, r1),
         jnp.where(up_all, r0, 0.0), jnp.where(up_all, r1, 0.0)]
        + [jnp.zeros((TABLE, width), F32)] * (width // TABLE - 4), axis=0).T
    copies = []
    for k in range(vars_):
        v = speed_ref[k]
        s = jnp.where(inside, jnp.abs(v), 0.0)
        up = v > 0.0
        apart = lane != jnp.where(up, cells - 1, 0)

        def shifted(value):
            return jnp.where(
                apart, jnp.where(up, pltpu.roll(value, cells - 1, 1), pltpu.roll(value, 1, 1)), 0.0)

        for part in range(2):
            at = part * lines + FACE_DEV * k
            h = jnp.concatenate([h_f[at : at + FACE_DEV], h_ref[part, k, FACE_DEV:]], axis=0)
            g = s * adj_ref[part, k]
            rows = table[part * lines : (part + 1) * lines]
            column = lambda r: rows[:, TABLE * r + k : TABLE * r + k + 1]
            flux = shifted(2.0 * g - 0.5 * shifted(g))
            flux = jnp.where(lane == 0, flux + column(0), flux)
            flux = jnp.where(lane == 1, flux + column(1), flux)
            flux = jnp.where(lane == cells - 1, flux + column(2), flux)
            flux = jnp.where(lane == cells - 2, flux + column(3), flux)
            out_ref[part, k] = h + jnp.where(inside, flux, 0.0)
            copies.append(pltpu.make_async_copy(
                out_ref.at[part, k], out_hbm.at[part, k], sems.at[2 * k + part]))
            copies[-1].start()
    poses = [jnp.broadcast_to(sign_ref[k : k + 1, :], (SEGS, width)) > 0.0 for k in range(groups)]
    state = []
    for k in range(groups):
        ent = ent_ref.at[k] if k < vars_ else ent_f.at[0]
        state.append([ent[r] for r in range(4)])
    for t in range(steps):
        lo = pl.ds(steps - 1 - t, SEGS, stride=steps)
        hi = pl.ds(t, SEGS, stride=steps)
        for k in range(groups):
            main = k < vars_
            c = c_s[k, t] if main else c_f[0, t]
            b = b_s[k, t] if main else b_f[0, t]
            y1, y2, n1, n2 = state[k]
            u = 2.0 * y1 - 0.5 * y2
            x = 2.0 * n1 - 0.5 * n2
            new = c * u + b
            state[k] = [new, y1, c * x if main else n1, n1]
            for value, keep, turned in ((u, u_s, u_t), (x, x_s, x_t))[: 2 if main else 1]:
                if t < steps // 2:
                    keep[k, t] = value
                else:
                    other = keep[k, steps - 1 - t]
                    turned.at[k][lo, :] = jnp.where(poses[k], value, other)
                    turned.at[k][hi, :] = jnp.where(poses[k], other, value)
    face_u = u_t[vars_].T
    for k in range(vars_):
        scale = scale_ref[k]
        u = u_t[k].T
        x = x_t[k].T
        for part in range(2):
            at = part * lines + FACE_DEV * k
            lift_ref[part, k] = x[part * lines : (part + 1) * lines] * scale
            h = jnp.concatenate([h_f[at : at + FACE_DEV], h_ref[part, k, FACE_DEV:]], axis=0)
            us = jnp.concatenate(
                [face_u[at : at + FACE_DEV], u[part * lines + FACE_DEV : (part + 1) * lines]], axis=0)
            part_ref[part, k] = jnp.where(inside, adj_ref[part, k], 0.0) + (h + us) * scale
    for copy in copies:
        copy.wait()


def finish(count, sign_ref, part_ref, lift_ref, *rest):
    got = rest[: count - 1]
    new_hbm, new_ref, sems = rest[count - 1 :]
    _, vars_, lines, cells = part_ref.shape
    width = 2 * lines
    place = lax.axis_index("ax")
    pos = sign_ref[...] > 0.0
    zero = jnp.zeros((TABLE, width), F32)
    z1, z2 = zero, zero
    for i in range(count - 1, 0, -1):
        low, high = got[i - 1], got[count - i - 1]
        near = jnp.where(place >= i, 1.0, 0.0)
        far = jnp.where(place + i <= count - 1, 1.0, 0.0)
        has = jnp.where(pos, far, near) > 0.0
        m = [jnp.where(pos, high[r], low[r]) for r in range(6)]
        n1 = m[0] * z1 + m[1] * z2 + m[4]
        n2 = m[2] * z1 + m[3] * z2 + m[5]
        z1, z2 = jnp.where(has, n1, z1), jnp.where(has, n2, z2)
    table = jnp.concatenate([z1, z2] + [zero] * (width // TABLE - 2), axis=0).T
    copies = []
    for k in range(vars_):
        for part in range(2):
            at = part * lines + FACE_DEV * k

            def entering(r):
                face, main = TABLE * r + vars_, TABLE * r + k
                return jnp.concatenate(
                    [table[at : at + FACE_DEV, face : face + 1],
                     table[part * lines + FACE_DEV : (part + 1) * lines, main : main + 1]], axis=0)

            new_ref[part, k] = part_ref[part, k] + (
                lift_ref[0, k] * entering(0) + lift_ref[1, k] * entering(1))
            copies.append(pltpu.make_async_copy(
                new_ref.at[part, k], new_hbm.at[part, k], sems.at[2 * k + part]))
            copies[-1].start()
    for copy in copies:
        copy.wait()


def shards(adjoint, source, speed, inverse_step, coupling, face_line, face_owner, line_length):
    lines, rows, cells = adjoint.shape
    vars_ = speed.shape[1]
    faces = face_line.shape[0]
    blocks = lax.axis_size("xs")
    count = lax.axis_size("ax")
    cap = max(1, faces // blocks)
    width = 2 * lines
    steps = cells // SEGS
    adj = jnp.transpose(adjoint, (1, 0, 2)).reshape(2, vars_, lines, cells)
    src = jnp.transpose(source, (1, 0, 2)).reshape(2, vars_, lines, cells)
    spd = jnp.transpose(speed, (1, 0, 2))
    inv = jnp.transpose(inverse_step, (1, 0, 2))
    cpl = jnp.transpose(coupling, (1, 0, 2))
    vmem = pl.BlockSpec(memory_space=pltpu.VMEM)
    hbm = pl.BlockSpec(memory_space=pltpu.HBM)
    stay = lambda x: pltpu.with_memory_space_constraint(x, pltpu.HBM)
    shape = lambda *dims: jax.ShapeDtypeStruct(dims, F32)
    scratch = lambda *dims: pltpu.VMEM(dims, F32)
    dma = lambda number: pltpu.SemaphoreType.DMA((number,))
    limit = lambda mib: pltpu.CompilerParams(vmem_limit_bytes=mib << 20)
    cost = lambda flops, moved: pl.CostEstimate(
        flops=flops, bytes_accessed=moved, transcendentals=0)
    table_shape = shape(8, TABLE, width)
    sign_shape = shape(TABLE, width)
    order_shape = shape(vars_, steps, SEGS, width)
    field_shape = shape(2, vars_, lines, cells)
    var_shape = shape(vars_, lines, cells)
    face_order = shape(1, steps, SEGS, width)
    paired = blocks == 8
    entries = blocks * cap
    pieces = blocks // 2 if paired else 1
    adj, *packed = pl.pallas_call(
        functools.partial(pack_faces, blocks, cap, paired),
        out_shape=[field_shape] + [shape(entries // pieces, PACK_ROWS, cells // 2)] * pieces,
        in_specs=[hbm] * 4,
        out_specs=[vmem] * (1 + pieces),
        scratch_shapes=[scratch(entries, PACK_ROWS, cells // 2), pltpu.SMEM((faces,), jnp.int32),
                        pltpu.SMEM((faces,), jnp.int32), scratch(vars_, faces, cells), dma(3 + vars_)],
        compiler_params=limit(6),
        name="pack_faces",
    )(stay(face_line), stay(face_owner), stay(adj), stay(cpl))
    hop = lambda x, m: lax.ppermute(x, "xs", [(i, i ^ m) for i in range(blocks)])
    if paired:
        landed = [packed[0]] + [hop(packed[m], 2 * m) for m in range(1, pieces)]
    msg, sign, ent, c_s, b_s, h, scale, mask, src, spd, inv = pl.pallas_call(
        main_maps,
        out_shape=[table_shape, sign_shape, shape(vars_, 4, SEGS, width), order_shape, order_shape,
                   field_shape, var_shape, shape(lines, cells), field_shape, var_shape, var_shape],
        in_specs=[vmem] + [hbm] * 4,
        out_specs=[vmem] * 11,
        scratch_shapes=[scratch(vars_, cells, width)] * 2
        + [pltpu.VMEM((1, lines), jnp.int32), dma(1 + 3 * vars_)],
        compiler_params=limit(14),
        cost_estimate=cost(2 * 10**6, 4 * 10**6),
        name="main_maps",
    )(adj, stay(line_length.reshape(1, lines)), stay(src), stay(spd), stay(inv))
    if paired:
        halves = shape(pieces * cap, PACK_ROWS, cells // 2)
        near_half, far_half = pl.pallas_call(
            functools.partial(sort_halves, cap),
            out_shape=[halves] * 2,
            in_specs=[vmem] * (1 + pieces),
            out_specs=[vmem] * 2,
            compiler_params=limit(4),
            name="sort_halves",
        )(sign, *landed)
        recv, counts = [near_half, hop(far_half, 1)], [pieces * cap] * 2
    else:
        recv, counts = [lax.all_to_all(packed[0], "xs", 0, 0, tiled=True)], [entries]
    msg, sign, ent_f, c_f, b_f, h_f = pl.pallas_call(
        functools.partial(face_maps, counts),
        out_shape=[table_shape, sign_shape, shape(1, 4, SEGS, width), face_order, face_order,
                   shape(width, cells)],
        in_specs=[vmem] * (7 + len(recv)),
        out_specs=[vmem] * 6,
        scratch_shapes=[scratch(1, cells, width)] * 2,
        compiler_params=limit(10),
        name="face_maps",
    )(mask, adj, src, spd, inv, msg, sign, *recv)
    shift = lambda k: lax.ppermute(msg, "ax", [(i, (i + k) % count) for i in range(count)])
    got = [shift(k) for k in range(1, count)]
    kept = scratch(vars_ + 1, steps // 2, SEGS, width)
    part, lift, out = pl.pallas_call(
        substitute,
        out_shape=[field_shape] * 3,
        in_specs=[vmem] * 15,
        out_specs=[vmem] * 2 + [hbm],
        scratch_shapes=[kept, kept, scratch(vars_ + 1, cells, width), scratch(vars_, cells, width),
                        scratch(2, vars_, lines, cells), dma(2 * vars_)],
        compiler_params=limit(18),
        cost_estimate=cost(2 * 10**6, 5 * 10**6),
        name="substitute",
    )(mask, adj, spd, sign, ent, c_s, b_s, h, scale, ent_f, c_f, b_f, h_f, got[0], got[-1])
    new = pl.pallas_call(
        functools.partial(finish, count),
        out_shape=field_shape,
        in_specs=[vmem] * (3 + len(got)),
        out_specs=hbm,
        scratch_shapes=[scratch(2, vars_, lines, cells), dma(2 * vars_)],
        compiler_params=limit(6),
        name="finish",
    )(sign, part, lift, *got)
    back = lambda x: jnp.transpose(x.reshape(rows, lines, cells), (1, 0, 2))
    return (back(new), back(out))


def solution(mesh):
    line = P("xs", None, "ax")
    in_specs = (line,) * 5 + (P("xs"),) * 3
    return jax.shard_map(
        shards, mesh=mesh, in_specs=in_specs, out_specs=(line, line), check_vma=False
    )
```

```python
import functools
import jax
import jax.numpy as jnp
from jax import lax
from jax.experimental import pallas as pl
from jax.experimental.pallas import tpu as pltpu
from jax.sharding import PartitionSpec as P

FACE_DEV = 8

frequency = 0.7
relaxation = 0.02

SEGS = 8
PACK_ROWS = 24
TABLE = 8
F32 = jnp.float32


def pack_faces(blocks, cap, paired, line_hbm, owner_hbm, adj_hbm, coup_hbm, len_hbm, *rest):
    adj_ref, len_ref = rest[:2]
    outs = rest[2:-5]
    stage, line_ref, owner_ref, coup_ref, sems = rest[-5:]
    vars_, faces, cells = coup_ref.shape
    half = cells // 2
    slots = FACE_DEV * blocks
    small = [
        pltpu.make_async_copy(owner_hbm, owner_ref, sems.at[0]),
        pltpu.make_async_copy(line_hbm, line_ref, sems.at[1]),
        pltpu.make_async_copy(coup_hbm, coup_ref, sems.at[2]),
        pltpu.make_async_copy(len_hbm, len_ref, sems.at[3]),
    ]
    large = [
        pltpu.make_async_copy(adj_hbm.at[:, k], adj_ref.at[:, k], sems.at[4 + k])
        for k in range(vars_)
    ]
    for copy in small + large:
        copy.start()
    for copy in small[:2]:
        copy.wait()
    if blocks * cap != faces:
        for e in range(blocks * cap):
            stage[e, 16:24, :] = jnp.full((8, 128), -1.0, F32)
    dests, places = [], []
    for f in range(faces):
        slot = lax.rem(owner_ref[f], slots)
        dest = lax.div(slot, FACE_DEV)
        spot = jnp.int32(0)
        for other in dests:
            spot = spot + (other == dest).astype(jnp.int32)
        dests.append(dest)
        if paired:
            dest = lax.bitwise_xor(dest, lax.axis_index("xs"))
        entry = dest * cap + jnp.minimum(spot, cap - 1)
        places.append((entry, line_ref[f]))
        number = lax.rem(slot, FACE_DEV).astype(F32)
        stage[entry, 20:24, :] = jnp.full((4, 128), number, F32)
    small[2].wait()
    for k in range(vars_):
        large[k].wait()
        for f, (entry, line) in enumerate(places):
            c = coup_ref[k, f : f + 1, :]
            re = c * adj_ref[0, k, pl.ds(line, 1), :]
            im = c * adj_ref[1, k, pl.ds(line, 1), :]
            stage[entry, 4 * k : 4 * k + 1, :] = re[:, :half]
            stage[entry, 4 * k + 1 : 4 * k + 2, :] = re[:, half:]
            stage[entry, 4 * k + 2 : 4 * k + 3, :] = im[:, :half]
            stage[entry, 4 * k + 3 : 4 * k + 4, :] = im[:, half:]
    small[3].wait()
    size = outs[0].shape[0]
    for i, out in enumerate(outs):
        out[...] = stage[i * size : (i + 1) * size]


def sort_halves(cap, sign_ref, *refs):
    *landed, near_ref, far_ref = refs
    for i, ref in enumerate(landed):
        near_ref[i * cap : (i + 1) * cap] = ref[:cap]
        far_ref[i * cap : (i + 1) * cap] = ref[cap:]


def cells_inside(len_ref, cells):
    row = len_ref[...].astype(F32)
    lines = row.shape[1]
    both = jnp.concatenate([row, row], axis=1)
    column = jnp.broadcast_to(both, (8, both.shape[1])).T[:lines, 0:1]
    cell = lax.axis_index("ax") * cells + lax.broadcasted_iota(jnp.int32, (lines, cells), 1)
    return cell.astype(F32) < column


def coefficients(v, iv, a_re, a_im, inside):
    s = jnp.where(inside, jnp.abs(v), 0.0)
    rd = 1.0 / (iv + 1.5 * s)
    c = s * rd
    g_re, g_im = s * a_re, s * a_im
    scale = jnp.where(inside, relaxation * rd, 0.0)
    half = v.shape[1] // 2
    lane = lax.broadcasted_iota(jnp.int32, (2 * v.shape[0], half), 1)
    low = jnp.concatenate([g_re[:, :half], g_im[:, :half]], axis=0)
    high = jnp.concatenate([g_re[:, half:], g_im[:, half:]], axis=0)
    sign = jnp.concatenate([v[:, :half], v[:, :half]], axis=0)
    edges = jnp.where(lane < 2, low, jnp.where(lane >= half - 2, high, sign)).T
    return c, scale, g_re, g_im, edges


def drives(c, g, q, inside):
    h = jnp.where(inside, q, 0.0) - 1.5 * g
    return h, g + c * h


def doubled(x):
    return jnp.concatenate([x, x], axis=0)


def orders(sign_row):
    width = sign_row.shape[1]
    pos = jnp.broadcast_to(sign_row, (SEGS, width)) > 0.0
    seg = lax.broadcasted_iota(jnp.int32, (SEGS, width), 0)
    return pos, jnp.where(pos, SEGS - 1 - seg, seg)


def before(value, reach, fill, pos, order):
    up = pltpu.roll(value, reach, 0)
    down = pltpu.roll(value, SEGS - reach, 0)
    return jnp.where(order >= reach, jnp.where(pos, down, up), fill)


def segment_scan(slots, c_t, b_t, c_s, b_s, poses):
    steps = c_s.shape[1]
    width = c_s.shape[3]
    zero = jnp.zeros((SEGS, width), F32)
    real = lax.broadcasted_iota(jnp.int32, (SEGS, width), 1) < width // 2
    first, second = jnp.where(real, 1.0, 0.0), jnp.where(real, 0.0, 1.0)
    state = [(zero, zero, first, second) for _ in slots]
    for t in range(steps):
        for i, k in enumerate(slots):
            pos = poses[i]
            y1, y2, n1, n2 = state[i]
            lo, hi = pl.ds(t, SEGS, stride=steps), pl.ds(steps - 1 - t, SEGS, stride=steps)
            cs, bs = c_t.at[k], b_t.at[k]
            c = jnp.where(pos, cs[hi, :], cs[lo, :])
            b = jnp.where(pos, bs[hi, :], bs[lo, :])
            c_s[k, t] = c
            b_s[k, t] = b
            c1, c2 = 2.0 * c, -0.5 * c
            state[i] = ((b + c2 * y2) + c1 * y1, y1, c2 * n2 + c1 * n1, n1)
    return state


def compose(state, pos, order):
    y1, y2, n1, n2 = state
    width = y1.shape[1]
    real = lax.broadcasted_iota(jnp.int32, (SEGS, width), 1) < width // 2
    o1, o2 = pltpu.roll(n1, width // 2, 1), pltpu.roll(n2, width // 2, 1)
    m11, m12 = jnp.where(real, n1, o1), jnp.where(real, o1, n1)
    m21, m22 = jnp.where(real, n2, o2), jnp.where(real, o2, n2)
    v1, v2 = y1, y2
    prev = functools.partial(before, pos=pos, order=order)
    for reach in (1, 2, 4):
        a11, a12 = prev(m11, reach, 1.0), prev(m12, reach, 0.0)
        a21, a22 = prev(m21, reach, 0.0), prev(m22, reach, 1.0)
        u1, u2 = prev(v1, reach, 0.0), prev(v2, reach, 0.0)
        m11, m12, m21, m22, v1, v2 = (
            m11 * a11 + m12 * a21,
            m11 * a12 + m12 * a22,
            m21 * a11 + m22 * a21,
            m21 * a12 + m22 * a22,
            m11 * u1 + m12 * u2 + v1,
            m21 * u1 + m22 * u2 + v2,
        )
    entry = (
        prev(v1, 1, 0.0),
        prev(v2, 1, 0.0),
        jnp.where(real, prev(m11, 1, 1.0), prev(m12, 1, 0.0)),
        jnp.where(real, prev(m21, 1, 0.0), prev(m22, 1, 1.0)),
    )
    return (m11, m12, m21, m22, v1, v2), entry


def put_maps(msg_ref, sign_ref, ent_ref, k, slot, state, edges):
    half = edges.shape[0]
    sign_row = edges[half // 2 : half // 2 + 1]
    pos, order = orders(sign_row)
    maps, entry = compose(state, pos, order)
    up = sign_row > 0.0
    for row, value in enumerate(maps):
        msg_ref[row, k : k + 1, :] = jnp.where(up, value[0:1], value[SEGS - 1 : SEGS])
    msg_ref[6, k : k + 1, :] = jnp.where(up, edges[0:1], edges[half - 1 : half])
    msg_ref[7, k : k + 1, :] = jnp.where(up, edges[1:2], edges[half - 2 : half - 1])
    sign_ref[k : k + 1, :] = sign_row
    for row, value in enumerate(entry):
        ent_ref[slot, row] = value


def main_maps(
    adj_ref, len_ref, speed_ref, inv_ref, src_hbm,
    msg_ref, sign_ref, ent_ref, c_s, b_s, h_ref, scale_ref, in_ref, src_ref,
    c_n, c_t, b_t, sems,
):
    vars_, lines, cells = speed_ref.shape
    copies = [
        pltpu.make_async_copy(src_hbm.at[:, k], src_ref.at[:, k], sems.at[k]) for k in range(vars_)
    ]
    for copy in copies:
        copy.start()
    inside = cells_inside(len_ref, cells)
    in_ref[...] = jnp.where(inside, 1.0, 0.0)
    all_edges, poses = [], []
    for k in range(vars_):
        c, scale, g_re, g_im, edges = coefficients(
            speed_ref[k], inv_ref[k], adj_ref[0, k], adj_ref[1, k], inside)
        c_t[k] = doubled(c).T
        h_ref[0, k], h_ref[1, k] = g_re, g_im
        c_n[k] = c
        scale_ref[k] = scale
        all_edges.append(edges)
        mid = edges.shape[0] // 2
        poses.append(orders(edges[mid : mid + 1])[0])
    for k in range(vars_):
        copies[k].wait()
        c = c_n[k]
        h_re, b_re = drives(c, h_ref[0, k], src_ref[0, k] + frequency * adj_ref[1, k], inside)
        h_im, b_im = drives(c, h_ref[1, k], src_ref[1, k] - frequency * adj_ref[0, k], inside)
        h_ref[0, k], h_ref[1, k] = h_re, h_im
        b_t[k] = jnp.concatenate([b_re, b_im], axis=0).T
    states = segment_scan(range(vars_), c_t, b_t, c_s, b_s, poses)
    for k in range(vars_):
        put_maps(msg_ref, sign_ref, ent_ref, k, k, states[k], all_edges[k])


def face_maps(
    counts, lift_ref, in_ref, adj_ref, src_ref, speed_ref, inv_ref, old_msg, old_sign, *rest
):
    recv = rest[: len(counts)]
    msg_ref, sign_ref, ent_ref, c_s, b_s, h_ref, c_t, b_t = rest[len(counts) :]
    vars_, lines, cells = speed_ref.shape
    sub = lax.broadcasted_iota(jnp.int32, (FACE_DEV, 128), 0).astype(F32)
    acc = [jnp.zeros((FACE_DEV, 128), F32) for _ in range(4 * vars_)]
    for ref, number in zip(recv, counts):
        for e in range(number):
            hit = jnp.broadcast_to(ref[e, 20:21, :], (FACE_DEV, 128)) == sub
            for j in range(4 * vars_):
                row = jnp.broadcast_to(ref[e, j : j + 1, :], (FACE_DEV, 128))
                acc[j] = acc[j] + jnp.where(hit, row, 0.0)
    picks = [min(k, vars_ - 1) for k in range(lines // FACE_DEV)]

    def gather(ref):
        return jnp.concatenate([ref[k, :FACE_DEV] for k in picks], axis=0)

    def faces(j):
        return jnp.concatenate(
            [jnp.concatenate([acc[4 * k + j], acc[4 * k + j + 1]], axis=1) for k in picks], axis=0)

    a_re, a_im = gather(adj_ref.at[0]), gather(adj_ref.at[1])
    q_re = gather(src_ref.at[0]) + frequency * a_im - faces(0)
    q_im = gather(src_ref.at[1]) - frequency * a_re - faces(2)
    inside = jnp.concatenate([in_ref[:FACE_DEV]] * len(picks), axis=0) > 0.0
    c, _, g_re, g_im, edges = coefficients(
        gather(speed_ref), gather(inv_ref), a_re, a_im, inside)
    h_re, b_re = drives(c, g_re, q_re, inside)
    h_im, b_im = drives(c, g_im, q_im, inside)
    h_ref[:lines], h_ref[lines:] = h_re, h_im
    c_t[0] = doubled(c).T
    b_t[0] = jnp.concatenate([b_re, b_im], axis=0).T
    mid = edges.shape[0] // 2
    state = segment_scan([0], c_t, b_t, c_s, b_s, [orders(edges[mid : mid + 1])[0]])[0]
    msg_ref[...] = old_msg[...]
    sign_ref[...] = old_sign[...]
    put_maps(msg_ref, sign_ref, ent_ref, vars_, 0, state, edges)


def unfold(k, t, steps, value, kept, turned, pos):
    if t < steps // 2:
        kept[k, t] = value
    else:
        other = kept[k, steps - 1 - t]
        turned.at[k][pl.ds(steps - 1 - t, SEGS, stride=steps), :] = jnp.where(pos, value, other)
        turned.at[k][pl.ds(t, SEGS, stride=steps), :] = jnp.where(pos, other, value)


def lifts(sign_ref, ent_ref, c_s, scale_ref, after_ref, lift_ref, x_s, x_t):
    vars_, lines, cells = scale_ref.shape
    steps, width = c_s.shape[1], c_s.shape[3]
    poses = [jnp.broadcast_to(sign_ref[k : k + 1, :], (SEGS, width)) > 0.0 for k in range(vars_)]
    state = [(ent_ref[k, 2], ent_ref[k, 3]) for k in range(vars_)]
    for t in range(steps):
        for k in range(vars_):
            n1, n2 = state[k]
            x = 2.0 * n1 - 0.5 * n2
            state[k] = (c_s[k, t] * x, n1)
            unfold(k, t, steps, x, x_s, x_t, poses[k])
    for k in range(vars_):
        x = x_t[k].T
        for part in range(2):
            lift_ref[part, k] = x[part * lines : (part + 1) * lines] * scale_ref[k]


def substitute(
    in_ref, adj_ref, speed_ref, sign_ref, ent_ref, c_s, b_s, h_ref, scale_ref,
    ent_f, c_f, b_f, h_f,
    part_ref, res_ref,
    u_s, u_t,
):
    vars_, lines, cells = speed_ref.shape
    steps, width = c_s.shape[1], c_s.shape[3]
    groups = vars_ + 1
    inside = in_ref[...] > 0.0
    lane = lax.broadcasted_iota(jnp.int32, (lines, cells), 1)
    poses = [jnp.broadcast_to(sign_ref[k : k + 1, :], (SEGS, width)) > 0.0 for k in range(groups)]
    state = []
    for k in range(groups):
        ent = ent_ref.at[k] if k < vars_ else ent_f.at[0]
        state.append((ent[0], ent[1]))
    for t in range(steps):
        for k in range(groups):
            main = k < vars_
            c = c_s[k, t] if main else c_f[0, t]
            b = b_s[k, t] if main else b_f[0, t]
            y1, y2 = state[k]
            u = 2.0 * y1 - 0.5 * y2
            state[k] = (c * u + b, y1)
            unfold(k, t, steps, u, u_s, u_t, poses[k])
    face_u = u_t[vars_].T
    for k in range(vars_):
        scale = scale_ref[k]
        v = speed_ref[k]
        s = jnp.where(inside, jnp.abs(v), 0.0)
        up = v > 0.0
        apart = lane != jnp.where(up, cells - 1, 0)

        def shifted(value):
            return jnp.where(
                apart, jnp.where(up, pltpu.roll(value, cells - 1, 1), pltpu.roll(value, 1, 1)), 0.0)

        u = u_t[k].T
        for part in range(2):
            at = part * lines + FACE_DEV * k
            h = jnp.concatenate([h_f[at : at + FACE_DEV], h_ref[part, k, FACE_DEV:]], axis=0)
            us = jnp.concatenate(
                [face_u[at : at + FACE_DEV], u[part * lines + FACE_DEV : (part + 1) * lines]], axis=0)
            a = adj_ref[part, k]
            part_ref[part, k] = jnp.where(inside, a, 0.0) + (h + us) * scale
            g = s * a
            res_ref[part, k] = h + jnp.where(inside, shifted(2.0 * g - 0.5 * shifted(g)), 0.0)


def finish(count, pairwise, in_ref, sign_ref, part_ref, lift_ref, res_ref, *rest):
    got = rest[: count - 1]
    new_hbm, out_hbm, new_ref, out_ref, sems = rest[count - 1 :]
    _, vars_, lines, cells = part_ref.shape
    width = 2 * lines
    place = lax.axis_index("ax")
    odd = lax.rem(place, 2) == 1
    pos = sign_ref[...] > 0.0
    zero = jnp.zeros((TABLE, width), F32)
    z1, z2, g1, g2 = zero, zero, zero, zero
    for i in range(count - 1, 0, -1):
        near = jnp.where(place >= i, 1.0, 0.0)
        far = jnp.where(place + i <= count - 1, 1.0, 0.0)
        has = jnp.where(pos, far, near) > 0.0

        def field(r):
            if not pairwise:
                return jnp.where(pos, got[count - i - 1][r], got[i - 1][r])
            if i > 1:
                return got[i - 1][r]
            one, three = got[0][r], got[2][r]
            return jnp.where(pos, jnp.where(odd, three, one), jnp.where(odd, one, three))

        m = [field(r) for r in range(8 if i == 1 else 6)]
        n1 = m[0] * z1 + m[1] * z2 + m[4]
        n2 = m[2] * z1 + m[3] * z2 + m[5]
        z1, z2 = jnp.where(has, n1, z1), jnp.where(has, n2, z2)
        if i == 1:
            g1, g2 = jnp.where(has, m[6], 0.0), jnp.where(has, m[7], 0.0)
    r0, r1 = 2.0 * g1 - 0.5 * g2, -0.5 * g1
    table = jnp.concatenate(
        [z1, z2, jnp.where(pos, 0.0, r0), jnp.where(pos, 0.0, r1),
         jnp.where(pos, r0, 0.0), jnp.where(pos, r1, 0.0)]
        + [zero] * (width // TABLE - 6), axis=0).T
    half = cells // 2
    lane = lax.broadcasted_iota(jnp.int32, (lines, half), 1)
    copies = []
    for k in range(vars_):
        for part in range(2):
            at = part * lines + FACE_DEV * k
            rows = slice(part * lines, (part + 1) * lines)
            halo = lambda r: table[rows, TABLE * r + k : TABLE * r + k + 1]

            def entering(r):
                face = TABLE * r + vars_
                return jnp.concatenate(
                    [table[at : at + FACE_DEV, face : face + 1], halo(r)[FACE_DEV:]], axis=0)

            low = jnp.where(lane == 0, halo(2), jnp.where(lane == 1, halo(3), 0.0))
            high = jnp.where(lane == half - 1, halo(4), jnp.where(lane == half - 2, halo(5), 0.0))
            out_ref[part, k, :, :half] = res_ref[part, k, :, :half] + low * in_ref[:, :half]
            out_ref[part, k, :, half:] = res_ref[part, k, :, half:] + high * in_ref[:, half:]
            new_ref[part, k] = part_ref[part, k] + (
                lift_ref[0, k] * entering(0) + lift_ref[1, k] * entering(1))
            for j, (src, dst) in enumerate(((out_ref, out_hbm), (new_ref, new_hbm))):
                copies.append(pltpu.make_async_copy(
                    src.at[part, k], dst.at[part, k], sems.at[4 * k + 2 * part + j]))
                copies[-1].start()
    for copy in copies:
        copy.wait()


def shards(adjoint, source, speed, inverse_step, coupling, face_line, face_owner, line_length):
    lines, rows, cells = adjoint.shape
    vars_ = speed.shape[1]
    faces = face_line.shape[0]
    blocks = lax.axis_size("xs")
    count = lax.axis_size("ax")
    cap = max(1, faces // blocks)
    width = 2 * lines
    steps = cells // SEGS
    adj = jnp.transpose(adjoint, (1, 0, 2)).reshape(2, vars_, lines, cells)
    src = jnp.transpose(source, (1, 0, 2)).reshape(2, vars_, lines, cells)
    spd = jnp.transpose(speed, (1, 0, 2))
    inv = jnp.transpose(inverse_step, (1, 0, 2))
    cpl = jnp.transpose(coupling, (1, 0, 2))
    vmem = pl.BlockSpec(memory_space=pltpu.VMEM)
    hbm = pl.BlockSpec(memory_space=pltpu.HBM)
    stay = lambda x: pltpu.with_memory_space_constraint(x, pltpu.HBM)
    shape = lambda *dims: jax.ShapeDtypeStruct(dims, F32)
    scratch = lambda *dims: pltpu.VMEM(dims, F32)
    dma = lambda number: pltpu.SemaphoreType.DMA((number,))
    limit = lambda mib: pltpu.CompilerParams(vmem_limit_bytes=mib << 20)
    cost = lambda flops, moved: pl.CostEstimate(
        flops=flops, bytes_accessed=moved, transcendentals=0)
    table_shape = shape(8, TABLE, width)
    sign_shape = shape(TABLE, width)
    order_shape = shape(vars_, steps, SEGS, width)
    field_shape = shape(2, vars_, lines, cells)
    var_shape = shape(vars_, lines, cells)
    face_order = shape(1, steps, SEGS, width)
    paired = blocks == 8
    entries = blocks * cap
    pieces = blocks // 2 if paired else 1
    adj, lengths, *packed = pl.pallas_call(
        functools.partial(pack_faces, blocks, cap, paired),
        out_shape=[field_shape, jax.ShapeDtypeStruct((1, lines), jnp.int32)]
        + [shape(entries // pieces, PACK_ROWS, cells // 2)] * pieces,
        in_specs=[hbm] * 5,
        out_specs=[vmem] * (2 + pieces),
        scratch_shapes=[scratch(entries, PACK_ROWS, cells // 2), pltpu.SMEM((faces,), jnp.int32),
                        pltpu.SMEM((faces,), jnp.int32), scratch(vars_, faces, cells), dma(4 + vars_)],
        compiler_params=limit(6),
        cost_estimate=cost(2 * 10**6, 4 * 10**6),
        name="pack_faces",
    )(stay(face_line), stay(face_owner), stay(adj), stay(cpl), stay(line_length.reshape(1, lines)))
    hop = lambda x, m: lax.ppermute(x, "xs", [(i, i ^ m) for i in range(blocks)])
    if paired:
        landed = [packed[0]] + [hop(packed[m], 2 * m) for m in range(1, pieces)]
    msg, sign, ent, c_s, b_s, h, scale, mask, src = pl.pallas_call(
        main_maps,
        out_shape=[table_shape, sign_shape, shape(vars_, 4, SEGS, width), order_shape, order_shape,
                   field_shape, var_shape, shape(lines, cells), field_shape],
        in_specs=[vmem] * 4 + [hbm],
        out_specs=[vmem] * 9,
        scratch_shapes=[scratch(vars_, lines, cells)] + [scratch(vars_, cells, width)] * 2
        + [dma(vars_)],
        compiler_params=limit(14),
        cost_estimate=cost(2 * 10**6, 4 * 10**6),
        name="main_maps",
    )(adj, lengths, spd, inv, stay(src))
    if paired:
        halves = shape(pieces * cap, PACK_ROWS, cells // 2)
        near_half, far_half = pl.pallas_call(
            functools.partial(sort_halves, cap),
            out_shape=[halves] * 2,
            in_specs=[vmem] * (1 + pieces),
            out_specs=[vmem] * 2,
            compiler_params=limit(4),
            name="sort_halves",
        )(sign, *landed)
        recv, counts, after = [near_half, hop(far_half, 1)], [pieces * cap] * 2, near_half
    else:
        recv, counts, after = [lax.all_to_all(packed[0], "xs", 0, 0, tiled=True)], [entries], packed[0]
    kept = lambda number: scratch(number, steps // 2, SEGS, width)
    lift = pl.pallas_call(
        lifts,
        out_shape=field_shape,
        in_specs=[vmem] * 5,
        out_specs=vmem,
        scratch_shapes=[kept(vars_), scratch(vars_, cells, width)],
        compiler_params=limit(8),
        cost_estimate=cost(10**6, 2 * 10**6),
        name="lifts",
    )(sign, ent, c_s, scale, after)
    msg, sign, ent_f, c_f, b_f, h_f = pl.pallas_call(
        functools.partial(face_maps, counts),
        out_shape=[table_shape, sign_shape, shape(1, 4, SEGS, width), face_order, face_order,
                   shape(width, cells)],
        in_specs=[vmem] * (8 + len(recv)),
        out_specs=[vmem] * 6,
        scratch_shapes=[scratch(1, cells, width)] * 2,
        compiler_params=limit(10),
        name="face_maps",
    )(lift, mask, adj, src, spd, inv, msg, sign, *recv)
    pairwise = count == 4
    meet = (lambda i, k: i ^ k) if pairwise else (lambda i, k: (i + k) % count)
    got = [
        lax.ppermute(msg, "ax", [(i, meet(i, k)) for i in range(count)]) for k in range(1, count)
    ]
    part, res = pl.pallas_call(
        substitute,
        out_shape=[field_shape] * 2,
        in_specs=[vmem] * 13,
        out_specs=[vmem] * 2,
        scratch_shapes=[kept(vars_ + 1), scratch(vars_ + 1, cells, width)],
        compiler_params=limit(14),
        cost_estimate=cost(2 * 10**6, 5 * 10**6),
        name="substitute",
    )(mask, adj, spd, sign, ent, c_s, b_s, h, scale, ent_f, c_f, b_f, h_f)
    new, out = pl.pallas_call(
        functools.partial(finish, count, pairwise),
        out_shape=[field_shape] * 2,
        in_specs=[vmem] * (5 + len(got)),
        out_specs=[hbm] * 2,
        scratch_shapes=[scratch(2, vars_, lines, cells)] * 2 + [dma(4 * vars_)],
        compiler_params=limit(8),
        name="finish",
    )(mask, sign, part, lift, res, *got)
    back = lambda x: jnp.transpose(x.reshape(rows, lines, cells), (1, 0, 2))
    return (back(new), back(out))


def solution(mesh):
    line = P("xs", None, "ax")
    in_specs = (line,) * 5 + (P("xs"),) * 3
    return jax.shard_map(
        shards, mesh=mesh, in_specs=in_specs, out_specs=(line, line), check_vma=False
    )
```

```python
import functools
import jax
import jax.numpy as jnp
from jax import lax
from jax.experimental import pallas as pl
from jax.experimental.pallas import tpu as pltpu
from jax.sharding import PartitionSpec as P

FACE_DEV = 8

frequency = 0.7
relaxation = 0.02

SEGS = 8
PACK_ROWS = 24
TABLE = 8
F32 = jnp.float32


def pack_faces(blocks, cap, paired, line_hbm, owner_hbm, adj_hbm, coup_hbm, len_hbm, inv_hbm, *rest):
    adj_ref, len_ref, inv_ref, stage = rest[:4]
    line_ref, owner_ref, coup_ref, sems = rest[4:]
    vars_, faces, cells = coup_ref.shape
    half = cells // 2
    slots = FACE_DEV * blocks
    small = [
        pltpu.make_async_copy(owner_hbm, owner_ref, sems.at[0]),
        pltpu.make_async_copy(line_hbm, line_ref, sems.at[1]),
        pltpu.make_async_copy(coup_hbm, coup_ref, sems.at[2]),
        pltpu.make_async_copy(len_hbm, len_ref, sems.at[3]),
    ]
    large = [
        pltpu.make_async_copy(adj_hbm.at[:, k], adj_ref.at[:, k], sems.at[4 + k])
        for k in range(vars_)
    ]
    step = pltpu.make_async_copy(inv_hbm, inv_ref, sems.at[4 + vars_])
    for copy in small + large + [step]:
        copy.start()
    for copy in small[:2]:
        copy.wait()
    if blocks * cap != faces:
        for e in range(blocks * cap):
            stage[e, 16:24, :] = jnp.full((8, 128), -1.0, F32)
    dests, places = [], []
    for f in range(faces):
        slot = lax.rem(owner_ref[f], slots)
        dest = lax.div(slot, FACE_DEV)
        spot = jnp.int32(0)
        for other in dests:
            spot = spot + (other == dest).astype(jnp.int32)
        dests.append(dest)
        if paired:
            dest = lax.bitwise_xor(dest, lax.axis_index("xs"))
        entry = dest * cap + jnp.minimum(spot, cap - 1)
        places.append((entry, line_ref[f]))
        number = lax.rem(slot, FACE_DEV).astype(F32)
        stage[entry, 20:24, :] = jnp.full((4, 128), number, F32)
    small[2].wait()
    for k in range(vars_):
        large[k].wait()
        for f, (entry, line) in enumerate(places):
            c = coup_ref[k, f : f + 1, :]
            re = c * adj_ref[0, k, pl.ds(line, 1), :]
            im = c * adj_ref[1, k, pl.ds(line, 1), :]
            stage[entry, 4 * k : 4 * k + 1, :] = re[:, :half]
            stage[entry, 4 * k + 1 : 4 * k + 2, :] = re[:, half:]
            stage[entry, 4 * k + 2 : 4 * k + 3, :] = im[:, :half]
            stage[entry, 4 * k + 3 : 4 * k + 4, :] = im[:, half:]
    small[3].wait()
    step.wait()


def deal(packed_ref, *outs):
    size = outs[0].shape[0]
    for i, out in enumerate(outs):
        out[...] = packed_ref[i * size : (i + 1) * size]


def sort_halves(cap, after_ref, *refs):
    *landed, near_ref, far_ref = refs
    for i, ref in enumerate(landed):
        near_ref[i * cap : (i + 1) * cap] = ref[:cap]
        far_ref[i * cap : (i + 1) * cap] = ref[cap:]


def cells_inside(len_ref, cells):
    row = len_ref[...].astype(F32)
    lines = row.shape[1]
    both = jnp.concatenate([row, row], axis=1)
    column = jnp.broadcast_to(both, (8, both.shape[1])).T[:lines, 0:1]
    cell = lax.axis_index("ax") * cells + lax.broadcasted_iota(jnp.int32, (lines, cells), 1)
    return cell.astype(F32) < column


def coefficients(v, iv, a_re, a_im, inside):
    s = jnp.where(inside, jnp.abs(v), 0.0)
    rd = 1.0 / (iv + 1.5 * s)
    c = s * rd
    g_re, g_im = s * a_re, s * a_im
    scale = jnp.where(inside, relaxation * rd, 0.0)
    half = v.shape[1] // 2
    lane = lax.broadcasted_iota(jnp.int32, (2 * v.shape[0], half), 1)
    low = jnp.concatenate([g_re[:, :half], g_im[:, :half]], axis=0)
    high = jnp.concatenate([g_re[:, half:], g_im[:, half:]], axis=0)
    sign = jnp.concatenate([v[:, :half], v[:, :half]], axis=0)
    edges = jnp.where(lane < 2, low, jnp.where(lane >= half - 2, high, sign)).T
    return c, scale, g_re, g_im, edges


def drives(c, g, q, inside):
    h = jnp.where(inside, q, 0.0) - 1.5 * g
    return h, g + c * h


def doubled(x):
    return jnp.concatenate([x, x], axis=0)


def orders(sign_row):
    width = sign_row.shape[1]
    pos = jnp.broadcast_to(sign_row, (SEGS, width)) > 0.0
    seg = lax.broadcasted_iota(jnp.int32, (SEGS, width), 0)
    return pos, jnp.where(pos, SEGS - 1 - seg, seg)


def before(value, reach, fill, pos, order):
    up = pltpu.roll(value, reach, 0)
    down = pltpu.roll(value, SEGS - reach, 0)
    return jnp.where(order >= reach, jnp.where(pos, down, up), fill)


def segment_scan(slots, c_t, b_t, c_s, b_s, poses):
    steps = c_s.shape[1]
    width = c_s.shape[3]
    zero = jnp.zeros((SEGS, width), F32)
    real = lax.broadcasted_iota(jnp.int32, (SEGS, width), 1) < width // 2
    first, second = jnp.where(real, 1.0, 0.0), jnp.where(real, 0.0, 1.0)
    state = [(zero, zero, first, second) for _ in slots]
    for t in range(steps):
        for i, k in enumerate(slots):
            pos = poses[i]
            y1, y2, n1, n2 = state[i]
            lo, hi = pl.ds(t, SEGS, stride=steps), pl.ds(steps - 1 - t, SEGS, stride=steps)
            cs, bs = c_t.at[k], b_t.at[k]
            c = jnp.where(pos, cs[hi, :], cs[lo, :])
            b = jnp.where(pos, bs[hi, :], bs[lo, :])
            c_s[k, t] = c
            b_s[k, t] = b
            c1, c2 = 2.0 * c, -0.5 * c
            state[i] = ((b + c2 * y2) + c1 * y1, y1, c2 * n2 + c1 * n1, n1)
    return state


def compose(state, pos, order):
    y1, y2, n1, n2 = state
    width = y1.shape[1]
    real = lax.broadcasted_iota(jnp.int32, (SEGS, width), 1) < width // 2
    o1, o2 = pltpu.roll(n1, width // 2, 1), pltpu.roll(n2, width // 2, 1)
    m11, m12 = jnp.where(real, n1, o1), jnp.where(real, o1, n1)
    m21, m22 = jnp.where(real, n2, o2), jnp.where(real, o2, n2)
    v1, v2 = y1, y2
    prev = functools.partial(before, pos=pos, order=order)
    for reach in (1, 2, 4):
        a11, a12 = prev(m11, reach, 1.0), prev(m12, reach, 0.0)
        a21, a22 = prev(m21, reach, 0.0), prev(m22, reach, 1.0)
        u1, u2 = prev(v1, reach, 0.0), prev(v2, reach, 0.0)
        m11, m12, m21, m22, v1, v2 = (
            m11 * a11 + m12 * a21,
            m11 * a12 + m12 * a22,
            m21 * a11 + m22 * a21,
            m21 * a12 + m22 * a22,
            m11 * u1 + m12 * u2 + v1,
            m21 * u1 + m22 * u2 + v2,
        )
    entry = (
        prev(v1, 1, 0.0),
        prev(v2, 1, 0.0),
        jnp.where(real, prev(m11, 1, 1.0), prev(m12, 1, 0.0)),
        jnp.where(real, prev(m21, 1, 0.0), prev(m22, 1, 1.0)),
    )
    return (m11, m12, m21, m22, v1, v2), entry


def put_maps(msg_ref, sign_ref, ent_ref, k, slot, state, edges):
    half = edges.shape[0]
    sign_row = edges[half // 2 : half // 2 + 1]
    pos, order = orders(sign_row)
    maps, entry = compose(state, pos, order)
    up = sign_row > 0.0
    for row, value in enumerate(maps):
        msg_ref[row, k : k + 1, :] = jnp.where(up, value[0:1], value[SEGS - 1 : SEGS])
    msg_ref[6, k : k + 1, :] = jnp.where(up, edges[0:1], edges[half - 1 : half])
    msg_ref[7, k : k + 1, :] = jnp.where(up, edges[1:2], edges[half - 2 : half - 1])
    sign_ref[k : k + 1, :] = sign_row
    for row, value in enumerate(entry):
        ent_ref[slot, row] = value


def main_maps(
    adj_ref, len_ref, src_ref, speed_ref, inv_ref,
    msg_ref, sign_ref, ent_ref, c_s, b_s, h_ref, scale_ref, in_ref,
    c_t, b_t,
):
    vars_, lines, cells = speed_ref.shape
    inside = cells_inside(len_ref, cells)
    in_ref[...] = jnp.where(inside, 1.0, 0.0)
    all_edges, poses = [], []
    for k in range(vars_):
        a_re, a_im = adj_ref[0, k], adj_ref[1, k]
        c, scale, g_re, g_im, edges = coefficients(speed_ref[k], inv_ref[k], a_re, a_im, inside)
        h_re, b_re = drives(c, g_re, src_ref[0, k] + frequency * a_im, inside)
        h_im, b_im = drives(c, g_im, src_ref[1, k] - frequency * a_re, inside)
        h_ref[0, k], h_ref[1, k] = h_re, h_im
        scale_ref[k] = scale
        c_t[k] = doubled(c).T
        b_t[k] = jnp.concatenate([b_re, b_im], axis=0).T
        all_edges.append(edges)
        mid = edges.shape[0] // 2
        poses.append(orders(edges[mid : mid + 1])[0])
    states = segment_scan(range(vars_), c_t, b_t, c_s, b_s, poses)
    for k in range(vars_):
        put_maps(msg_ref, sign_ref, ent_ref, k, k, states[k], all_edges[k])


def face_maps(
    counts, lift_ref, in_ref, adj_ref, src_ref, speed_ref, inv_ref, old_msg, old_sign, *rest
):
    recv = rest[: len(counts)]
    msg_ref, sign_ref, ent_ref, c_s, b_s, h_ref, c_t, b_t = rest[len(counts) :]
    vars_, lines, cells = speed_ref.shape
    sub = lax.broadcasted_iota(jnp.int32, (FACE_DEV, 128), 0).astype(F32)
    acc = [jnp.zeros((FACE_DEV, 128), F32) for _ in range(4 * vars_)]
    for ref, number in zip(recv, counts):
        for e in range(number):
            hit = jnp.broadcast_to(ref[e, 20:21, :], (FACE_DEV, 128)) == sub
            for j in range(4 * vars_):
                row = jnp.broadcast_to(ref[e, j : j + 1, :], (FACE_DEV, 128))
                acc[j] = acc[j] + jnp.where(hit, row, 0.0)
    picks = [min(k, vars_ - 1) for k in range(lines // FACE_DEV)]

    def gather(ref):
        return jnp.concatenate([ref[k, :FACE_DEV] for k in picks], axis=0)

    def faces(j):
        return jnp.concatenate(
            [jnp.concatenate([acc[4 * k + j], acc[4 * k + j + 1]], axis=1) for k in picks], axis=0)

    a_re, a_im = gather(adj_ref.at[0]), gather(adj_ref.at[1])
    q_re = gather(src_ref.at[0]) + frequency * a_im - faces(0)
    q_im = gather(src_ref.at[1]) - frequency * a_re - faces(2)
    inside = jnp.concatenate([in_ref[:FACE_DEV]] * len(picks), axis=0) > 0.0
    c, _, g_re, g_im, edges = coefficients(
        gather(speed_ref), gather(inv_ref), a_re, a_im, inside)
    h_re, b_re = drives(c, g_re, q_re, inside)
    h_im, b_im = drives(c, g_im, q_im, inside)
    h_ref[:lines], h_ref[lines:] = h_re, h_im
    c_t[0] = doubled(c).T
    b_t[0] = jnp.concatenate([b_re, b_im], axis=0).T
    mid = edges.shape[0] // 2
    state = segment_scan([0], c_t, b_t, c_s, b_s, [orders(edges[mid : mid + 1])[0]])[0]
    msg_ref[...] = old_msg[...]
    sign_ref[...] = old_sign[...]
    put_maps(msg_ref, sign_ref, ent_ref, vars_, 0, state, edges)


def unfold(k, t, steps, value, kept, turned, pos):
    if t < steps // 2:
        kept[k, t] = value
    else:
        other = kept[k, steps - 1 - t]
        turned.at[k][pl.ds(steps - 1 - t, SEGS, stride=steps), :] = jnp.where(pos, value, other)
        turned.at[k][pl.ds(t, SEGS, stride=steps), :] = jnp.where(pos, other, value)


def lifts(sign_ref, ent_ref, c_s, scale_ref, after_ref, lift_ref, x_s, x_t):
    vars_, lines, cells = scale_ref.shape
    steps, width = c_s.shape[1], c_s.shape[3]
    poses = [jnp.broadcast_to(sign_ref[k : k + 1, :], (SEGS, width)) > 0.0 for k in range(vars_)]
    state = [(ent_ref[k, 2], ent_ref[k, 3]) for k in range(vars_)]
    for t in range(steps):
        for k in range(vars_):
            n1, n2 = state[k]
            x = 2.0 * n1 - 0.5 * n2
            state[k] = (c_s[k, t] * x, n1)
            unfold(k, t, steps, x, x_s, x_t, poses[k])
    for k in range(vars_):
        x = x_t[k].T
        for part in range(2):
            lift_ref[part, k] = x[part * lines : (part + 1) * lines] * scale_ref[k]


def substitute(
    in_ref, adj_ref, sign_ref, ent_ref, c_s, b_s, h_ref, scale_ref, ent_f, c_f, b_f, h_f,
    part_ref, u_s, u_t,
):
    vars_, lines, cells = scale_ref.shape
    steps, width = c_s.shape[1], c_s.shape[3]
    groups = vars_ + 1
    inside = in_ref[...] > 0.0
    poses = [jnp.broadcast_to(sign_ref[k : k + 1, :], (SEGS, width)) > 0.0 for k in range(groups)]
    state = []
    for k in range(groups):
        ent = ent_ref.at[k] if k < vars_ else ent_f.at[0]
        state.append((ent[0], ent[1]))
    for t in range(steps):
        for k in range(groups):
            main = k < vars_
            c = c_s[k, t] if main else c_f[0, t]
            b = b_s[k, t] if main else b_f[0, t]
            y1, y2 = state[k]
            u = 2.0 * y1 - 0.5 * y2
            state[k] = (c * u + b, y1)
            unfold(k, t, steps, u, u_s, u_t, poses[k])
    face_u = u_t[vars_].T
    for k in range(vars_):
        scale = scale_ref[k]
        u = u_t[k].T
        for part in range(2):
            at = part * lines + FACE_DEV * k
            h = jnp.concatenate([h_f[at : at + FACE_DEV], h_ref[part, k, FACE_DEV:]], axis=0)
            us = jnp.concatenate(
                [face_u[at : at + FACE_DEV], u[part * lines + FACE_DEV : (part + 1) * lines]], axis=0)
            part_ref[part, k] = jnp.where(inside, adj_ref[part, k], 0.0) + (h + us) * scale


def fluxes(after_ref, in_ref, adj_ref, speed_ref, flux_ref):
    vars_, lines, cells = speed_ref.shape
    half = cells // 2
    lane = lax.broadcasted_iota(jnp.int32, (lines, half), 1)
    for k in range(vars_):
        v = speed_ref[k]
        s = jnp.abs(v) * in_ref[...]
        up = v[:, :half] > 0.0
        last = jnp.where(up, lane, 0) == half - 1
        first = jnp.where(up, 1, lane) == 0

        def shifted(low, high):
            low, high = (
                jnp.where(up, pltpu.roll(x, half - 1, 1), pltpu.roll(x, 1, 1)) for x in (low, high))
            return (jnp.where(last, high, jnp.where(first, 0.0, low)),
                    jnp.where(first, low, jnp.where(last, 0.0, high)))

        for part in range(2):
            g = s * adj_ref[part, k]
            low, high = g[:, :half], g[:, half:]
            near = shifted(low, high)
            low, high = shifted(2.0 * low - 0.5 * near[0], 2.0 * high - 0.5 * near[1])
            flux_ref[part, k, :, :half] = low * in_ref[:, :half]
            flux_ref[part, k, :, half:] = high * in_ref[:, half:]


def finish(count, pairwise, in_ref, sign_ref, part_ref, lift_ref, h_ref, h_f, flux_ref, *rest):
    got = rest[: count - 1]
    new_hbm, out_hbm, new_ref, out_ref, sems = rest[count - 1 :]
    _, vars_, lines, cells = part_ref.shape
    width = 2 * lines
    place = lax.axis_index("ax")
    odd = lax.rem(place, 2) == 1
    pos = sign_ref[...] > 0.0
    zero = jnp.zeros((TABLE, width), F32)
    z1, z2, g1, g2 = zero, zero, zero, zero
    for i in range(count - 1, 0, -1):
        near = jnp.where(place >= i, 1.0, 0.0)
        far = jnp.where(place + i <= count - 1, 1.0, 0.0)
        has = jnp.where(pos, far, near) > 0.0

        def field(r):
            if not pairwise:
                return jnp.where(pos, got[count - i - 1][r], got[i - 1][r])
            if i > 1:
                return got[i - 1][r]
            one, three = got[0][r], got[2][r]
            return jnp.where(pos, jnp.where(odd, three, one), jnp.where(odd, one, three))

        m = [field(r) for r in range(8 if i == 1 else 6)]
        n1 = m[0] * z1 + m[1] * z2 + m[4]
        n2 = m[2] * z1 + m[3] * z2 + m[5]
        z1, z2 = jnp.where(has, n1, z1), jnp.where(has, n2, z2)
        if i == 1:
            g1, g2 = jnp.where(has, m[6], 0.0), jnp.where(has, m[7], 0.0)
    r0, r1 = 2.0 * g1 - 0.5 * g2, -0.5 * g1
    down0, down1 = jnp.where(pos, 0.0, r0), jnp.where(pos, 0.0, r1)
    up0, up1 = jnp.where(pos, r0, 0.0), jnp.where(pos, r1, 0.0)
    table = jnp.concatenate([z1, z2, jnp.zeros((width - 2 * TABLE, width), F32)], axis=0).T
    half = cells // 2
    sub = lax.broadcasted_iota(jnp.int32, (8, width), 0)
    left = lax.broadcasted_iota(jnp.int32, (lines, half), 1) < half // 2
    copies = []
    for k in range(vars_):
        row = lambda x: jnp.broadcast_to(x[k : k + 1, :], (8, width))
        low = jnp.where(sub == 0, row(down0), jnp.where(sub == 1, row(down1), 0.0))
        high = jnp.where(sub == 7, row(up0), jnp.where(sub == 6, row(up1), 0.0))
        edges = jnp.concatenate([low, jnp.zeros((half - 16, width), F32), high], axis=0).T
        for part in range(2):
            at = part * lines + FACE_DEV * k
            rows = slice(part * lines, (part + 1) * lines)

            def entering(r):
                face, main = TABLE * r + vars_, TABLE * r + k
                return jnp.concatenate(
                    [table[at : at + FACE_DEV, face : face + 1],
                     table[part * lines + FACE_DEV : (part + 1) * lines, main : main + 1]], axis=0)

            edge = edges[rows]
            h = jnp.concatenate([h_f[at : at + FACE_DEV], h_ref[part, k, FACE_DEV:]], axis=0)
            h = h + flux_ref[part, k]
            out_ref[part, k, :, :half] = h[:, :half] + jnp.where(left, edge, 0.0) * in_ref[:, :half]
            out_ref[part, k, :, half:] = h[:, half:] + jnp.where(left, 0.0, edge) * in_ref[:, half:]
            new_ref[part, k] = part_ref[part, k] + (
                lift_ref[0, k] * entering(0) + lift_ref[1, k] * entering(1))
            for j, (src, dst) in enumerate(((out_ref, out_hbm), (new_ref, new_hbm))):
                copies.append(pltpu.make_async_copy(
                    src.at[part, k], dst.at[part, k], sems.at[4 * k + 2 * part + j]))
                copies[-1].start()
    for copy in copies:
        copy.wait()


def shards(adjoint, source, speed, inverse_step, coupling, face_line, face_owner, line_length):
    lines, rows, cells = adjoint.shape
    vars_ = speed.shape[1]
    faces = face_line.shape[0]
    blocks = lax.axis_size("xs")
    count = lax.axis_size("ax")
    cap = max(1, faces // blocks)
    width = 2 * lines
    steps = cells // SEGS
    adj = jnp.transpose(adjoint, (1, 0, 2)).reshape(2, vars_, lines, cells)
    src = jnp.transpose(source, (1, 0, 2)).reshape(2, vars_, lines, cells)
    spd = jnp.transpose(speed, (1, 0, 2))
    inv = jnp.transpose(inverse_step, (1, 0, 2))
    cpl = jnp.transpose(coupling, (1, 0, 2))
    vmem = pl.BlockSpec(memory_space=pltpu.VMEM)
    hbm = pl.BlockSpec(memory_space=pltpu.HBM)
    stay = lambda x: pltpu.with_memory_space_constraint(x, pltpu.HBM)
    shape = lambda *dims: jax.ShapeDtypeStruct(dims, F32)
    scratch = lambda *dims: pltpu.VMEM(dims, F32)
    dma = lambda number: pltpu.SemaphoreType.DMA((number,))
    limit = lambda mib: pltpu.CompilerParams(vmem_limit_bytes=mib << 20)
    cost = lambda flops, moved: pl.CostEstimate(
        flops=flops, bytes_accessed=moved, transcendentals=0)
    table_shape = shape(8, TABLE, width)
    sign_shape = shape(TABLE, width)
    order_shape = shape(vars_, steps, SEGS, width)
    field_shape = shape(2, vars_, lines, cells)
    var_shape = shape(vars_, lines, cells)
    face_order = shape(1, steps, SEGS, width)
    paired = blocks == 8
    entries = blocks * cap
    pieces = blocks // 2 if paired else 1
    adj, lengths, inv, packed = pl.pallas_call(
        functools.partial(pack_faces, blocks, cap, paired),
        out_shape=[field_shape, jax.ShapeDtypeStruct((1, lines), jnp.int32), var_shape,
                   shape(entries, PACK_ROWS, cells // 2)],
        in_specs=[hbm] * 6,
        out_specs=[vmem] * 4,
        scratch_shapes=[pltpu.SMEM((faces,), jnp.int32), pltpu.SMEM((faces,), jnp.int32),
                        scratch(vars_, faces, cells), dma(5 + vars_)],
        compiler_params=limit(6),
        name="pack_faces",
    )(stay(face_line), stay(face_owner), stay(adj), stay(cpl), stay(line_length.reshape(1, lines)),
      stay(inv))
    packed = pl.pallas_call(
        deal,
        out_shape=[shape(entries // pieces, PACK_ROWS, cells // 2)] * pieces,
        in_specs=[vmem],
        out_specs=[vmem] * pieces,
        compiler_params=limit(4),
        cost_estimate=cost(2 * 10**6, 4 * 10**7),
        name="deal",
    )(packed)
    hop = lambda x, m: lax.ppermute(x, "xs", [(i, i ^ m) for i in range(blocks)])
    if paired:
        landed = [packed[0]] + [hop(packed[m], 2 * m) for m in range(1, pieces)]
    msg, sign, ent, c_s, b_s, h, scale, mask = pl.pallas_call(
        main_maps,
        out_shape=[table_shape, sign_shape, shape(vars_, 4, SEGS, width), order_shape, order_shape,
                   field_shape, var_shape, shape(lines, cells)],
        in_specs=[vmem] * 5,
        out_specs=[vmem] * 8,
        scratch_shapes=[scratch(vars_, cells, width)] * 2,
        compiler_params=limit(14),
        cost_estimate=cost(2 * 10**6, 4 * 10**6),
        name="main_maps",
    )(adj, lengths, src, spd, inv)
    if paired:
        halves = shape(pieces * cap, PACK_ROWS, cells // 2)
        near_half, far_half = pl.pallas_call(
            functools.partial(sort_halves, cap),
            out_shape=[halves] * 2,
            in_specs=[vmem] * (1 + pieces),
            out_specs=[vmem] * 2,
            compiler_params=limit(4),
            name="sort_halves",
        )(sign, *landed)
        recv, counts, after = [near_half, hop(far_half, 1)], [pieces * cap] * 2, near_half
    else:
        recv, counts, after = [lax.all_to_all(packed[0], "xs", 0, 0, tiled=True)], [entries], packed[0]
    kept = lambda number: scratch(number, steps // 2, SEGS, width)
    lift = pl.pallas_call(
        lifts,
        out_shape=field_shape,
        in_specs=[vmem] * 5,
        out_specs=vmem,
        scratch_shapes=[kept(vars_), scratch(vars_, cells, width)],
        compiler_params=limit(8),
        cost_estimate=cost(10**6, 2 * 10**6),
        name="lifts",
    )(sign, ent, c_s, scale, after)
    msg, sign, ent_f, c_f, b_f, h_f = pl.pallas_call(
        functools.partial(face_maps, counts),
        out_shape=[table_shape, sign_shape, shape(1, 4, SEGS, width), face_order, face_order,
                   shape(width, cells)],
        in_specs=[vmem] * (8 + len(recv)),
        out_specs=[vmem] * 6,
        scratch_shapes=[scratch(1, cells, width)] * 2,
        compiler_params=limit(10),
        name="face_maps",
    )(lift, mask, adj, src, spd, inv, msg, sign, *recv)
    pairwise = count == 4
    meet = (lambda i, k: i ^ k) if pairwise else (lambda i, k: (i + k) % count)
    got = [
        lax.ppermute(msg, "ax", [(i, meet(i, k)) for i in range(count)]) for k in range(1, count)
    ]
    part = pl.pallas_call(
        substitute,
        out_shape=field_shape,
        in_specs=[vmem] * 12,
        out_specs=vmem,
        scratch_shapes=[kept(vars_ + 1), scratch(vars_ + 1, cells, width)],
        compiler_params=limit(14),
        cost_estimate=cost(2 * 10**6, 3 * 10**6),
        name="substitute",
    )(mask, adj, sign, ent, c_s, b_s, h, scale, ent_f, c_f, b_f, h_f)
    flux = pl.pallas_call(
        fluxes,
        out_shape=field_shape,
        in_specs=[vmem] * 4,
        out_specs=vmem,
        compiler_params=limit(6),
        cost_estimate=cost(10**6, 2 * 10**6),
        name="fluxes",
    )(part, mask, adj, spd)
    new, out = pl.pallas_call(
        functools.partial(finish, count, pairwise),
        out_shape=[field_shape] * 2,
        in_specs=[vmem] * (7 + len(got)),
        out_specs=[hbm] * 2,
        scratch_shapes=[scratch(2, vars_, lines, cells)] * 2 + [dma(4 * vars_)],
        compiler_params=limit(10),
        name="finish",
    )(mask, sign, part, lift, h, h_f, flux, *got)
    back = lambda x: jnp.transpose(x.reshape(rows, lines, cells), (1, 0, 2))
    return (back(new), back(out))


def solution(mesh):
    line = P("xs", None, "ax")
    in_specs = (line,) * 5 + (P("xs"),) * 3
    return jax.shard_map(
        shards, mesh=mesh, in_specs=in_specs, out_specs=(line, line), check_vma=False
    )
```

```python
import functools
import jax
import jax.numpy as jnp
from jax import lax
from jax.experimental import pallas as pl
from jax.experimental.pallas import tpu as pltpu
from jax.sharding import PartitionSpec as P

FACE_DEV = 8

frequency = 0.7
relaxation = 0.02

SEGS = 8
PACK_ROWS = 24
TABLE = 8
F32 = jnp.float32


def pack_faces(blocks, cap, paired, line_hbm, owner_hbm, adj_hbm, coup_hbm, len_hbm, inv_hbm, *rest):
    adj_ref, len_ref, inv_ref, stage = rest[:4]
    line_ref, owner_ref, coup_ref, sems = rest[4:]
    vars_, faces, cells = coup_ref.shape
    half = cells // 2
    slots = FACE_DEV * blocks
    small = [
        pltpu.make_async_copy(owner_hbm, owner_ref, sems.at[0]),
        pltpu.make_async_copy(line_hbm, line_ref, sems.at[1]),
        pltpu.make_async_copy(coup_hbm, coup_ref, sems.at[2]),
        pltpu.make_async_copy(len_hbm, len_ref, sems.at[3]),
    ]
    large = [
        pltpu.make_async_copy(adj_hbm.at[:, k], adj_ref.at[:, k], sems.at[4 + k])
        for k in range(vars_)
    ]
    step = pltpu.make_async_copy(inv_hbm, inv_ref, sems.at[4 + vars_])
    for copy in small + large + [step]:
        copy.start()
    for copy in small[:2]:
        copy.wait()
    if blocks * cap != faces:
        for e in range(blocks * cap):
            stage[e, 16:24, :] = jnp.full((8, 128), -1.0, F32)
    dests, places = [], []
    for f in range(faces):
        slot = lax.rem(owner_ref[f], slots)
        dest = lax.div(slot, FACE_DEV)
        spot = jnp.int32(0)
        for other in dests:
            spot = spot + (other == dest).astype(jnp.int32)
        dests.append(dest)
        if paired:
            dest = lax.bitwise_xor(dest, lax.axis_index("xs"))
        entry = dest * cap + jnp.minimum(spot, cap - 1)
        places.append((entry, line_ref[f]))
        number = lax.rem(slot, FACE_DEV).astype(F32)
        stage[entry, 20:24, :] = jnp.full((4, 128), number, F32)
    small[2].wait()
    for k in range(vars_):
        large[k].wait()
        for f, (entry, line) in enumerate(places):
            c = coup_ref[k, f : f + 1, :]
            re = c * adj_ref[0, k, pl.ds(line, 1), :]
            im = c * adj_ref[1, k, pl.ds(line, 1), :]
            stage[entry, 4 * k : 4 * k + 1, :] = re[:, :half]
            stage[entry, 4 * k + 1 : 4 * k + 2, :] = re[:, half:]
            stage[entry, 4 * k + 2 : 4 * k + 3, :] = im[:, :half]
            stage[entry, 4 * k + 3 : 4 * k + 4, :] = im[:, half:]
    small[3].wait()
    step.wait()


def deal(packed_ref, *outs):
    size = outs[0].shape[0]
    for i, out in enumerate(outs):
        out[...] = packed_ref[i * size : (i + 1) * size]


def sort_halves(cap, after_ref, *refs):
    *landed, near_ref, far_ref = refs
    for i, ref in enumerate(landed):
        near_ref[i * cap : (i + 1) * cap] = ref[:cap]
        far_ref[i * cap : (i + 1) * cap] = ref[cap:]


def cells_inside(len_ref, cells):
    row = len_ref[...].astype(F32)
    lines = row.shape[1]
    both = jnp.concatenate([row, row], axis=1)
    column = jnp.broadcast_to(both, (8, both.shape[1])).T[:lines, 0:1]
    cell = lax.axis_index("ax") * cells + lax.broadcasted_iota(jnp.int32, (lines, cells), 1)
    return cell.astype(F32) < column


def coefficients(v, iv, a_re, a_im, inside):
    s = jnp.where(inside, jnp.abs(v), 0.0)
    rd = 1.0 / (iv + 1.5 * s)
    c = s * rd
    g_re, g_im = s * a_re, s * a_im
    scale = jnp.where(inside, relaxation * rd, 0.0)
    half = v.shape[1] // 2
    lane = lax.broadcasted_iota(jnp.int32, (2 * v.shape[0], half), 1)
    low = jnp.concatenate([g_re[:, :half], g_im[:, :half]], axis=0)
    high = jnp.concatenate([g_re[:, half:], g_im[:, half:]], axis=0)
    sign = jnp.concatenate([v[:, :half], v[:, :half]], axis=0)
    edges = jnp.where(lane < 2, low, jnp.where(lane >= half - 2, high, sign)).T
    return c, scale, g_re, g_im, edges


def drives(c, g, q, inside):
    h = jnp.where(inside, q, 0.0) - 1.5 * g
    return h, g + c * h


def doubled(x):
    return jnp.concatenate([x, x], axis=0)


def orders(sign_row):
    width = sign_row.shape[1]
    pos = jnp.broadcast_to(sign_row, (SEGS, width)) > 0.0
    seg = lax.broadcasted_iota(jnp.int32, (SEGS, width), 0)
    return pos, jnp.where(pos, SEGS - 1 - seg, seg)


def before(value, reach, fill, pos, order):
    up = pltpu.roll(value, reach, 0)
    down = pltpu.roll(value, SEGS - reach, 0)
    return jnp.where(order >= reach, jnp.where(pos, down, up), fill)


def segment_scan(slots, c_t, b_t, c_s, b_s, poses):
    steps = c_s.shape[1]
    width = c_s.shape[3]
    zero = jnp.zeros((SEGS, width), F32)
    real = lax.broadcasted_iota(jnp.int32, (SEGS, width), 1) < width // 2
    first, second = jnp.where(real, 1.0, 0.0), jnp.where(real, 0.0, 1.0)
    state = [(zero, zero, first, second) for _ in slots]
    for t in range(steps):
        for i, k in enumerate(slots):
            pos = poses[i]
            y1, y2, n1, n2 = state[i]
            lo, hi = pl.ds(t, SEGS, stride=steps), pl.ds(steps - 1 - t, SEGS, stride=steps)
            cs, bs = c_t.at[k], b_t.at[k]
            c = jnp.where(pos, cs[hi, :], cs[lo, :])
            b = jnp.where(pos, bs[hi, :], bs[lo, :])
            c_s[k, t] = c
            b_s[k, t] = b
            c1, c2 = 2.0 * c, -0.5 * c
            state[i] = ((b + c2 * y2) + c1 * y1, y1, c2 * n2 + c1 * n1, n1)
    return state


def compose(state, pos, order):
    y1, y2, n1, n2 = state
    width = y1.shape[1]
    real = lax.broadcasted_iota(jnp.int32, (SEGS, width), 1) < width // 2
    o1, o2 = pltpu.roll(n1, width // 2, 1), pltpu.roll(n2, width // 2, 1)
    m11, m12 = jnp.where(real, n1, o1), jnp.where(real, o1, n1)
    m21, m22 = jnp.where(real, n2, o2), jnp.where(real, o2, n2)
    v1, v2 = y1, y2
    prev = functools.partial(before, pos=pos, order=order)
    for reach in (1, 2, 4):
        a11, a12 = prev(m11, reach, 1.0), prev(m12, reach, 0.0)
        a21, a22 = prev(m21, reach, 0.0), prev(m22, reach, 1.0)
        u1, u2 = prev(v1, reach, 0.0), prev(v2, reach, 0.0)
        m11, m12, m21, m22, v1, v2 = (
            m11 * a11 + m12 * a21,
            m11 * a12 + m12 * a22,
            m21 * a11 + m22 * a21,
            m21 * a12 + m22 * a22,
            m11 * u1 + m12 * u2 + v1,
            m21 * u1 + m22 * u2 + v2,
        )
    entry = (
        prev(v1, 1, 0.0),
        prev(v2, 1, 0.0),
        jnp.where(real, prev(m11, 1, 1.0), prev(m12, 1, 0.0)),
        jnp.where(real, prev(m21, 1, 0.0), prev(m22, 1, 1.0)),
    )
    return (jnp.where(real, m11, m12), jnp.where(real, m21, m22), v1, v2), entry


def end_rows(state, edges):
    half = edges.shape[0]
    sign_row = edges[half // 2 : half // 2 + 1]
    maps, entry = compose(state, *orders(sign_row))
    up = sign_row > 0.0
    rows = [jnp.where(up, value[0:1], value[SEGS - 1 : SEGS]) for value in maps]
    rows.append(jnp.where(up, edges[0:1], edges[half - 1 : half]))
    rows.append(jnp.where(up, edges[1:2], edges[half - 2 : half - 1]))
    return rows, entry, sign_row


def main_maps(
    adj_ref, len_ref, src_ref, speed_ref, inv_ref,
    msg_ref, sign_ref, ent_ref, c_s, b_s, h_ref, scale_ref, in_ref,
    c_t, b_t,
):
    vars_, lines, cells = speed_ref.shape
    inside = cells_inside(len_ref, cells)
    in_ref[...] = jnp.where(inside, 1.0, 0.0)
    all_edges, poses = [], []
    for k in range(vars_):
        a_re, a_im = adj_ref[0, k], adj_ref[1, k]
        c, scale, g_re, g_im, edges = coefficients(speed_ref[k], inv_ref[k], a_re, a_im, inside)
        h_re, b_re = drives(c, g_re, src_ref[0, k] + frequency * a_im, inside)
        h_im, b_im = drives(c, g_im, src_ref[1, k] - frequency * a_re, inside)
        h_ref[0, k], h_ref[1, k] = h_re, h_im
        scale_ref[k] = scale
        c_t[k] = doubled(c).T
        b_t[k] = jnp.concatenate([b_re, b_im], axis=0).T
        all_edges.append(edges)
        mid = edges.shape[0] // 2
        poses.append(orders(edges[mid : mid + 1])[0])
    states = segment_scan(range(vars_), c_t, b_t, c_s, b_s, poses)
    for k in range(vars_):
        rows, entry, sign_row = end_rows(states[k], all_edges[k])
        for i, row in enumerate(rows):
            msg_ref[vars_ * i + k : vars_ * i + k + 1, :] = row
        for i, value in enumerate(entry):
            ent_ref[k, i] = value
        sign_ref[k : k + 1, :] = sign_row


def face_maps(
    counts, lift_ref, in_ref, adj_ref, src_ref, speed_ref, inv_ref, old_msg, old_sign, *rest
):
    recv = rest[: len(counts)]
    msg_ref, sign_ref, ent_ref, c_s, b_s, h_ref, c_t, b_t = rest[len(counts) :]
    vars_, lines, cells = speed_ref.shape
    sub = lax.broadcasted_iota(jnp.int32, (FACE_DEV, 128), 0).astype(F32)
    acc = [jnp.zeros((FACE_DEV, 128), F32) for _ in range(4 * vars_)]
    for ref, number in zip(recv, counts):
        for e in range(number):
            hit = jnp.broadcast_to(ref[e, 20:21, :], (FACE_DEV, 128)) == sub
            for j in range(4 * vars_):
                row = jnp.broadcast_to(ref[e, j : j + 1, :], (FACE_DEV, 128))
                acc[j] = acc[j] + jnp.where(hit, row, 0.0)
    picks = [min(k, vars_ - 1) for k in range(lines // FACE_DEV)]

    def gather(ref):
        return jnp.concatenate([ref[k, :FACE_DEV] for k in picks], axis=0)

    def faces(j):
        return jnp.concatenate(
            [jnp.concatenate([acc[4 * k + j], acc[4 * k + j + 1]], axis=1) for k in picks], axis=0)

    a_re, a_im = gather(adj_ref.at[0]), gather(adj_ref.at[1])
    q_re = gather(src_ref.at[0]) + frequency * a_im - faces(0)
    q_im = gather(src_ref.at[1]) - frequency * a_re - faces(2)
    inside = jnp.concatenate([in_ref[:FACE_DEV]] * len(picks), axis=0) > 0.0
    c, _, g_re, g_im, edges = coefficients(
        gather(speed_ref), gather(inv_ref), a_re, a_im, inside)
    h_re, b_re = drives(c, g_re, q_re, inside)
    h_im, b_im = drives(c, g_im, q_im, inside)
    h_ref[:lines], h_ref[lines:] = h_re, h_im
    c_t[0] = doubled(c).T
    b_t[0] = jnp.concatenate([b_re, b_im], axis=0).T
    mid = edges.shape[0] // 2
    state = segment_scan([0], c_t, b_t, c_s, b_s, [orders(edges[mid : mid + 1])[0]])[0]
    msg_ref[...] = old_msg[...]
    sign_ref[...] = old_sign[...]
    rows, entry, sign_row = end_rows(state, edges)
    for i, value in enumerate(entry):
        ent_ref[0, i] = value
    sign_ref[vars_ : vars_ + 1, :] = sign_row
    width = 2 * lines
    facing = lax.rem(lax.broadcasted_iota(jnp.int32, (1, width), 1), lines) < FACE_DEV
    for i in (2, 3):
        for k in range(vars_):
            at = slice(vars_ * i + k, vars_ * i + k + 1)
            moved = pltpu.roll(rows[i], width - FACE_DEV * k, 1) if k else rows[i]
            msg_ref[at, :] = jnp.where(facing, moved, old_msg[at, :])


def unfold(k, t, steps, value, kept, turned, pos):
    if t < steps // 2:
        kept[k, t] = value
    else:
        other = kept[k, steps - 1 - t]
        turned.at[k][pl.ds(steps - 1 - t, SEGS, stride=steps), :] = jnp.where(pos, value, other)
        turned.at[k][pl.ds(t, SEGS, stride=steps), :] = jnp.where(pos, other, value)


def lifts(sign_ref, ent_ref, c_s, scale_ref, after_ref, lift_ref, x_s, x_t):
    vars_, lines, cells = scale_ref.shape
    steps, width = c_s.shape[1], c_s.shape[3]
    poses = [jnp.broadcast_to(sign_ref[k : k + 1, :], (SEGS, width)) > 0.0 for k in range(vars_)]
    state = [(ent_ref[k, 2], ent_ref[k, 3]) for k in range(vars_)]
    for t in range(steps):
        for k in range(vars_):
            n1, n2 = state[k]
            x = 2.0 * n1 - 0.5 * n2
            state[k] = (c_s[k, t] * x, n1)
            unfold(k, t, steps, x, x_s, x_t, poses[k])
    for k in range(vars_):
        x = x_t[k].T
        for part in range(2):
            lift_ref[part, k] = x[part * lines : (part + 1) * lines] * scale_ref[k]


def substitute(
    in_ref, adj_ref, sign_ref, ent_ref, c_s, b_s, h_ref, scale_ref, ent_f, c_f, b_f, h_f,
    part_ref, u_s, u_t,
):
    vars_, lines, cells = scale_ref.shape
    steps, width = c_s.shape[1], c_s.shape[3]
    groups = vars_ + 1
    inside = in_ref[...] > 0.0
    poses = [jnp.broadcast_to(sign_ref[k : k + 1, :], (SEGS, width)) > 0.0 for k in range(groups)]
    state = []
    for k in range(groups):
        ent = ent_ref.at[k] if k < vars_ else ent_f.at[0]
        state.append((ent[0], ent[1]))
    for t in range(steps):
        for k in range(groups):
            main = k < vars_
            c = c_s[k, t] if main else c_f[0, t]
            b = b_s[k, t] if main else b_f[0, t]
            y1, y2 = state[k]
            u = 2.0 * y1 - 0.5 * y2
            state[k] = (c * u + b, y1)
            unfold(k, t, steps, u, u_s, u_t, poses[k])
    face_u = u_t[vars_].T
    for k in range(vars_):
        scale = scale_ref[k]
        u = u_t[k].T
        for part in range(2):
            at = part * lines + FACE_DEV * k
            h = jnp.concatenate([h_f[at : at + FACE_DEV], h_ref[part, k, FACE_DEV:]], axis=0)
            us = jnp.concatenate(
                [face_u[at : at + FACE_DEV], u[part * lines + FACE_DEV : (part + 1) * lines]], axis=0)
            part_ref[part, k] = jnp.where(inside, adj_ref[part, k], 0.0) + (h + us) * scale


def fluxes(after_ref, in_ref, adj_ref, speed_ref, flux_ref):
    vars_, lines, cells = speed_ref.shape
    half = cells // 2
    lane = lax.broadcasted_iota(jnp.int32, (lines, half), 1)
    for k in range(vars_):
        v = speed_ref[k]
        s = jnp.abs(v) * in_ref[...]
        up = v[:, :half] > 0.0
        last = jnp.where(up, lane, 0) == half - 1
        first = jnp.where(up, 1, lane) == 0

        def shifted(low, high):
            low, high = (
                jnp.where(up, pltpu.roll(x, half - 1, 1), pltpu.roll(x, 1, 1)) for x in (low, high))
            return (jnp.where(last, high, jnp.where(first, 0.0, low)),
                    jnp.where(first, low, jnp.where(last, 0.0, high)))

        for part in range(2):
            g = s * adj_ref[part, k]
            low, high = g[:, :half], g[:, half:]
            near = shifted(low, high)
            low, high = shifted(2.0 * low - 0.5 * near[0], 2.0 * high - 0.5 * near[1])
            flux_ref[part, k, :, :half] = low * in_ref[:, :half]
            flux_ref[part, k, :, half:] = high * in_ref[:, half:]


def finish(count, sources, in_ref, sign_ref, part_ref, lift_ref, h_ref, h_f, flux_ref, *rest):
    got = rest[: count - 1]
    new_hbm, out_hbm, new_ref, out_ref, sems = rest[count - 1 :]
    _, vars_, lines, cells = part_ref.shape
    width = 2 * lines
    place = lax.axis_index("ax")
    odd = lax.rem(place, 2) == 1
    pos = sign_ref[:vars_] > 0.0
    real = lax.broadcasted_iota(jnp.int32, (vars_, width), 1) < lines
    zero = jnp.zeros((vars_, width), F32)
    z1, z2, g1, g2 = zero, zero, zero, zero
    for i in range(count - 1, 0, -1):
        near = jnp.where(place >= i, 1.0, 0.0)
        far = jnp.where(place + i <= count - 1, 1.0, 0.0)
        has = jnp.where(pos, far, near) > 0.0

        def pick(offset, at):
            value = got[0][at]
            for j in range(1, count - 1):
                here = [p for p in range(count) if p + offset == sources[j][p]]
                hit = functools.reduce(jnp.logical_or, [place == p for p in here], place < 0)
                value = jnp.where(hit, got[j][at], value)
            return value

        def field(r):
            at = slice(vars_ * r, vars_ * (r + 1))
            return jnp.where(pos, pick(i, at), pick(-i, at))

        n1, n2, b1, b2 = [field(r) for r in range(4)]
        o1, o2 = pltpu.roll(n1, lines, 1), pltpu.roll(n2, lines, 1)
        t1 = jnp.where(real, n1, o1) * z1 + jnp.where(real, o1, n1) * z2 + b1
        t2 = jnp.where(real, n2, o2) * z1 + jnp.where(real, o2, n2) * z2 + b2
        z1, z2 = jnp.where(has, t1, z1), jnp.where(has, t2, z2)
        if i == 1:
            g1, g2 = jnp.where(has, field(4), 0.0), jnp.where(has, field(5), 0.0)
    r0, r1 = 2.0 * g1 - 0.5 * g2, -0.5 * g1
    down0, down1 = jnp.where(pos, 0.0, r0), jnp.where(pos, 0.0, r1)
    up0, up1 = jnp.where(pos, r0, 0.0), jnp.where(pos, r1, 0.0)
    fill = jnp.zeros((TABLE - vars_, width), F32)
    table = jnp.concatenate([z1, fill, z2, fill, jnp.zeros((width - 2 * TABLE, width), F32)], axis=0).T
    half = cells // 2
    sub = lax.broadcasted_iota(jnp.int32, (8, width), 0)
    left = lax.broadcasted_iota(jnp.int32, (lines, half), 1) < half // 2
    copies = []
    for k in range(vars_):
        row = lambda x: jnp.broadcast_to(x[k : k + 1, :], (8, width))
        low = jnp.where(sub == 0, row(down0), jnp.where(sub == 1, row(down1), 0.0))
        high = jnp.where(sub == 7, row(up0), jnp.where(sub == 6, row(up1), 0.0))
        edges = jnp.concatenate([low, jnp.zeros((half - 16, width), F32), high], axis=0).T
        for part in range(2):
            at = part * lines + FACE_DEV * k
            rows = slice(part * lines, (part + 1) * lines)

            def entering(r):
                return table[rows, TABLE * r + k : TABLE * r + k + 1]

            edge = edges[rows]
            h = jnp.concatenate([h_f[at : at + FACE_DEV], h_ref[part, k, FACE_DEV:]], axis=0)
            h = h + flux_ref[part, k]
            out_ref[part, k, :, :half] = h[:, :half] + jnp.where(left, edge, 0.0) * in_ref[:, :half]
            out_ref[part, k, :, half:] = h[:, half:] + jnp.where(left, 0.0, edge) * in_ref[:, half:]
            new_ref[part, k] = part_ref[part, k] + (
                lift_ref[0, k] * entering(0) + lift_ref[1, k] * entering(1))
            for j, (src, dst) in enumerate(((out_ref, out_hbm), (new_ref, new_hbm))):
                copies.append(pltpu.make_async_copy(
                    src.at[part, k], dst.at[part, k], sems.at[4 * k + 2 * part + j]))
                copies[-1].start()
    for copy in copies:
        copy.wait()


def shards(adjoint, source, speed, inverse_step, coupling, face_line, face_owner, line_length):
    lines, rows, cells = adjoint.shape
    vars_ = speed.shape[1]
    faces = face_line.shape[0]
    blocks = lax.axis_size("xs")
    count = lax.axis_size("ax")
    cap = max(1, faces // blocks)
    width = 2 * lines
    steps = cells // SEGS
    adj = jnp.transpose(adjoint, (1, 0, 2)).reshape(2, vars_, lines, cells)
    src = jnp.transpose(source, (1, 0, 2)).reshape(2, vars_, lines, cells)
    spd = jnp.transpose(speed, (1, 0, 2))
    inv = jnp.transpose(inverse_step, (1, 0, 2))
    cpl = jnp.transpose(coupling, (1, 0, 2))
    vmem = pl.BlockSpec(memory_space=pltpu.VMEM)
    hbm = pl.BlockSpec(memory_space=pltpu.HBM)
    stay = lambda x: pltpu.with_memory_space_constraint(x, pltpu.HBM)
    shape = lambda *dims: jax.ShapeDtypeStruct(dims, F32)
    scratch = lambda *dims: pltpu.VMEM(dims, F32)
    dma = lambda number: pltpu.SemaphoreType.DMA((number,))
    limit = lambda mib: pltpu.CompilerParams(vmem_limit_bytes=mib << 20)
    cost = lambda flops, moved: pl.CostEstimate(
        flops=flops, bytes_accessed=moved, transcendentals=0)
    table_shape = shape(TABLE * pl.cdiv(6 * vars_, TABLE), width)
    sign_shape = shape(TABLE, width)
    order_shape = shape(vars_, steps, SEGS, width)
    field_shape = shape(2, vars_, lines, cells)
    var_shape = shape(vars_, lines, cells)
    face_order = shape(1, steps, SEGS, width)
    paired = blocks == 8
    entries = blocks * cap
    pieces = blocks // 2 if paired else 1
    adj, lengths, inv, packed = pl.pallas_call(
        functools.partial(pack_faces, blocks, cap, paired),
        out_shape=[field_shape, jax.ShapeDtypeStruct((1, lines), jnp.int32), var_shape,
                   shape(entries, PACK_ROWS, cells // 2)],
        in_specs=[hbm] * 6,
        out_specs=[vmem] * 4,
        scratch_shapes=[pltpu.SMEM((faces,), jnp.int32), pltpu.SMEM((faces,), jnp.int32),
                        scratch(vars_, faces, cells), dma(5 + vars_)],
        compiler_params=limit(6),
        name="pack_faces",
    )(stay(face_line), stay(face_owner), stay(adj), stay(cpl), stay(line_length.reshape(1, lines)),
      stay(inv))
    packed = pl.pallas_call(
        deal,
        out_shape=[shape(entries // pieces, PACK_ROWS, cells // 2)] * pieces,
        in_specs=[vmem],
        out_specs=[vmem] * pieces,
        compiler_params=limit(4),
        cost_estimate=cost(2 * 10**6, 4 * 10**7),
        name="deal",
    )(packed)
    hop = lambda x, m: lax.ppermute(x, "xs", [(i, i ^ m) for i in range(blocks)])
    if paired:
        landed = [packed[0]] + [hop(packed[m], 2 * m) for m in range(1, pieces)]
    msg, sign, ent, c_s, b_s, h, scale, mask = pl.pallas_call(
        main_maps,
        out_shape=[table_shape, sign_shape, shape(vars_, 4, SEGS, width), order_shape, order_shape,
                   field_shape, var_shape, shape(lines, cells)],
        in_specs=[vmem] * 5,
        out_specs=[vmem] * 8,
        scratch_shapes=[scratch(vars_, cells, width)] * 2,
        compiler_params=limit(14),
        cost_estimate=cost(2 * 10**6, 4 * 10**6),
        name="main_maps",
    )(adj, lengths, src, spd, inv)
    if paired:
        halves = shape(pieces * cap, PACK_ROWS, cells // 2)
        near_half, far_half = pl.pallas_call(
            functools.partial(sort_halves, cap),
            out_shape=[halves] * 2,
            in_specs=[vmem] * (1 + pieces),
            out_specs=[vmem] * 2,
            compiler_params=limit(4),
            name="sort_halves",
        )(sign, *landed)
        recv, counts, after = [near_half, hop(far_half, 1)], [pieces * cap] * 2, near_half
    else:
        recv, counts, after = [lax.all_to_all(packed[0], "xs", 0, 0, tiled=True)], [entries], packed[0]
    kept = lambda number: scratch(number, steps // 2, SEGS, width)
    lift = pl.pallas_call(
        lifts,
        out_shape=field_shape,
        in_specs=[vmem] * 5,
        out_specs=vmem,
        scratch_shapes=[kept(vars_), scratch(vars_, cells, width)],
        compiler_params=limit(8),
        cost_estimate=cost(10**6, 2 * 10**6),
        name="lifts",
    )(sign, ent, c_s, scale, after)
    msg, sign, ent_f, c_f, b_f, h_f = pl.pallas_call(
        functools.partial(face_maps, counts),
        out_shape=[table_shape, sign_shape, shape(1, 4, SEGS, width), face_order, face_order,
                   shape(width, cells)],
        in_specs=[vmem] * (8 + len(recv)),
        out_specs=[vmem] * 6,
        scratch_shapes=[scratch(1, cells, width)] * 2,
        compiler_params=limit(10),
        name="face_maps",
    )(lift, mask, adj, src, spd, inv, msg, sign, *recv)
    if count == 4:
        routes = [(1, 0, 3, 2), (3, 2, 0, 1), (2, 3, 1, 0)]
    else:
        routes = [[(i + k) % count for i in range(count)] for k in range(1, count)]
    sources = [[r.index(p) for p in range(count)] for r in routes]
    got = [lax.ppermute(msg, "ax", list(enumerate(r))) for r in routes]
    part = pl.pallas_call(
        substitute,
        out_shape=field_shape,
        in_specs=[vmem] * 12,
        out_specs=vmem,
        scratch_shapes=[kept(vars_ + 1), scratch(vars_ + 1, cells, width)],
        compiler_params=limit(14),
        cost_estimate=cost(2 * 10**6, 3 * 10**6),
        name="substitute",
    )(mask, adj, sign, ent, c_s, b_s, h, scale, ent_f, c_f, b_f, h_f)
    flux = pl.pallas_call(
        fluxes,
        out_shape=field_shape,
        in_specs=[vmem] * 4,
        out_specs=vmem,
        compiler_params=limit(6),
        cost_estimate=cost(10**6, 2 * 10**6),
        name="fluxes",
    )(part, mask, adj, spd)
    new, out = pl.pallas_call(
        functools.partial(finish, count, sources),
        out_shape=[field_shape] * 2,
        in_specs=[vmem] * (7 + len(got)),
        out_specs=[hbm] * 2,
        scratch_shapes=[scratch(2, vars_, lines, cells)] * 2 + [dma(4 * vars_)],
        compiler_params=limit(10),
        name="finish",
    )(mask, sign, part, lift, h, h_f, flux, *got)
    back = lambda x: jnp.transpose(x.reshape(rows, lines, cells), (1, 0, 2))
    return (back(new), back(out))


def solution(mesh):
    line = P("xs", None, "ax")
    in_specs = (line,) * 5 + (P("xs"),) * 3
    return jax.shard_map(
        shards, mesh=mesh, in_specs=in_specs, out_specs=(line, line), check_vma=False
    )
```

```python
import functools
import jax
import jax.numpy as jnp
from jax import lax
from jax.experimental import pallas as pl
from jax.experimental.pallas import tpu as pltpu
from jax.sharding import PartitionSpec as P

FACE_DEV = 8

frequency = 0.7
relaxation = 0.02

SEGS = 8
PACK_ROWS = 24
TABLE = 8
F32 = jnp.float32


def pack_faces(blocks, cap, paired, line_hbm, owner_hbm, adj_hbm, coup_hbm, len_hbm, inv_hbm, *rest):
    adj_ref, len_ref, inv_ref, stage = rest[:4]
    line_ref, owner_ref, coup_ref, sems = rest[4:]
    vars_, faces, cells = coup_ref.shape
    half = cells // 2
    slots = FACE_DEV * blocks
    small = [
        pltpu.make_async_copy(owner_hbm, owner_ref, sems.at[0]),
        pltpu.make_async_copy(line_hbm, line_ref, sems.at[1]),
        pltpu.make_async_copy(coup_hbm, coup_ref, sems.at[2]),
        pltpu.make_async_copy(len_hbm, len_ref, sems.at[3]),
    ]
    large = [
        pltpu.make_async_copy(adj_hbm.at[:, k], adj_ref.at[:, k], sems.at[4 + k])
        for k in range(vars_)
    ]
    step = pltpu.make_async_copy(inv_hbm, inv_ref, sems.at[4 + vars_])
    for copy in small + large + [step]:
        copy.start()
    for copy in small[:2]:
        copy.wait()
    if blocks * cap != faces:
        for e in range(blocks * cap):
            stage[e, 16:24, :] = jnp.full((8, 128), -1.0, F32)
    dests, places = [], []
    for f in range(faces):
        slot = lax.rem(owner_ref[f], slots)
        dest = lax.div(slot, FACE_DEV)
        spot = jnp.int32(0)
        for other in dests:
            spot = spot + (other == dest).astype(jnp.int32)
        dests.append(dest)
        if paired:
            dest = lax.bitwise_xor(dest, lax.axis_index("xs"))
        entry = dest * cap + jnp.minimum(spot, cap - 1)
        places.append((entry, line_ref[f]))
        number = lax.rem(slot, FACE_DEV).astype(F32)
        stage[entry, 20:24, :] = jnp.full((4, 128), number, F32)
    small[2].wait()
    for k in range(vars_):
        large[k].wait()
        for f, (entry, line) in enumerate(places):
            c = coup_ref[k, f : f + 1, :]
            re = c * adj_ref[0, k, pl.ds(line, 1), :]
            im = c * adj_ref[1, k, pl.ds(line, 1), :]
            stage[entry, 4 * k : 4 * k + 1, :] = re[:, :half]
            stage[entry, 4 * k + 1 : 4 * k + 2, :] = re[:, half:]
            stage[entry, 4 * k + 2 : 4 * k + 3, :] = im[:, :half]
            stage[entry, 4 * k + 3 : 4 * k + 4, :] = im[:, half:]
    small[3].wait()
    step.wait()


def deal(packed_ref, *outs):
    size = outs[0].shape[0]
    for i, out in enumerate(outs):
        out[...] = packed_ref[i * size : (i + 1) * size]


def sort_halves(cap, after_ref, *refs):
    *landed, near_ref, far_ref = refs
    for i, ref in enumerate(landed):
        near_ref[i * cap : (i + 1) * cap] = ref[:cap]
        far_ref[i * cap : (i + 1) * cap] = ref[cap:]


def cells_inside(len_ref, cells):
    row = len_ref[...].astype(F32)
    lines = row.shape[1]
    both = jnp.concatenate([row, row], axis=1)
    column = jnp.broadcast_to(both, (8, both.shape[1])).T[:lines, 0:1]
    cell = lax.axis_index("ax") * cells + lax.broadcasted_iota(jnp.int32, (lines, cells), 1)
    return cell.astype(F32) < column


def coefficients(v, iv, a_re, a_im, inside):
    s = jnp.where(inside, jnp.abs(v), 0.0)
    rd = 1.0 / (iv + 1.5 * s)
    c = s * rd
    g_re, g_im = s * a_re, s * a_im
    scale = jnp.where(inside, relaxation * rd, 0.0)
    half = v.shape[1] // 2
    lane = lax.broadcasted_iota(jnp.int32, (2 * v.shape[0], half), 1)
    low = jnp.concatenate([g_re[:, :half], g_im[:, :half]], axis=0)
    high = jnp.concatenate([g_re[:, half:], g_im[:, half:]], axis=0)
    sign = jnp.concatenate([v[:, :half], v[:, :half]], axis=0)
    edges = jnp.where(lane < 2, low, jnp.where(lane >= half - 2, high, sign)).T
    return c, scale, g_re, g_im, edges


def drives(c, g, q, inside):
    h = jnp.where(inside, q, 0.0) - 1.5 * g
    return h, g + c * h


def doubled(x):
    return jnp.concatenate([x, x], axis=0)


def orders(sign_row):
    width = sign_row.shape[1]
    pos = jnp.broadcast_to(sign_row, (SEGS, width)) > 0.0
    seg = lax.broadcasted_iota(jnp.int32, (SEGS, width), 0)
    return pos, jnp.where(pos, SEGS - 1 - seg, seg)


def before(value, reach, fill, pos, order):
    up = pltpu.roll(value, reach, 0)
    down = pltpu.roll(value, SEGS - reach, 0)
    return jnp.where(order >= reach, jnp.where(pos, down, up), fill)


def segment_scan(slots, c_t, b_t, c_s, b_s, poses):
    steps = c_s.shape[1]
    width = c_s.shape[3]
    zero = jnp.zeros((SEGS, width), F32)
    real = lax.broadcasted_iota(jnp.int32, (SEGS, width), 1) < width // 2
    first, second = jnp.where(real, 1.0, 0.0), jnp.where(real, 0.0, 1.0)
    state = [(zero, zero, first, second) for _ in slots]
    for t in range(steps):
        for i, k in enumerate(slots):
            pos = poses[i]
            y1, y2, n1, n2 = state[i]
            lo, hi = pl.ds(t, SEGS, stride=steps), pl.ds(steps - 1 - t, SEGS, stride=steps)
            cs, bs = c_t.at[k], b_t.at[k]
            c = jnp.where(pos, cs[hi, :], cs[lo, :])
            b = jnp.where(pos, bs[hi, :], bs[lo, :])
            c_s[k, t] = c
            b_s[k, t] = b
            c1, c2 = 2.0 * c, -0.5 * c
            state[i] = ((b + c2 * y2) + c1 * y1, y1, c2 * n2 + c1 * n1, n1)
    return state


def compose(state, pos, order):
    y1, y2, n1, n2 = state
    width = y1.shape[1]
    real = lax.broadcasted_iota(jnp.int32, (SEGS, width), 1) < width // 2
    o1, o2 = pltpu.roll(n1, width // 2, 1), pltpu.roll(n2, width // 2, 1)
    m11, m12 = jnp.where(real, n1, o1), jnp.where(real, o1, n1)
    m21, m22 = jnp.where(real, n2, o2), jnp.where(real, o2, n2)
    v1, v2 = y1, y2
    prev = functools.partial(before, pos=pos, order=order)
    for reach in (1, 2, 4):
        a11, a12 = prev(m11, reach, 1.0), prev(m12, reach, 0.0)
        a21, a22 = prev(m21, reach, 0.0), prev(m22, reach, 1.0)
        u1, u2 = prev(v1, reach, 0.0), prev(v2, reach, 0.0)
        m11, m12, m21, m22, v1, v2 = (
            m11 * a11 + m12 * a21,
            m11 * a12 + m12 * a22,
            m21 * a11 + m22 * a21,
            m21 * a12 + m22 * a22,
            m11 * u1 + m12 * u2 + v1,
            m21 * u1 + m22 * u2 + v2,
        )
    entry = (
        prev(v1, 1, 0.0),
        prev(v2, 1, 0.0),
        jnp.where(real, prev(m11, 1, 1.0), prev(m12, 1, 0.0)),
        jnp.where(real, prev(m21, 1, 0.0), prev(m22, 1, 1.0)),
    )
    return (jnp.where(real, m11, m12), jnp.where(real, m21, m22), v1, v2), entry


def end_rows(state, edges):
    half = edges.shape[0]
    sign_row = edges[half // 2 : half // 2 + 1]
    maps, entry = compose(state, *orders(sign_row))
    up = sign_row > 0.0
    rows = [jnp.where(up, value[0:1], value[SEGS - 1 : SEGS]) for value in maps]
    rows.append(jnp.where(up, edges[0:1], edges[half - 1 : half]))
    rows.append(jnp.where(up, edges[1:2], edges[half - 2 : half - 1]))
    return rows, entry, sign_row


def main_maps(
    adj_ref, len_ref, src_ref, speed_ref, inv_ref,
    msg_ref, sign_ref, ent_ref, c_s, b_s, h_ref, scale_ref, in_ref,
    c_t, b_t,
):
    vars_, lines, cells = speed_ref.shape
    inside = cells_inside(len_ref, cells)
    in_ref[...] = jnp.where(inside, 1.0, 0.0)
    all_edges, poses = [], []
    for k in range(vars_):
        a_re, a_im = adj_ref[0, k], adj_ref[1, k]
        c, scale, g_re, g_im, edges = coefficients(speed_ref[k], inv_ref[k], a_re, a_im, inside)
        h_re, b_re = drives(c, g_re, src_ref[0, k] + frequency * a_im, inside)
        h_im, b_im = drives(c, g_im, src_ref[1, k] - frequency * a_re, inside)
        h_ref[0, k], h_ref[1, k] = h_re, h_im
        scale_ref[k] = scale
        c_t[k] = doubled(c).T
        b_t[k] = jnp.concatenate([b_re, b_im], axis=0).T
        all_edges.append(edges)
        mid = edges.shape[0] // 2
        poses.append(orders(edges[mid : mid + 1])[0])
    states = segment_scan(range(vars_), c_t, b_t, c_s, b_s, poses)
    for k in range(vars_):
        rows, entry, sign_row = end_rows(states[k], all_edges[k])
        for i, row in enumerate(rows):
            msg_ref[vars_ * i + k : vars_ * i + k + 1, :] = row
        for i, value in enumerate(entry):
            ent_ref[k, i] = value
        sign_ref[k : k + 1, :] = sign_row


def face_maps(
    counts, lift_ref, in_ref, adj_ref, src_ref, speed_ref, inv_ref, old_msg, old_sign, *rest
):
    recv = rest[: len(counts)]
    msg_ref, sign_ref, ent_ref, c_s, b_s, h_ref, c_t, b_t = rest[len(counts) :]
    vars_, lines, cells = speed_ref.shape
    sub = lax.broadcasted_iota(jnp.int32, (FACE_DEV, 128), 0).astype(F32)
    acc = [jnp.zeros((FACE_DEV, 128), F32) for _ in range(4 * vars_)]
    for ref, number in zip(recv, counts):
        for e in range(number):
            hit = jnp.broadcast_to(ref[e, 20:21, :], (FACE_DEV, 128)) == sub
            for j in range(4 * vars_):
                row = jnp.broadcast_to(ref[e, j : j + 1, :], (FACE_DEV, 128))
                acc[j] = acc[j] + jnp.where(hit, row, 0.0)
    picks = [min(k, vars_ - 1) for k in range(lines // FACE_DEV)]

    def gather(ref):
        return jnp.concatenate([ref[k, :FACE_DEV] for k in picks], axis=0)

    def faces(j):
        return jnp.concatenate(
            [jnp.concatenate([acc[4 * k + j], acc[4 * k + j + 1]], axis=1) for k in picks], axis=0)

    a_re, a_im = gather(adj_ref.at[0]), gather(adj_ref.at[1])
    q_re = gather(src_ref.at[0]) + frequency * a_im - faces(0)
    q_im = gather(src_ref.at[1]) - frequency * a_re - faces(2)
    inside = jnp.concatenate([in_ref[:FACE_DEV]] * len(picks), axis=0) > 0.0
    c, _, g_re, g_im, edges = coefficients(
        gather(speed_ref), gather(inv_ref), a_re, a_im, inside)
    h_re, b_re = drives(c, g_re, q_re, inside)
    h_im, b_im = drives(c, g_im, q_im, inside)
    h_ref[:lines], h_ref[lines:] = h_re, h_im
    c_t[0] = doubled(c).T
    b_t[0] = jnp.concatenate([b_re, b_im], axis=0).T
    mid = edges.shape[0] // 2
    state = segment_scan([0], c_t, b_t, c_s, b_s, [orders(edges[mid : mid + 1])[0]])[0]
    msg_ref[...] = old_msg[...]
    sign_ref[...] = old_sign[...]
    rows, entry, sign_row = end_rows(state, edges)
    for i, value in enumerate(entry):
        ent_ref[0, i] = value
    sign_ref[vars_ : vars_ + 1, :] = sign_row
    width = 2 * lines
    facing = lax.rem(lax.broadcasted_iota(jnp.int32, (1, width), 1), lines) < FACE_DEV
    for i in (2, 3):
        for k in range(vars_):
            at = slice(vars_ * i + k, vars_ * i + k + 1)
            moved = pltpu.roll(rows[i], width - FACE_DEV * k, 1) if k else rows[i]
            msg_ref[at, :] = jnp.where(facing, moved, old_msg[at, :])


def unfold(k, t, steps, value, kept, turned, pos):
    if t < steps // 2:
        kept[k, t] = value
    else:
        other = kept[k, steps - 1 - t]
        turned.at[k][pl.ds(steps - 1 - t, SEGS, stride=steps), :] = jnp.where(pos, value, other)
        turned.at[k][pl.ds(t, SEGS, stride=steps), :] = jnp.where(pos, other, value)


def lifts(sign_ref, ent_ref, c_s, scale_ref, after_ref, lift_ref, x_s, x_t):
    vars_, lines, cells = scale_ref.shape
    steps, width = c_s.shape[1], c_s.shape[3]
    poses = [jnp.broadcast_to(sign_ref[k : k + 1, :], (SEGS, width)) > 0.0 for k in range(vars_)]
    state = [(ent_ref[k, 2], ent_ref[k, 3]) for k in range(vars_)]
    for t in range(steps):
        for k in range(vars_):
            n1, n2 = state[k]
            x = 2.0 * n1 - 0.5 * n2
            state[k] = (c_s[k, t] * x, n1)
            unfold(k, t, steps, x, x_s, x_t, poses[k])
    for k in range(vars_):
        x = x_t[k].T
        for part in range(2):
            lift_ref[part, k] = x[part * lines : (part + 1) * lines] * scale_ref[k]


def substitute(
    in_ref, adj_ref, sign_ref, ent_ref, c_s, b_s, h_ref, scale_ref, ent_f, c_f, b_f, h_f,
    part_ref, u_s, u_t,
):
    vars_, lines, cells = scale_ref.shape
    steps, width = c_s.shape[1], c_s.shape[3]
    groups = vars_ + 1
    inside = in_ref[...] > 0.0
    poses = [jnp.broadcast_to(sign_ref[k : k + 1, :], (SEGS, width)) > 0.0 for k in range(groups)]
    state = []
    for k in range(groups):
        ent = ent_ref.at[k] if k < vars_ else ent_f.at[0]
        state.append((ent[0], ent[1]))
    for t in range(steps):
        for k in range(groups):
            main = k < vars_
            c = c_s[k, t] if main else c_f[0, t]
            b = b_s[k, t] if main else b_f[0, t]
            y1, y2 = state[k]
            u = 2.0 * y1 - 0.5 * y2
            state[k] = (c * u + b, y1)
            unfold(k, t, steps, u, u_s, u_t, poses[k])
    face_u = u_t[vars_].T
    for k in range(vars_):
        scale = scale_ref[k]
        u = u_t[k].T
        for part in range(2):
            at = part * lines + FACE_DEV * k
            h = jnp.concatenate([h_f[at : at + FACE_DEV], h_ref[part, k, FACE_DEV:]], axis=0)
            us = jnp.concatenate(
                [face_u[at : at + FACE_DEV], u[part * lines + FACE_DEV : (part + 1) * lines]], axis=0)
            part_ref[part, k] = jnp.where(inside, adj_ref[part, k], 0.0) + (h + us) * scale


def fluxes(after_ref, in_ref, adj_ref, speed_ref, flux_ref):
    vars_, lines, cells = speed_ref.shape
    half = cells // 2
    lane = lax.broadcasted_iota(jnp.int32, (lines, half), 1)
    for k in range(vars_):
        v = speed_ref[k]
        s = jnp.abs(v) * in_ref[...]
        up = v[:, :half] > 0.0
        last = jnp.where(up, lane, 0) == half - 1
        first = jnp.where(up, 1, lane) == 0

        def shifted(low, high):
            low, high = (
                jnp.where(up, pltpu.roll(x, half - 1, 1), pltpu.roll(x, 1, 1)) for x in (low, high))
            return (jnp.where(last, high, jnp.where(first, 0.0, low)),
                    jnp.where(first, low, jnp.where(last, 0.0, high)))

        for part in range(2):
            g = s * adj_ref[part, k]
            low, high = g[:, :half], g[:, half:]
            near = shifted(low, high)
            low, high = shifted(2.0 * low - 0.5 * near[0], 2.0 * high - 0.5 * near[1])
            flux_ref[part, k, :, :half] = low * in_ref[:, :half]
            flux_ref[part, k, :, half:] = high * in_ref[:, half:]


def finish(count, sources, in_ref, sign_ref, part_ref, lift_ref, h_ref, h_f, flux_ref, *rest):
    got = rest[: count - 1]
    new_hbm, out_hbm, new_ref, out_ref, sems = rest[count - 1 :]
    _, vars_, lines, cells = part_ref.shape
    width = 2 * lines
    place = lax.axis_index("ax")
    odd = lax.rem(place, 2) == 1
    pos = sign_ref[:vars_] > 0.0
    real = lax.broadcasted_iota(jnp.int32, (vars_, width), 1) < lines
    zero = jnp.zeros((vars_, width), F32)
    z1, z2, g1, g2 = zero, zero, zero, zero
    for i in range(count - 1, 0, -1):
        near = jnp.where(place >= i, 1.0, 0.0)
        far = jnp.where(place + i <= count - 1, 1.0, 0.0)
        has = jnp.where(pos, far, near) > 0.0

        def pick(offset, at):
            value = got[0][at]
            for j in range(1, count - 1):
                here = [p for p in range(count) if p + offset == sources[j][p]]
                hit = functools.reduce(jnp.logical_or, [place == p for p in here], place < 0)
                value = jnp.where(hit, got[j][at], value)
            return value

        def field(r):
            at = slice(vars_ * r, vars_ * (r + 1))
            return jnp.where(pos, pick(i, at), pick(-i, at))

        n1, n2, b1, b2 = [field(r) for r in range(4)]
        o1, o2 = pltpu.roll(n1, lines, 1), pltpu.roll(n2, lines, 1)
        t1 = jnp.where(real, n1, o1) * z1 + jnp.where(real, o1, n1) * z2 + b1
        t2 = jnp.where(real, n2, o2) * z1 + jnp.where(real, o2, n2) * z2 + b2
        z1, z2 = jnp.where(has, t1, z1), jnp.where(has, t2, z2)
        if i == 1:
            g1, g2 = jnp.where(has, field(4), 0.0), jnp.where(has, field(5), 0.0)
    r0, r1 = 2.0 * g1 - 0.5 * g2, -0.5 * g1
    down0, down1 = jnp.where(pos, 0.0, r0), jnp.where(pos, 0.0, r1)
    up0, up1 = jnp.where(pos, r0, 0.0), jnp.where(pos, r1, 0.0)
    fill = jnp.zeros((TABLE - vars_, width), F32)
    table = jnp.concatenate([z1, fill, z2, fill, jnp.zeros((width - 2 * TABLE, width), F32)], axis=0).T
    half = cells // 2
    sub = lax.broadcasted_iota(jnp.int32, (8, width), 0)
    left = lax.broadcasted_iota(jnp.int32, (lines, half), 1) < half // 2
    copies = []
    for k in range(vars_):
        row = lambda x: jnp.broadcast_to(x[k : k + 1, :], (8, width))
        low = jnp.where(sub == 0, row(down0), jnp.where(sub == 1, row(down1), 0.0))
        high = jnp.where(sub == 7, row(up0), jnp.where(sub == 6, row(up1), 0.0))
        edges = jnp.concatenate([low, jnp.zeros((half - 16, width), F32), high], axis=0).T
        for part in range(2):
            at = part * lines + FACE_DEV * k
            rows = slice(part * lines, (part + 1) * lines)

            def entering(r):
                return table[rows, TABLE * r + k : TABLE * r + k + 1]

            edge = edges[rows]
            h = jnp.concatenate([h_f[at : at + FACE_DEV], h_ref[part, k, FACE_DEV:]], axis=0)
            h = h + flux_ref[part, k]
            out_ref[part, k, :, :half] = h[:, :half] + jnp.where(left, edge, 0.0) * in_ref[:, :half]
            out_ref[part, k, :, half:] = h[:, half:] + jnp.where(left, 0.0, edge) * in_ref[:, half:]
            new_ref[part, k] = part_ref[part, k] + (
                lift_ref[0, k] * entering(0) + lift_ref[1, k] * entering(1))
            for j, (src, dst) in enumerate(((out_ref, out_hbm), (new_ref, new_hbm))):
                copies.append(pltpu.make_async_copy(
                    src.at[part, k], dst.at[part, k], sems.at[4 * k + 2 * part + j]))
                copies[-1].start()
    for copy in copies:
        copy.wait()


def shards(adjoint, source, speed, inverse_step, coupling, face_line, face_owner, line_length):
    lines, rows, cells = adjoint.shape
    vars_ = speed.shape[1]
    faces = face_line.shape[0]
    blocks = lax.axis_size("xs")
    count = lax.axis_size("ax")
    cap = max(1, faces // blocks)
    width = 2 * lines
    steps = cells // SEGS
    adj = jnp.transpose(adjoint, (1, 0, 2)).reshape(2, vars_, lines, cells)
    src = jnp.transpose(source, (1, 0, 2)).reshape(2, vars_, lines, cells)
    spd = jnp.transpose(speed, (1, 0, 2))
    inv = jnp.transpose(inverse_step, (1, 0, 2))
    cpl = jnp.transpose(coupling, (1, 0, 2))
    vmem = pl.BlockSpec(memory_space=pltpu.VMEM)
    hbm = pl.BlockSpec(memory_space=pltpu.HBM)
    stay = lambda x: pltpu.with_memory_space_constraint(x, pltpu.HBM)
    shape = lambda *dims: jax.ShapeDtypeStruct(dims, F32)
    scratch = lambda *dims: pltpu.VMEM(dims, F32)
    dma = lambda number: pltpu.SemaphoreType.DMA((number,))
    limit = lambda mib: pltpu.CompilerParams(vmem_limit_bytes=mib << 20)
    cost = lambda flops, moved: pl.CostEstimate(
        flops=flops, bytes_accessed=moved, transcendentals=0)
    table_shape = shape(TABLE * pl.cdiv(6 * vars_, TABLE), width)
    sign_shape = shape(TABLE, width)
    order_shape = shape(vars_, steps, SEGS, width)
    field_shape = shape(2, vars_, lines, cells)
    var_shape = shape(vars_, lines, cells)
    face_order = shape(1, steps, SEGS, width)
    paired = blocks == 8
    entries = blocks * cap
    pieces = blocks // 2 if paired else 1
    adj, lengths, inv, packed = pl.pallas_call(
        functools.partial(pack_faces, blocks, cap, paired),
        out_shape=[field_shape, jax.ShapeDtypeStruct((1, lines), jnp.int32), var_shape,
                   shape(entries, PACK_ROWS, cells // 2)],
        in_specs=[hbm] * 6,
        out_specs=[vmem] * 4,
        scratch_shapes=[pltpu.SMEM((faces,), jnp.int32), pltpu.SMEM((faces,), jnp.int32),
                        scratch(vars_, faces, cells), dma(5 + vars_)],
        compiler_params=limit(6),
        name="pack_faces",
    )(stay(face_line), stay(face_owner), stay(adj), stay(cpl), stay(line_length.reshape(1, lines)),
      stay(inv))
    packed = pl.pallas_call(
        deal,
        out_shape=[shape(entries // pieces, PACK_ROWS, cells // 2)] * pieces,
        in_specs=[vmem],
        out_specs=[vmem] * pieces,
        compiler_params=limit(4),
        cost_estimate=cost(2 * 10**6, 4 * 10**7),
        name="deal",
    )(packed)
    hop = lambda x, m: lax.ppermute(x, "xs", [(i, i ^ m) for i in range(blocks)])
    if paired:
        landed = [packed[0]] + [hop(packed[m], 2 * m) for m in (1, 3, 2)]
    msg, sign, ent, c_s, b_s, h, scale, mask = pl.pallas_call(
        main_maps,
        out_shape=[table_shape, sign_shape, shape(vars_, 4, SEGS, width), order_shape, order_shape,
                   field_shape, var_shape, shape(lines, cells)],
        in_specs=[vmem] * 5,
        out_specs=[vmem] * 8,
        scratch_shapes=[scratch(vars_, cells, width)] * 2,
        compiler_params=limit(14),
        cost_estimate=cost(2 * 10**6, 4 * 10**6),
        name="main_maps",
    )(adj, lengths, src, spd, inv)
    if paired:
        halves = shape(pieces * cap, PACK_ROWS, cells // 2)
        near_half, far_half = pl.pallas_call(
            functools.partial(sort_halves, cap),
            out_shape=[halves] * 2,
            in_specs=[vmem] * (1 + pieces),
            out_specs=[vmem] * 2,
            compiler_params=limit(4),
            name="sort_halves",
        )(sign, *landed)
        recv, counts, after = [near_half, hop(far_half, 1)], [pieces * cap] * 2, near_half
    else:
        recv, counts, after = [lax.all_to_all(packed[0], "xs", 0, 0, tiled=True)], [entries], packed[0]
    kept = lambda number: scratch(number, steps // 2, SEGS, width)
    lift = pl.pallas_call(
        lifts,
        out_shape=field_shape,
        in_specs=[vmem] * 5,
        out_specs=vmem,
        scratch_shapes=[kept(vars_), scratch(vars_, cells, width)],
        compiler_params=limit(8),
        cost_estimate=cost(10**6, 2 * 10**6),
        name="lifts",
    )(sign, ent, c_s, scale, after)
    msg, sign, ent_f, c_f, b_f, h_f = pl.pallas_call(
        functools.partial(face_maps, counts),
        out_shape=[table_shape, sign_shape, shape(1, 4, SEGS, width), face_order, face_order,
                   shape(width, cells)],
        in_specs=[vmem] * (8 + len(recv)),
        out_specs=[vmem] * 6,
        scratch_shapes=[scratch(1, cells, width)] * 2,
        compiler_params=limit(10),
        name="face_maps",
    )(lift, mask, adj, src, spd, inv, msg, sign, *recv)
    if count == 4:
        routes = [(1, 0, 3, 2), (3, 2, 0, 1), (2, 3, 1, 0)]
    else:
        routes = [[(i + k) % count for i in range(count)] for k in range(1, count)]
    sources = [[r.index(p) for p in range(count)] for r in routes]
    got = [lax.ppermute(msg, "ax", list(enumerate(r))) for r in routes]
    part = pl.pallas_call(
        substitute,
        out_shape=field_shape,
        in_specs=[vmem] * 12,
        out_specs=vmem,
        scratch_shapes=[kept(vars_ + 1), scratch(vars_ + 1, cells, width)],
        compiler_params=limit(14),
        cost_estimate=cost(2 * 10**6, 3 * 10**6),
        name="substitute",
    )(mask, adj, sign, ent, c_s, b_s, h, scale, ent_f, c_f, b_f, h_f)
    flux = pl.pallas_call(
        fluxes,
        out_shape=field_shape,
        in_specs=[vmem] * 4,
        out_specs=vmem,
        compiler_params=limit(6),
        cost_estimate=cost(10**6, 2 * 10**6),
        name="fluxes",
    )(part, mask, adj, spd)
    new, out = pl.pallas_call(
        functools.partial(finish, count, sources),
        out_shape=[field_shape] * 2,
        in_specs=[vmem] * (7 + len(got)),
        out_specs=[hbm] * 2,
        scratch_shapes=[scratch(2, vars_, lines, cells)] * 2 + [dma(4 * vars_)],
        compiler_params=limit(10),
        name="finish",
    )(mask, sign, part, lift, h, h_f, flux, *got)
    back = lambda x: jnp.transpose(x.reshape(rows, lines, cells), (1, 0, 2))
    return (back(new), back(out))


def solution(mesh):
    line = P("xs", None, "ax")
    in_specs = (line,) * 5 + (P("xs"),) * 3
    return jax.shard_map(
        shards, mesh=mesh, in_specs=in_specs, out_specs=(line, line), check_vma=False
    )
```

```python
import functools
import jax
import jax.numpy as jnp
from jax import lax
from jax.experimental import pallas as pl
from jax.experimental.pallas import tpu as pltpu
from jax.sharding import PartitionSpec as P

FACE_DEV = 8

frequency = 0.7
relaxation = 0.02

SEGS = 8
PACK_ROWS = 24
TABLE = 8
F32 = jnp.float32


def pack_faces(blocks, cap, paired, line_hbm, owner_hbm, adj_hbm, coup_hbm, len_hbm, inv_hbm, *rest):
    adj_ref, len_ref, inv_ref, stage = rest[:4]
    line_ref, owner_ref, coup_ref, sems = rest[4:]
    vars_, faces, cells = coup_ref.shape
    half = cells // 2
    slots = FACE_DEV * blocks
    small = [
        pltpu.make_async_copy(owner_hbm, owner_ref, sems.at[0]),
        pltpu.make_async_copy(line_hbm, line_ref, sems.at[1]),
        pltpu.make_async_copy(coup_hbm, coup_ref, sems.at[2]),
        pltpu.make_async_copy(len_hbm, len_ref, sems.at[3]),
    ]
    large = [
        pltpu.make_async_copy(adj_hbm.at[:, k], adj_ref.at[:, k], sems.at[4 + k])
        for k in range(vars_)
    ]
    step = pltpu.make_async_copy(inv_hbm, inv_ref, sems.at[4 + vars_])
    for copy in small + large + [step]:
        copy.start()
    for copy in small[:2]:
        copy.wait()
    if blocks * cap != faces:
        for e in range(blocks * cap):
            stage[e, 16:24, :] = jnp.full((8, 128), -1.0, F32)
    dests, places = [], []
    for f in range(faces):
        slot = lax.rem(owner_ref[f], slots)
        dest = lax.div(slot, FACE_DEV)
        spot = jnp.int32(0)
        for other in dests:
            spot = spot + (other == dest).astype(jnp.int32)
        dests.append(dest)
        if paired:
            dest = lax.bitwise_xor(dest, lax.axis_index("xs"))
        entry = dest * cap + jnp.minimum(spot, cap - 1)
        places.append((entry, line_ref[f]))
        number = lax.rem(slot, FACE_DEV).astype(F32)
        stage[entry, 20:24, :] = jnp.full((4, 128), number, F32)
    small[2].wait()
    for k in range(vars_):
        large[k].wait()
        for f, (entry, line) in enumerate(places):
            c = coup_ref[k, f : f + 1, :]
            re = c * adj_ref[0, k, pl.ds(line, 1), :]
            im = c * adj_ref[1, k, pl.ds(line, 1), :]
            stage[entry, 4 * k : 4 * k + 1, :] = re[:, :half]
            stage[entry, 4 * k + 1 : 4 * k + 2, :] = re[:, half:]
            stage[entry, 4 * k + 2 : 4 * k + 3, :] = im[:, :half]
            stage[entry, 4 * k + 3 : 4 * k + 4, :] = im[:, half:]
    small[3].wait()
    step.wait()


def deal(packed_ref, *outs):
    size = outs[0].shape[0]
    for i, out in enumerate(outs):
        out[...] = packed_ref[i * size : (i + 1) * size]


def sort_halves(cap, after_ref, *refs):
    *landed, near_ref, far_ref = refs
    for i, ref in enumerate(landed):
        near_ref[i * cap : (i + 1) * cap] = ref[:cap]
        far_ref[i * cap : (i + 1) * cap] = ref[cap:]


def cells_inside(len_ref, cells):
    row = len_ref[...].astype(F32)
    lines = row.shape[1]
    both = jnp.concatenate([row, row], axis=1)
    column = jnp.broadcast_to(both, (8, both.shape[1])).T[:lines, 0:1]
    cell = lax.axis_index("ax") * cells + lax.broadcasted_iota(jnp.int32, (lines, cells), 1)
    return cell.astype(F32) < column


def coefficients(v, iv, a_re, a_im, inside):
    s = jnp.where(inside, jnp.abs(v), 0.0)
    rd = 1.0 / jnp.where(inside, iv + 1.5 * s, 1.0)
    c = s * rd
    g_re, g_im = s * a_re, s * a_im
    scale = jnp.where(inside, relaxation * rd, 0.0)
    half = v.shape[1] // 2
    lane = lax.broadcasted_iota(jnp.int32, (2 * v.shape[0], half), 1)
    low = jnp.concatenate([g_re[:, :half], g_im[:, :half]], axis=0)
    high = jnp.concatenate([g_re[:, half:], g_im[:, half:]], axis=0)
    sign = jnp.concatenate([v[:, :half], v[:, :half]], axis=0)
    edges = jnp.where(lane < 2, low, jnp.where(lane >= half - 2, high, sign)).T
    return c, scale, g_re, g_im, edges


def drives(c, g, q, inside):
    h = jnp.where(inside, q, 0.0) - 1.5 * g
    return h, g + c * h


def doubled(x):
    return jnp.concatenate([x, x], axis=0)


def orders(sign_row):
    width = sign_row.shape[1]
    pos = jnp.broadcast_to(sign_row, (SEGS, width)) > 0.0
    seg = lax.broadcasted_iota(jnp.int32, (SEGS, width), 0)
    return pos, jnp.where(pos, SEGS - 1 - seg, seg)


def before(value, reach, fill, pos, order):
    up = pltpu.roll(value, reach, 0)
    down = pltpu.roll(value, SEGS - reach, 0)
    return jnp.where(order >= reach, jnp.where(pos, down, up), fill)


def segment_scan(slots, c_t, b_t, c_s, b_s, poses):
    steps = c_s.shape[1]
    width = c_s.shape[3]
    zero = jnp.zeros((SEGS, width), F32)
    real = lax.broadcasted_iota(jnp.int32, (SEGS, width), 1) < width // 2
    first, second = jnp.where(real, 1.0, 0.0), jnp.where(real, 0.0, 1.0)
    state = [(zero, zero, first, second) for _ in slots]
    for t in range(steps):
        for i, k in enumerate(slots):
            pos = poses[i]
            y1, y2, n1, n2 = state[i]
            lo, hi = pl.ds(t, SEGS, stride=steps), pl.ds(steps - 1 - t, SEGS, stride=steps)
            cs, bs = c_t.at[k], b_t.at[k]
            c = jnp.where(pos, cs[hi, :], cs[lo, :])
            b = jnp.where(pos, bs[hi, :], bs[lo, :])
            c_s[k, t] = c
            b_s[k, t] = b
            c1, c2 = 2.0 * c, -0.5 * c
            state[i] = ((b + c2 * y2) + c1 * y1, y1, c2 * n2 + c1 * n1, n1)
    return state


def compose(state, pos, order):
    y1, y2, n1, n2 = state
    width = y1.shape[1]
    real = lax.broadcasted_iota(jnp.int32, (SEGS, width), 1) < width // 2
    o1, o2 = pltpu.roll(n1, width // 2, 1), pltpu.roll(n2, width // 2, 1)
    m11, m12 = jnp.where(real, n1, o1), jnp.where(real, o1, n1)
    m21, m22 = jnp.where(real, n2, o2), jnp.where(real, o2, n2)
    v1, v2 = y1, y2
    prev = functools.partial(before, pos=pos, order=order)
    for reach in (1, 2, 4):
        a11, a12 = prev(m11, reach, 1.0), prev(m12, reach, 0.0)
        a21, a22 = prev(m21, reach, 0.0), prev(m22, reach, 1.0)
        u1, u2 = prev(v1, reach, 0.0), prev(v2, reach, 0.0)
        m11, m12, m21, m22, v1, v2 = (
            m11 * a11 + m12 * a21,
            m11 * a12 + m12 * a22,
            m21 * a11 + m22 * a21,
            m21 * a12 + m22 * a22,
            m11 * u1 + m12 * u2 + v1,
            m21 * u1 + m22 * u2 + v2,
        )
    entry = (
        prev(v1, 1, 0.0),
        prev(v2, 1, 0.0),
        jnp.where(real, prev(m11, 1, 1.0), prev(m12, 1, 0.0)),
        jnp.where(real, prev(m21, 1, 0.0), prev(m22, 1, 1.0)),
    )
    return (jnp.where(real, m11, m12), jnp.where(real, m21, m22), v1, v2), entry


def end_rows(state, edges):
    half = edges.shape[0]
    sign_row = edges[half // 2 : half // 2 + 1]
    maps, entry = compose(state, *orders(sign_row))
    up = sign_row > 0.0
    rows = [jnp.where(up, value[0:1], value[SEGS - 1 : SEGS]) for value in maps]
    rows.append(jnp.where(up, edges[0:1], edges[half - 1 : half]))
    rows.append(jnp.where(up, edges[1:2], edges[half - 2 : half - 1]))
    return rows, entry, sign_row


def main_maps(
    adj_ref, len_ref, src_ref, speed_ref, inv_ref,
    msg_ref, sign_ref, ent_ref, c_s, b_s, h_ref, scale_ref, in_ref,
    c_t, b_t,
):
    vars_, lines, cells = speed_ref.shape
    inside = cells_inside(len_ref, cells)
    in_ref[...] = jnp.where(inside, 1.0, 0.0)
    all_edges, poses = [], []
    for k in range(vars_):
        a_re, a_im = adj_ref[0, k], adj_ref[1, k]
        c, scale, g_re, g_im, edges = coefficients(speed_ref[k], inv_ref[k], a_re, a_im, inside)
        h_re, b_re = drives(c, g_re, src_ref[0, k] + frequency * a_im, inside)
        h_im, b_im = drives(c, g_im, src_ref[1, k] - frequency * a_re, inside)
        h_ref[0, k], h_ref[1, k] = h_re, h_im
        scale_ref[k] = scale
        c_t[k] = doubled(c).T
        b_t[k] = jnp.concatenate([b_re, b_im], axis=0).T
        all_edges.append(edges)
        mid = edges.shape[0] // 2
        poses.append(orders(edges[mid : mid + 1])[0])
    states = segment_scan(range(vars_), c_t, b_t, c_s, b_s, poses)
    for k in range(vars_):
        rows, entry, sign_row = end_rows(states[k], all_edges[k])
        for i, row in enumerate(rows):
            msg_ref[vars_ * i + k : vars_ * i + k + 1, :] = row
        for i, value in enumerate(entry):
            ent_ref[k, i] = value
        sign_ref[k : k + 1, :] = sign_row


def face_maps(
    counts, lift_ref, in_ref, adj_ref, src_ref, speed_ref, inv_ref, old_msg, old_sign, *rest
):
    recv = rest[: len(counts)]
    msg_ref, sign_ref, ent_ref, c_s, b_s, h_ref, c_t, b_t = rest[len(counts) :]
    vars_, lines, cells = speed_ref.shape
    sub = lax.broadcasted_iota(jnp.int32, (FACE_DEV, 128), 0).astype(F32)
    acc = [jnp.zeros((FACE_DEV, 128), F32) for _ in range(4 * vars_)]
    for ref, number in zip(recv, counts):
        for e in range(number):
            hit = jnp.broadcast_to(ref[e, 20:21, :], (FACE_DEV, 128)) == sub
            for j in range(4 * vars_):
                row = jnp.broadcast_to(ref[e, j : j + 1, :], (FACE_DEV, 128))
                acc[j] = acc[j] + jnp.where(hit, row, 0.0)
    picks = [min(k, vars_ - 1) for k in range(lines // FACE_DEV)]

    def gather(ref):
        return jnp.concatenate([ref[k, :FACE_DEV] for k in picks], axis=0)

    def faces(j):
        return jnp.concatenate(
            [jnp.concatenate([acc[4 * k + j], acc[4 * k + j + 1]], axis=1) for k in picks], axis=0)

    a_re, a_im = gather(adj_ref.at[0]), gather(adj_ref.at[1])
    q_re = gather(src_ref.at[0]) + frequency * a_im - faces(0)
    q_im = gather(src_ref.at[1]) - frequency * a_re - faces(2)
    inside = jnp.concatenate([in_ref[:FACE_DEV]] * len(picks), axis=0) > 0.0
    c, _, g_re, g_im, edges = coefficients(
        gather(speed_ref), gather(inv_ref), a_re, a_im, inside)
    h_re, b_re = drives(c, g_re, q_re, inside)
    h_im, b_im = drives(c, g_im, q_im, inside)
    h_ref[:lines], h_ref[lines:] = h_re, h_im
    c_t[0] = doubled(c).T
    b_t[0] = jnp.concatenate([b_re, b_im], axis=0).T
    mid = edges.shape[0] // 2
    state = segment_scan([0], c_t, b_t, c_s, b_s, [orders(edges[mid : mid + 1])[0]])[0]
    msg_ref[...] = old_msg[...]
    sign_ref[...] = old_sign[...]
    rows, entry, sign_row = end_rows(state, edges)
    for i, value in enumerate(entry):
        ent_ref[0, i] = value
    sign_ref[vars_ : vars_ + 1, :] = sign_row
    width = 2 * lines
    facing = lax.rem(lax.broadcasted_iota(jnp.int32, (1, width), 1), lines) < FACE_DEV
    for i in (2, 3):
        for k in range(vars_):
            at = slice(vars_ * i + k, vars_ * i + k + 1)
            moved = pltpu.roll(rows[i], width - FACE_DEV * k, 1) if k else rows[i]
            msg_ref[at, :] = jnp.where(facing, moved, old_msg[at, :])


def unfold(k, t, steps, value, kept, turned, pos):
    if t < steps // 2:
        kept[k, t] = value
    else:
        other = kept[k, steps - 1 - t]
        turned.at[k][pl.ds(steps - 1 - t, SEGS, stride=steps), :] = jnp.where(pos, value, other)
        turned.at[k][pl.ds(t, SEGS, stride=steps), :] = jnp.where(pos, other, value)


def lifts(sign_ref, ent_ref, c_s, scale_ref, after_ref, lift_ref, x_s, x_t):
    vars_, lines, cells = scale_ref.shape
    steps, width = c_s.shape[1], c_s.shape[3]
    poses = [jnp.broadcast_to(sign_ref[k : k + 1, :], (SEGS, width)) > 0.0 for k in range(vars_)]
    state = [(ent_ref[k, 2], ent_ref[k, 3]) for k in range(vars_)]
    for t in range(steps):
        for k in range(vars_):
            n1, n2 = state[k]
            x = 2.0 * n1 - 0.5 * n2
            state[k] = (c_s[k, t] * x, n1)
            unfold(k, t, steps, x, x_s, x_t, poses[k])
    for k in range(vars_):
        x = x_t[k].T
        for part in range(2):
            lift_ref[part, k] = x[part * lines : (part + 1) * lines] * scale_ref[k]


def substitute(
    in_ref, adj_ref, sign_ref, ent_ref, c_s, b_s, h_ref, scale_ref, ent_f, c_f, b_f, h_f,
    part_ref, u_s, u_t,
):
    vars_, lines, cells = scale_ref.shape
    steps, width = c_s.shape[1], c_s.shape[3]
    groups = vars_ + 1
    inside = in_ref[...] > 0.0
    poses = [jnp.broadcast_to(sign_ref[k : k + 1, :], (SEGS, width)) > 0.0 for k in range(groups)]
    state = []
    for k in range(groups):
        ent = ent_ref.at[k] if k < vars_ else ent_f.at[0]
        state.append((ent[0], ent[1]))
    for t in range(steps):
        for k in range(groups):
            main = k < vars_
            c = c_s[k, t] if main else c_f[0, t]
            b = b_s[k, t] if main else b_f[0, t]
            y1, y2 = state[k]
            u = 2.0 * y1 - 0.5 * y2
            state[k] = (c * u + b, y1)
            unfold(k, t, steps, u, u_s, u_t, poses[k])
    face_u = u_t[vars_].T
    for k in range(vars_):
        scale = scale_ref[k]
        u = u_t[k].T
        for part in range(2):
            at = part * lines + FACE_DEV * k
            h = jnp.concatenate([h_f[at : at + FACE_DEV], h_ref[part, k, FACE_DEV:]], axis=0)
            us = jnp.concatenate(
                [face_u[at : at + FACE_DEV], u[part * lines + FACE_DEV : (part + 1) * lines]], axis=0)
            part_ref[part, k] = jnp.where(inside, adj_ref[part, k], 0.0) + (h + us) * scale


def fluxes(after_ref, in_ref, adj_ref, speed_ref, flux_ref):
    vars_, lines, cells = speed_ref.shape
    half = cells // 2
    lane = lax.broadcasted_iota(jnp.int32, (lines, half), 1)
    for k in range(vars_):
        v = speed_ref[k]
        s = jnp.abs(v) * in_ref[...]
        up = v[:, :half] > 0.0
        last = jnp.where(up, lane, 0) == half - 1
        first = jnp.where(up, 1, lane) == 0

        def shifted(low, high):
            low, high = (
                jnp.where(up, pltpu.roll(x, half - 1, 1), pltpu.roll(x, 1, 1)) for x in (low, high))
            return (jnp.where(last, high, jnp.where(first, 0.0, low)),
                    jnp.where(first, low, jnp.where(last, 0.0, high)))

        for part in range(2):
            g = s * adj_ref[part, k]
            low, high = g[:, :half], g[:, half:]
            near = shifted(low, high)
            low, high = shifted(2.0 * low - 0.5 * near[0], 2.0 * high - 0.5 * near[1])
            flux_ref[part, k, :, :half] = low * in_ref[:, :half]
            flux_ref[part, k, :, half:] = high * in_ref[:, half:]


def finish(count, sources, in_ref, sign_ref, part_ref, lift_ref, h_ref, h_f, flux_ref, *rest):
    got = rest[: count - 1]
    new_hbm, out_hbm, new_ref, out_ref, sems = rest[count - 1 :]
    _, vars_, lines, cells = part_ref.shape
    width = 2 * lines
    place = lax.axis_index("ax")
    odd = lax.rem(place, 2) == 1
    pos = sign_ref[:vars_] > 0.0
    real = lax.broadcasted_iota(jnp.int32, (vars_, width), 1) < lines
    zero = jnp.zeros((vars_, width), F32)
    z1, z2, g1, g2 = zero, zero, zero, zero
    for i in range(count - 1, 0, -1):
        near = jnp.where(place >= i, 1.0, 0.0)
        far = jnp.where(place + i <= count - 1, 1.0, 0.0)
        has = jnp.where(pos, far, near) > 0.0

        def pick(offset, at):
            value = got[0][at]
            for j in range(1, count - 1):
                here = [p for p in range(count) if p + offset == sources[j][p]]
                hit = functools.reduce(jnp.logical_or, [place == p for p in here], place < 0)
                value = jnp.where(hit, got[j][at], value)
            return value

        def field(r):
            at = slice(vars_ * r, vars_ * (r + 1))
            return jnp.where(pos, pick(i, at), pick(-i, at))

        n1, n2, b1, b2 = [field(r) for r in range(4)]
        o1, o2 = pltpu.roll(n1, lines, 1), pltpu.roll(n2, lines, 1)
        t1 = jnp.where(real, n1, o1) * z1 + jnp.where(real, o1, n1) * z2 + b1
        t2 = jnp.where(real, n2, o2) * z1 + jnp.where(real, o2, n2) * z2 + b2
        z1, z2 = jnp.where(has, t1, z1), jnp.where(has, t2, z2)
        if i == 1:
            g1, g2 = jnp.where(has, field(4), 0.0), jnp.where(has, field(5), 0.0)
    r0, r1 = 2.0 * g1 - 0.5 * g2, -0.5 * g1
    down0, down1 = jnp.where(pos, 0.0, r0), jnp.where(pos, 0.0, r1)
    up0, up1 = jnp.where(pos, r0, 0.0), jnp.where(pos, r1, 0.0)
    fill = jnp.zeros((TABLE - vars_, width), F32)
    table = jnp.concatenate([z1, fill, z2, fill, jnp.zeros((width - 2 * TABLE, width), F32)], axis=0).T
    half = cells // 2
    sub = lax.broadcasted_iota(jnp.int32, (8, width), 0)
    left = lax.broadcasted_iota(jnp.int32, (lines, half), 1) < half // 2
    copies = []
    for k in range(vars_):
        row = lambda x: jnp.broadcast_to(x[k : k + 1, :], (8, width))
        low = jnp.where(sub == 0, row(down0), jnp.where(sub == 1, row(down1), 0.0))
        high = jnp.where(sub == 7, row(up0), jnp.where(sub == 6, row(up1), 0.0))
        edges = jnp.concatenate([low, jnp.zeros((half - 16, width), F32), high], axis=0).T
        for part in range(2):
            at = part * lines + FACE_DEV * k
            rows = slice(part * lines, (part + 1) * lines)

            def entering(r):
                return table[rows, TABLE * r + k : TABLE * r + k + 1]

            edge = edges[rows]
            h = jnp.concatenate([h_f[at : at + FACE_DEV], h_ref[part, k, FACE_DEV:]], axis=0)
            h = h + flux_ref[part, k]
            out_ref[part, k, :, :half] = h[:, :half] + jnp.where(left, edge, 0.0) * in_ref[:, :half]
            out_ref[part, k, :, half:] = h[:, half:] + jnp.where(left, 0.0, edge) * in_ref[:, half:]
            new_ref[part, k] = part_ref[part, k] + (
                lift_ref[0, k] * entering(0) + lift_ref[1, k] * entering(1))
            for j, (src, dst) in enumerate(((out_ref, out_hbm), (new_ref, new_hbm))):
                copies.append(pltpu.make_async_copy(
                    src.at[part, k], dst.at[part, k], sems.at[4 * k + 2 * part + j]))
                copies[-1].start()
    for copy in copies:
        copy.wait()


def shards(adjoint, source, speed, inverse_step, coupling, face_line, face_owner, line_length):
    lines, rows, cells = adjoint.shape
    vars_ = speed.shape[1]
    faces = face_line.shape[0]
    blocks = lax.axis_size("xs")
    count = lax.axis_size("ax")
    cap = max(1, faces // blocks)
    width = 2 * lines
    steps = cells // SEGS
    adj = jnp.transpose(adjoint, (1, 0, 2)).reshape(2, vars_, lines, cells)
    src = jnp.transpose(source, (1, 0, 2)).reshape(2, vars_, lines, cells)
    spd = jnp.transpose(speed, (1, 0, 2))
    inv = jnp.transpose(inverse_step, (1, 0, 2))
    cpl = jnp.transpose(coupling, (1, 0, 2))
    vmem = pl.BlockSpec(memory_space=pltpu.VMEM)
    hbm = pl.BlockSpec(memory_space=pltpu.HBM)
    stay = lambda x: pltpu.with_memory_space_constraint(x, pltpu.HBM)
    shape = lambda *dims: jax.ShapeDtypeStruct(dims, F32)
    scratch = lambda *dims: pltpu.VMEM(dims, F32)
    dma = lambda number: pltpu.SemaphoreType.DMA((number,))
    limit = lambda mib: pltpu.CompilerParams(vmem_limit_bytes=mib << 20)
    cost = lambda flops, moved: pl.CostEstimate(
        flops=flops, bytes_accessed=moved, transcendentals=0)
    table_shape = shape(TABLE * pl.cdiv(6 * vars_, TABLE), width)
    sign_shape = shape(TABLE, width)
    order_shape = shape(vars_, steps, SEGS, width)
    field_shape = shape(2, vars_, lines, cells)
    var_shape = shape(vars_, lines, cells)
    face_order = shape(1, steps, SEGS, width)
    paired = blocks == 8
    entries = blocks * cap
    pieces = blocks // 2 if paired else 1
    adj, lengths, inv, packed = pl.pallas_call(
        functools.partial(pack_faces, blocks, cap, paired),
        out_shape=[field_shape, jax.ShapeDtypeStruct((1, lines), jnp.int32), var_shape,
                   shape(entries, PACK_ROWS, cells // 2)],
        in_specs=[hbm] * 6,
        out_specs=[vmem] * 4,
        scratch_shapes=[pltpu.SMEM((faces,), jnp.int32), pltpu.SMEM((faces,), jnp.int32),
                        scratch(vars_, faces, cells), dma(5 + vars_)],
        compiler_params=limit(6),
        name="pack_faces",
    )(stay(face_line), stay(face_owner), stay(adj), stay(cpl), stay(line_length.reshape(1, lines)),
      stay(inv))
    packed = pl.pallas_call(
        deal,
        out_shape=[shape(entries // pieces, PACK_ROWS, cells // 2)] * pieces,
        in_specs=[vmem],
        out_specs=[vmem] * pieces,
        compiler_params=limit(4),
        cost_estimate=cost(2 * 10**6, 4 * 10**7),
        name="deal",
    )(packed)
    hop = lambda x, m: lax.ppermute(x, "xs", [(i, i ^ m) for i in range(blocks)])
    if paired:
        landed = [packed[0]] + [hop(packed[m], 2 * m) for m in (1, 3, 2)]
    msg, sign, ent, c_s, b_s, h, scale, mask = pl.pallas_call(
        main_maps,
        out_shape=[table_shape, sign_shape, shape(vars_, 4, SEGS, width), order_shape, order_shape,
                   field_shape, var_shape, shape(lines, cells)],
        in_specs=[vmem] * 5,
        out_specs=[vmem] * 8,
        scratch_shapes=[scratch(vars_, cells, width)] * 2,
        compiler_params=limit(14),
        cost_estimate=cost(2 * 10**6, 4 * 10**6),
        name="main_maps",
    )(adj, lengths, src, spd, inv)
    if paired:
        halves = shape(pieces * cap, PACK_ROWS, cells // 2)
        near_half, far_half = pl.pallas_call(
            functools.partial(sort_halves, cap),
            out_shape=[halves] * 2,
            in_specs=[vmem] * (1 + pieces),
            out_specs=[vmem] * 2,
            compiler_params=limit(4),
            name="sort_halves",
        )(sign, *landed)
        recv, counts, after = [near_half, hop(far_half, 1)], [pieces * cap] * 2, near_half
    else:
        recv, counts, after = [lax.all_to_all(packed[0], "xs", 0, 0, tiled=True)], [entries], packed[0]
    kept = lambda number: scratch(number, steps // 2, SEGS, width)
    lift = pl.pallas_call(
        lifts,
        out_shape=field_shape,
        in_specs=[vmem] * 5,
        out_specs=vmem,
        scratch_shapes=[kept(vars_), scratch(vars_, cells, width)],
        compiler_params=limit(8),
        cost_estimate=cost(10**6, 2 * 10**6),
        name="lifts",
    )(sign, ent, c_s, scale, after)
    msg, sign, ent_f, c_f, b_f, h_f = pl.pallas_call(
        functools.partial(face_maps, counts),
        out_shape=[table_shape, sign_shape, shape(1, 4, SEGS, width), face_order, face_order,
                   shape(width, cells)],
        in_specs=[vmem] * (8 + len(recv)),
        out_specs=[vmem] * 6,
        scratch_shapes=[scratch(1, cells, width)] * 2,
        compiler_params=limit(10),
        name="face_maps",
    )(lift, mask, adj, src, spd, inv, msg, sign, *recv)
    if count == 4:
        routes = [(1, 0, 3, 2), (3, 2, 0, 1), (2, 3, 1, 0)]
    else:
        routes = [[(i + k) % count for i in range(count)] for k in range(1, count)]
    sources = [[r.index(p) for p in range(count)] for r in routes]
    got = [lax.ppermute(msg, "ax", list(enumerate(r))) for r in routes]
    part = pl.pallas_call(
        substitute,
        out_shape=field_shape,
        in_specs=[vmem] * 12,
        out_specs=vmem,
        scratch_shapes=[kept(vars_ + 1), scratch(vars_ + 1, cells, width)],
        compiler_params=limit(14),
        cost_estimate=cost(2 * 10**6, 3 * 10**6),
        name="substitute",
    )(mask, adj, sign, ent, c_s, b_s, h, scale, ent_f, c_f, b_f, h_f)
    flux = pl.pallas_call(
        fluxes,
        out_shape=field_shape,
        in_specs=[vmem] * 4,
        out_specs=vmem,
        compiler_params=limit(6),
        cost_estimate=cost(10**6, 2 * 10**6),
        name="fluxes",
    )(part, mask, adj, spd)
    new, out = pl.pallas_call(
        functools.partial(finish, count, sources),
        out_shape=[field_shape] * 2,
        in_specs=[vmem] * (7 + len(got)),
        out_specs=[hbm] * 2,
        scratch_shapes=[scratch(2, vars_, lines, cells)] * 2 + [dma(4 * vars_)],
        compiler_params=limit(10),
        name="finish",
    )(mask, sign, part, lift, h, h_f, flux, *got)
    back = lambda x: jnp.transpose(x.reshape(rows, lines, cells), (1, 0, 2))
    return (back(new), back(out))


def solution(mesh):
    line = P("xs", None, "ax")
    in_specs = (line,) * 5 + (P("xs"),) * 3
    return jax.shard_map(
        shards, mesh=mesh, in_specs=in_specs, out_specs=(line, line), check_vma=False
    )
```

```python
import functools
import jax
import jax.numpy as jnp
from jax import lax
from jax.experimental import pallas as pl
from jax.experimental.pallas import tpu as pltpu
from jax.sharding import PartitionSpec as P

FACE_DEV = 8

frequency = 0.7
relaxation = 0.02

SEGS = 8
PACK_ROWS = 24
TABLE = 8
F32 = jnp.float32


def pack_faces(blocks, cap, paired, line_hbm, owner_hbm, adj_hbm, coup_hbm, len_hbm, inv_hbm, *rest):
    adj_ref, len_ref, inv_ref, stage = rest[:4]
    line_ref, owner_ref, coup_ref, sems = rest[4:]
    vars_, faces, cells = coup_ref.shape
    half = cells // 2
    slots = FACE_DEV * blocks
    small = [
        pltpu.make_async_copy(owner_hbm, owner_ref, sems.at[0]),
        pltpu.make_async_copy(line_hbm, line_ref, sems.at[1]),
        pltpu.make_async_copy(coup_hbm, coup_ref, sems.at[2]),
        pltpu.make_async_copy(len_hbm, len_ref, sems.at[3]),
    ]
    large = [
        pltpu.make_async_copy(adj_hbm.at[:, k], adj_ref.at[:, k], sems.at[4 + k])
        for k in range(vars_)
    ]
    step = pltpu.make_async_copy(inv_hbm, inv_ref, sems.at[4 + vars_])
    for copy in small + large + [step]:
        copy.start()
    for copy in small[:2]:
        copy.wait()
    if blocks * cap != faces:
        for e in range(blocks * cap):
            stage[e, 16:24, :] = jnp.full((8, 128), -1.0, F32)
    dests, places = [], []
    for f in range(faces):
        slot = lax.rem(owner_ref[f], slots)
        dest = lax.div(slot, FACE_DEV)
        spot = jnp.int32(0)
        for other in dests:
            spot = spot + (other == dest).astype(jnp.int32)
        dests.append(dest)
        if paired:
            dest = lax.bitwise_xor(dest, lax.axis_index("xs"))
        entry = dest * cap + jnp.minimum(spot, cap - 1)
        places.append((entry, line_ref[f]))
        number = lax.rem(slot, FACE_DEV).astype(F32)
        stage[entry, 20:24, :] = jnp.full((4, 128), number, F32)
    small[2].wait()
    for k in range(vars_):
        large[k].wait()
        for f, (entry, line) in enumerate(places):
            c = coup_ref[k, f : f + 1, :]
            re = c * adj_ref[0, k, pl.ds(line, 1), :]
            im = c * adj_ref[1, k, pl.ds(line, 1), :]
            stage[entry, 4 * k : 4 * k + 1, :] = re[:, :half]
            stage[entry, 4 * k + 1 : 4 * k + 2, :] = re[:, half:]
            stage[entry, 4 * k + 2 : 4 * k + 3, :] = im[:, :half]
            stage[entry, 4 * k + 3 : 4 * k + 4, :] = im[:, half:]
    small[3].wait()
    step.wait()


def deal(packed_ref, *outs):
    size = outs[0].shape[0]
    for i, out in enumerate(outs):
        out[...] = packed_ref[i * size : (i + 1) * size]


def sort_halves(cap, after_ref, *refs):
    *landed, near_ref, far_ref = refs
    for i, ref in enumerate(landed):
        near_ref[i * cap : (i + 1) * cap] = ref[:cap]
        far_ref[i * cap : (i + 1) * cap] = ref[cap:]


def cells_inside(len_ref, cells):
    row = len_ref[...].astype(F32)
    lines = row.shape[1]
    both = jnp.concatenate([row, row], axis=1)
    column = jnp.broadcast_to(both, (8, both.shape[1])).T[:lines, 0:1]
    cell = lax.axis_index("ax") * cells + lax.broadcasted_iota(jnp.int32, (lines, cells), 1)
    return cell.astype(F32) < column


def coefficients(v, iv, a_re, a_im, inside):
    s = jnp.where(inside, jnp.abs(v), 0.0)
    rd = 1.0 / jnp.where(inside, iv + 1.5 * s, 1.0)
    c = s * rd
    g_re, g_im = s * a_re, s * a_im
    scale = jnp.where(inside, relaxation * rd, 0.0)
    half = v.shape[1] // 2
    lane = lax.broadcasted_iota(jnp.int32, (2 * v.shape[0], half), 1)
    low = jnp.concatenate([g_re[:, :half], g_im[:, :half]], axis=0)
    high = jnp.concatenate([g_re[:, half:], g_im[:, half:]], axis=0)
    sign = jnp.concatenate([v[:, :half], v[:, :half]], axis=0)
    edges = jnp.where(lane < 2, low, jnp.where(lane >= half - 2, high, sign)).T
    return c, scale, g_re, g_im, edges


def drives(c, g, q, inside):
    h = jnp.where(inside, q, 0.0) - 1.5 * g
    return h, g + c * h


def doubled(x):
    return jnp.concatenate([x, x], axis=0)


def orders(sign_row):
    width = sign_row.shape[1]
    pos = jnp.broadcast_to(sign_row, (SEGS, width)) > 0.0
    seg = lax.broadcasted_iota(jnp.int32, (SEGS, width), 0)
    return pos, jnp.where(pos, SEGS - 1 - seg, seg)


def before(value, reach, fill, pos, order):
    up = pltpu.roll(value, reach, 0)
    down = pltpu.roll(value, SEGS - reach, 0)
    return jnp.where(order >= reach, jnp.where(pos, down, up), fill)


def segment_scan(slots, c_t, b_t, c_s, b_s, poses):
    steps = c_s.shape[1]
    width = c_s.shape[3]
    zero = jnp.zeros((SEGS, width), F32)
    real = lax.broadcasted_iota(jnp.int32, (SEGS, width), 1) < width // 2
    first, second = jnp.where(real, 1.0, 0.0), jnp.where(real, 0.0, 1.0)
    state = [(zero, zero, first, second) for _ in slots]
    for t in range(steps):
        for i, k in enumerate(slots):
            pos = poses[i]
            y1, y2, n1, n2 = state[i]
            lo, hi = pl.ds(t, SEGS, stride=steps), pl.ds(steps - 1 - t, SEGS, stride=steps)
            cs, bs = c_t.at[k], b_t.at[k]
            c = jnp.where(pos, cs[hi, :], cs[lo, :])
            b = jnp.where(pos, bs[hi, :], bs[lo, :])
            c_s[k, t] = c
            b_s[k, t] = b
            c1, c2 = 2.0 * c, -0.5 * c
            state[i] = ((b + c2 * y2) + c1 * y1, y1, c2 * n2 + c1 * n1, n1)
    return state


def compose(state, pos, order):
    y1, y2, n1, n2 = state
    width = y1.shape[1]
    real = lax.broadcasted_iota(jnp.int32, (SEGS, width), 1) < width // 2
    o1, o2 = pltpu.roll(n1, width // 2, 1), pltpu.roll(n2, width // 2, 1)
    m11, m12 = jnp.where(real, n1, o1), jnp.where(real, o1, n1)
    m21, m22 = jnp.where(real, n2, o2), jnp.where(real, o2, n2)
    v1, v2 = y1, y2
    prev = functools.partial(before, pos=pos, order=order)
    for reach in (1, 2, 4):
        a11, a12 = prev(m11, reach, 1.0), prev(m12, reach, 0.0)
        a21, a22 = prev(m21, reach, 0.0), prev(m22, reach, 1.0)
        u1, u2 = prev(v1, reach, 0.0), prev(v2, reach, 0.0)
        m11, m12, m21, m22, v1, v2 = (
            m11 * a11 + m12 * a21,
            m11 * a12 + m12 * a22,
            m21 * a11 + m22 * a21,
            m21 * a12 + m22 * a22,
            m11 * u1 + m12 * u2 + v1,
            m21 * u1 + m22 * u2 + v2,
        )
    entry = (
        prev(v1, 1, 0.0),
        prev(v2, 1, 0.0),
        jnp.where(real, prev(m11, 1, 1.0), prev(m12, 1, 0.0)),
        jnp.where(real, prev(m21, 1, 0.0), prev(m22, 1, 1.0)),
    )
    return (jnp.where(real, m11, m12), jnp.where(real, m21, m22), v1, v2), entry


def end_rows(state, edges):
    half = edges.shape[0]
    sign_row = edges[half // 2 : half // 2 + 1]
    maps, entry = compose(state, *orders(sign_row))
    up = sign_row > 0.0
    rows = [jnp.where(up, value[0:1], value[SEGS - 1 : SEGS]) for value in maps]
    rows.append(jnp.where(up, edges[0:1], edges[half - 1 : half]))
    rows.append(jnp.where(up, edges[1:2], edges[half - 2 : half - 1]))
    return rows, entry, sign_row


def main_maps(
    adj_ref, len_ref, src_ref, speed_ref, inv_ref,
    msg_ref, sign_ref, ent_ref, c_s, b_s, h_ref, scale_ref, in_ref,
    c_t, b_t,
):
    vars_, lines, cells = speed_ref.shape
    inside = cells_inside(len_ref, cells)
    in_ref[...] = jnp.where(inside, 1.0, 0.0)
    all_edges, poses = [], []
    for k in range(vars_):
        a_re, a_im = adj_ref[0, k], adj_ref[1, k]
        c, scale, g_re, g_im, edges = coefficients(speed_ref[k], inv_ref[k], a_re, a_im, inside)
        h_re, b_re = drives(c, g_re, src_ref[0, k] + frequency * a_im, inside)
        h_im, b_im = drives(c, g_im, src_ref[1, k] - frequency * a_re, inside)
        h_ref[0, k], h_ref[1, k] = h_re, h_im
        scale_ref[k] = scale
        c_t[k] = doubled(c).T
        b_t[k] = jnp.concatenate([b_re, b_im], axis=0).T
        all_edges.append(edges)
        mid = edges.shape[0] // 2
        poses.append(orders(edges[mid : mid + 1])[0])
    states = segment_scan(range(vars_), c_t, b_t, c_s, b_s, poses)
    for k in range(vars_):
        rows, entry, sign_row = end_rows(states[k], all_edges[k])
        for i, row in enumerate(rows):
            msg_ref[vars_ * i + k : vars_ * i + k + 1, :] = row
        for i, value in enumerate(entry):
            ent_ref[k, i] = value
        sign_ref[k : k + 1, :] = sign_row


def face_maps(
    counts, after_ref, in_ref, adj_ref, src_ref, speed_ref, inv_ref, old_msg, old_sign, *rest
):
    recv = rest[: len(counts)]
    msg_ref, sign_ref, ent_ref, c_s, b_s, h_ref, c_t, b_t = rest[len(counts) :]
    vars_, lines, cells = speed_ref.shape
    sub = lax.broadcasted_iota(jnp.int32, (FACE_DEV, 128), 0).astype(F32)
    acc = [jnp.zeros((FACE_DEV, 128), F32) for _ in range(4 * vars_)]
    for ref, number in zip(recv, counts):
        for e in range(number):
            hit = jnp.broadcast_to(ref[e, 20:21, :], (FACE_DEV, 128)) == sub
            for j in range(4 * vars_):
                row = jnp.broadcast_to(ref[e, j : j + 1, :], (FACE_DEV, 128))
                acc[j] = acc[j] + jnp.where(hit, row, 0.0)
    picks = [min(k, vars_ - 1) for k in range(lines // FACE_DEV)]

    def gather(ref):
        return jnp.concatenate([ref[k, :FACE_DEV] for k in picks], axis=0)

    def faces(j):
        return jnp.concatenate(
            [jnp.concatenate([acc[4 * k + j], acc[4 * k + j + 1]], axis=1) for k in picks], axis=0)

    a_re, a_im = gather(adj_ref.at[0]), gather(adj_ref.at[1])
    q_re = gather(src_ref.at[0]) + frequency * a_im - faces(0)
    q_im = gather(src_ref.at[1]) - frequency * a_re - faces(2)
    inside = jnp.concatenate([in_ref[:FACE_DEV]] * len(picks), axis=0) > 0.0
    c, _, g_re, g_im, edges = coefficients(
        gather(speed_ref), gather(inv_ref), a_re, a_im, inside)
    h_re, b_re = drives(c, g_re, q_re, inside)
    h_im, b_im = drives(c, g_im, q_im, inside)
    h_ref[:lines], h_ref[lines:] = h_re, h_im
    c_t[0] = doubled(c).T
    b_t[0] = jnp.concatenate([b_re, b_im], axis=0).T
    mid = edges.shape[0] // 2
    state = segment_scan([0], c_t, b_t, c_s, b_s, [orders(edges[mid : mid + 1])[0]])[0]
    msg_ref[...] = old_msg[...]
    sign_ref[...] = old_sign[...]
    rows, entry, sign_row = end_rows(state, edges)
    for i, value in enumerate(entry):
        ent_ref[0, i] = value
    sign_ref[vars_ : vars_ + 1, :] = sign_row
    width = 2 * lines
    facing = lax.rem(lax.broadcasted_iota(jnp.int32, (1, width), 1), lines) < FACE_DEV
    for i in (2, 3):
        for k in range(vars_):
            at = slice(vars_ * i + k, vars_ * i + k + 1)
            moved = pltpu.roll(rows[i], width - FACE_DEV * k, 1) if k else rows[i]
            msg_ref[at, :] = jnp.where(facing, moved, old_msg[at, :])


def unfold(k, t, steps, value, kept, turned, pos):
    if t < steps // 2:
        kept[k, t] = value
    else:
        other = kept[k, steps - 1 - t]
        turned.at[k][pl.ds(steps - 1 - t, SEGS, stride=steps), :] = jnp.where(pos, value, other)
        turned.at[k][pl.ds(t, SEGS, stride=steps), :] = jnp.where(pos, other, value)


def lifts(sign_ref, ent_ref, c_s, scale_ref, after_ref, lift_ref, x_s, x_t):
    vars_, lines, cells = scale_ref.shape
    steps, width = c_s.shape[1], c_s.shape[3]
    poses = [jnp.broadcast_to(sign_ref[k : k + 1, :], (SEGS, width)) > 0.0 for k in range(vars_)]
    state = [(ent_ref[k, 2], ent_ref[k, 3]) for k in range(vars_)]
    for t in range(steps):
        for k in range(vars_):
            n1, n2 = state[k]
            x = 2.0 * n1 - 0.5 * n2
            state[k] = (c_s[k, t] * x, n1)
            unfold(k, t, steps, x, x_s, x_t, poses[k])
    for k in range(vars_):
        x = x_t[k].T
        for part in range(2):
            lift_ref[part, k] = x[part * lines : (part + 1) * lines] * scale_ref[k]


def substitute(
    in_ref, adj_ref, sign_ref, ent_ref, c_s, b_s, h_ref, scale_ref, ent_f, c_f, b_f, h_f,
    part_ref, u_s, u_t,
):
    vars_, lines, cells = scale_ref.shape
    steps, width = c_s.shape[1], c_s.shape[3]
    groups = vars_ + 1
    inside = in_ref[...] > 0.0
    poses = [jnp.broadcast_to(sign_ref[k : k + 1, :], (SEGS, width)) > 0.0 for k in range(groups)]
    state = []
    for k in range(groups):
        ent = ent_ref.at[k] if k < vars_ else ent_f.at[0]
        state.append((ent[0], ent[1]))
    for t in range(steps):
        for k in range(groups):
            main = k < vars_
            c = c_s[k, t] if main else c_f[0, t]
            b = b_s[k, t] if main else b_f[0, t]
            y1, y2 = state[k]
            u = 2.0 * y1 - 0.5 * y2
            state[k] = (c * u + b, y1)
            unfold(k, t, steps, u, u_s, u_t, poses[k])
    face_u = u_t[vars_].T
    for k in range(vars_):
        scale = scale_ref[k]
        u = u_t[k].T
        for part in range(2):
            at = part * lines + FACE_DEV * k
            h = jnp.concatenate([h_f[at : at + FACE_DEV], h_ref[part, k, FACE_DEV:]], axis=0)
            us = jnp.concatenate(
                [face_u[at : at + FACE_DEV], u[part * lines + FACE_DEV : (part + 1) * lines]], axis=0)
            part_ref[part, k] = jnp.where(inside, adj_ref[part, k], 0.0) + (h + us) * scale


def fluxes(begin, after_ref, in_ref, adj_ref, speed_ref, flux_ref):
    vars_, lines, cells = speed_ref.shape
    half = cells // 2
    lane = lax.broadcasted_iota(jnp.int32, (lines, half), 1)
    for i in range(flux_ref.shape[1]):
        k = begin + i
        v = speed_ref[k]
        s = jnp.abs(v) * in_ref[...]
        up = v[:, :half] > 0.0
        last = jnp.where(up, lane, 0) == half - 1
        first = jnp.where(up, 1, lane) == 0

        def shifted(low, high):
            low, high = (
                jnp.where(up, pltpu.roll(x, half - 1, 1), pltpu.roll(x, 1, 1)) for x in (low, high))
            return (jnp.where(last, high, jnp.where(first, 0.0, low)),
                    jnp.where(first, low, jnp.where(last, 0.0, high)))

        for part in range(2):
            g = s * adj_ref[part, k]
            low, high = g[:, :half], g[:, half:]
            near = shifted(low, high)
            low, high = shifted(2.0 * low - 0.5 * near[0], 2.0 * high - 0.5 * near[1])
            flux_ref[part, i, :, :half] = low * in_ref[:, :half]
            flux_ref[part, i, :, half:] = high * in_ref[:, half:]


def finish(count, sources, in_ref, sign_ref, part_ref, lift_ref, h_ref, h_f, early_ref, late_ref, *rest):
    got = rest[: count - 1]
    new_hbm, out_hbm, new_ref, out_ref, sems = rest[count - 1 :]
    _, vars_, lines, cells = part_ref.shape
    width = 2 * lines
    place = lax.axis_index("ax")
    odd = lax.rem(place, 2) == 1
    pos = sign_ref[:vars_] > 0.0
    real = lax.broadcasted_iota(jnp.int32, (vars_, width), 1) < lines
    zero = jnp.zeros((vars_, width), F32)
    z1, z2, g1, g2 = zero, zero, zero, zero
    for i in range(count - 1, 0, -1):
        near = jnp.where(place >= i, 1.0, 0.0)
        far = jnp.where(place + i <= count - 1, 1.0, 0.0)
        has = jnp.where(pos, far, near) > 0.0

        def pick(offset, at):
            value = got[0][at]
            for j in range(1, count - 1):
                here = [p for p in range(count) if p + offset == sources[j][p]]
                hit = functools.reduce(jnp.logical_or, [place == p for p in here], place < 0)
                value = jnp.where(hit, got[j][at], value)
            return value

        def field(r):
            at = slice(vars_ * r, vars_ * (r + 1))
            return jnp.where(pos, pick(i, at), pick(-i, at))

        n1, n2, b1, b2 = [field(r) for r in range(4)]
        o1, o2 = pltpu.roll(n1, lines, 1), pltpu.roll(n2, lines, 1)
        t1 = jnp.where(real, n1, o1) * z1 + jnp.where(real, o1, n1) * z2 + b1
        t2 = jnp.where(real, n2, o2) * z1 + jnp.where(real, o2, n2) * z2 + b2
        z1, z2 = jnp.where(has, t1, z1), jnp.where(has, t2, z2)
        if i == 1:
            g1, g2 = jnp.where(has, field(4), 0.0), jnp.where(has, field(5), 0.0)
    r0, r1 = 2.0 * g1 - 0.5 * g2, -0.5 * g1
    down0, down1 = jnp.where(pos, 0.0, r0), jnp.where(pos, 0.0, r1)
    up0, up1 = jnp.where(pos, r0, 0.0), jnp.where(pos, r1, 0.0)
    fill = jnp.zeros((TABLE - vars_, width), F32)
    table = jnp.concatenate([z1, fill, z2, fill, jnp.zeros((width - 2 * TABLE, width), F32)], axis=0).T
    half = cells // 2
    sub = lax.broadcasted_iota(jnp.int32, (8, width), 0)
    left = lax.broadcasted_iota(jnp.int32, (lines, half), 1) < half // 2
    copies = []
    for k in range(vars_):
        row = lambda x: jnp.broadcast_to(x[k : k + 1, :], (8, width))
        low = jnp.where(sub == 0, row(down0), jnp.where(sub == 1, row(down1), 0.0))
        high = jnp.where(sub == 7, row(up0), jnp.where(sub == 6, row(up1), 0.0))
        edges = jnp.concatenate([low, jnp.zeros((half - 16, width), F32), high], axis=0).T
        for part in range(2):
            at = part * lines + FACE_DEV * k
            rows = slice(part * lines, (part + 1) * lines)

            def entering(r):
                return table[rows, TABLE * r + k : TABLE * r + k + 1]

            edge = edges[rows]
            h = jnp.concatenate([h_f[at : at + FACE_DEV], h_ref[part, k, FACE_DEV:]], axis=0)
            split = early_ref.shape[1]
            h = h + (early_ref[part, k] if k < split else late_ref[part, k - split])
            out_ref[part, k, :, :half] = h[:, :half] + jnp.where(left, edge, 0.0) * in_ref[:, :half]
            out_ref[part, k, :, half:] = h[:, half:] + jnp.where(left, 0.0, edge) * in_ref[:, half:]
            new_ref[part, k] = part_ref[part, k] + (
                lift_ref[0, k] * entering(0) + lift_ref[1, k] * entering(1))
            for j, (src, dst) in enumerate(((out_ref, out_hbm), (new_ref, new_hbm))):
                copies.append(pltpu.make_async_copy(
                    src.at[part, k], dst.at[part, k], sems.at[4 * k + 2 * part + j]))
                copies[-1].start()
    for copy in copies:
        copy.wait()


def shards(adjoint, source, speed, inverse_step, coupling, face_line, face_owner, line_length):
    lines, rows, cells = adjoint.shape
    vars_ = speed.shape[1]
    faces = face_line.shape[0]
    blocks = lax.axis_size("xs")
    count = lax.axis_size("ax")
    cap = max(1, faces // blocks)
    width = 2 * lines
    steps = cells // SEGS
    adj = jnp.transpose(adjoint, (1, 0, 2)).reshape(2, vars_, lines, cells)
    src = jnp.transpose(source, (1, 0, 2)).reshape(2, vars_, lines, cells)
    spd = jnp.transpose(speed, (1, 0, 2))
    inv = jnp.transpose(inverse_step, (1, 0, 2))
    cpl = jnp.transpose(coupling, (1, 0, 2))
    vmem = pl.BlockSpec(memory_space=pltpu.VMEM)
    hbm = pl.BlockSpec(memory_space=pltpu.HBM)
    stay = lambda x: pltpu.with_memory_space_constraint(x, pltpu.HBM)
    shape = lambda *dims: jax.ShapeDtypeStruct(dims, F32)
    scratch = lambda *dims: pltpu.VMEM(dims, F32)
    dma = lambda number: pltpu.SemaphoreType.DMA((number,))
    limit = lambda mib: pltpu.CompilerParams(vmem_limit_bytes=mib << 20)
    cost = lambda flops, moved: pl.CostEstimate(
        flops=flops, bytes_accessed=moved, transcendentals=0)
    table_shape = shape(TABLE * pl.cdiv(6 * vars_, TABLE), width)
    sign_shape = shape(TABLE, width)
    order_shape = shape(vars_, steps, SEGS, width)
    field_shape = shape(2, vars_, lines, cells)
    var_shape = shape(vars_, lines, cells)
    face_order = shape(1, steps, SEGS, width)
    paired = blocks == 8
    entries = blocks * cap
    pieces = blocks // 2 if paired else 1
    adj, lengths, inv, packed = pl.pallas_call(
        functools.partial(pack_faces, blocks, cap, paired),
        out_shape=[field_shape, jax.ShapeDtypeStruct((1, lines), jnp.int32), var_shape,
                   shape(entries, PACK_ROWS, cells // 2)],
        in_specs=[hbm] * 6,
        out_specs=[vmem] * 4,
        scratch_shapes=[pltpu.SMEM((faces,), jnp.int32), pltpu.SMEM((faces,), jnp.int32),
                        scratch(vars_, faces, cells), dma(5 + vars_)],
        compiler_params=limit(6),
        name="pack_faces",
    )(stay(face_line), stay(face_owner), stay(adj), stay(cpl), stay(line_length.reshape(1, lines)),
      stay(inv))
    packed = pl.pallas_call(
        deal,
        out_shape=[shape(entries // pieces, PACK_ROWS, cells // 2)] * pieces,
        in_specs=[vmem],
        out_specs=[vmem] * pieces,
        compiler_params=limit(4),
        cost_estimate=cost(2 * 10**6, 4 * 10**7),
        name="deal",
    )(packed)
    hop = lambda x, m: lax.ppermute(x, "xs", [(i, i ^ m) for i in range(blocks)])
    if paired:
        landed = [packed[0]] + [hop(packed[m], 2 * m) for m in (1, 3, 2)]
    msg, sign, ent, c_s, b_s, h, scale, mask = pl.pallas_call(
        main_maps,
        out_shape=[table_shape, sign_shape, shape(vars_, 4, SEGS, width), order_shape, order_shape,
                   field_shape, var_shape, shape(lines, cells)],
        in_specs=[vmem] * 5,
        out_specs=[vmem] * 8,
        scratch_shapes=[scratch(vars_, cells, width)] * 2,
        compiler_params=limit(14),
        cost_estimate=cost(2 * 10**6, 4 * 10**6),
        name="main_maps",
    )(adj, lengths, src, spd, inv)
    if paired:
        halves = shape(pieces * cap, PACK_ROWS, cells // 2)
        near_half, far_half = pl.pallas_call(
            functools.partial(sort_halves, cap),
            out_shape=[halves] * 2,
            in_specs=[vmem] * (1 + pieces),
            out_specs=[vmem] * 2,
            compiler_params=limit(4),
            name="sort_halves",
        )(sign, *landed)
        recv, counts, after = [near_half, hop(far_half, 1)], [pieces * cap] * 2, near_half
    else:
        recv, counts, after = [lax.all_to_all(packed[0], "xs", 0, 0, tiled=True)], [entries], packed[0]
    kept = lambda number: scratch(number, steps // 2, SEGS, width)
    lift = pl.pallas_call(
        lifts,
        out_shape=field_shape,
        in_specs=[vmem] * 5,
        out_specs=vmem,
        scratch_shapes=[kept(vars_), scratch(vars_, cells, width)],
        compiler_params=limit(8),
        cost_estimate=cost(10**6, 2 * 10**6),
        name="lifts",
    )(sign, ent, c_s, scale, after)
    flux = lambda begin, number, when: pl.pallas_call(
        functools.partial(fluxes, begin),
        out_shape=shape(2, number, lines, cells),
        in_specs=[vmem] * 4,
        out_specs=vmem,
        compiler_params=limit(6),
        cost_estimate=cost(10**6, 2 * 10**6),
        name="fluxes",
    )(when, mask, adj, spd)
    early_vars = vars_ * 2 // 5
    early = flux(0, early_vars, lift)
    msg, sign, ent_f, c_f, b_f, h_f = pl.pallas_call(
        functools.partial(face_maps, counts),
        out_shape=[table_shape, sign_shape, shape(1, 4, SEGS, width), face_order, face_order,
                   shape(width, cells)],
        in_specs=[vmem] * (8 + len(recv)),
        out_specs=[vmem] * 6,
        scratch_shapes=[scratch(1, cells, width)] * 2,
        compiler_params=limit(10),
        name="face_maps",
    )(early, mask, adj, src, spd, inv, msg, sign, *recv)
    if count == 4:
        routes = [(1, 0, 3, 2), (3, 2, 0, 1), (2, 3, 1, 0)]
    else:
        routes = [[(i + k) % count for i in range(count)] for k in range(1, count)]
    sources = [[r.index(p) for p in range(count)] for r in routes]
    got = [lax.ppermute(msg, "ax", list(enumerate(r))) for r in routes]
    part = pl.pallas_call(
        substitute,
        out_shape=field_shape,
        in_specs=[vmem] * 12,
        out_specs=vmem,
        scratch_shapes=[kept(vars_ + 1), scratch(vars_ + 1, cells, width)],
        compiler_params=limit(14),
        cost_estimate=cost(2 * 10**6, 3 * 10**6),
        name="substitute",
    )(mask, adj, sign, ent, c_s, b_s, h, scale, ent_f, c_f, b_f, h_f)
    late = flux(early_vars, vars_ - early_vars, part)
    new, out = pl.pallas_call(
        functools.partial(finish, count, sources),
        out_shape=[field_shape] * 2,
        in_specs=[vmem] * (8 + len(got)),
        out_specs=[hbm] * 2,
        scratch_shapes=[scratch(2, vars_, lines, cells)] * 2 + [dma(4 * vars_)],
        compiler_params=limit(10),
        name="finish",
    )(mask, sign, part, lift, h, h_f, early, late, *got)
    back = lambda x: jnp.transpose(x.reshape(rows, lines, cells), (1, 0, 2))
    return (back(new), back(out))


def solution(mesh):
    line = P("xs", None, "ax")
    in_specs = (line,) * 5 + (P("xs"),) * 3
    return jax.shard_map(
        shards, mesh=mesh, in_specs=in_specs, out_specs=(line, line), check_vma=False
    )
```
